32 devices in a mesh: strip: 8 (over z, x), sect: 4 (over y, core).
Axes of the slice: x: 2, y: 2, z: 4, core: 2. Of those that a mesh axis runs over, the one named last changes fastest.
Arguments:
- currents: float32 [32768], P(('strip', 'sect')), may hold values from -6 to 6
- plane_weights: float32 [8, 32768], P(None, ('strip', 'sect')), may hold values from 0 to 1
- cell_weights: float32 [32768, 128], P(('strip', 'sect')), may hold values from 0 to 1
- brick_dest: int32 [8192, 1], P(('strip', 'sect')), may hold values from 0 to 3; in each aligned block of 256 rows (0 to 255, 256 to 511, ...) at most 96 rows name the same one
- brick_tile: int32 [8192], P(('strip', 'sect')), may hold values from 0 to 383
- brick_count: int32 [32], P(('strip', 'sect')), may hold values from 64 to 256, as said below
- kern_across: float32 [5, 2, 17], replicated, may hold values from -1.5 to 1.5
- kern_along: float32 [5, 2, 17], replicated, may hold values from -1.5 to 1.5
- plane_mix: float32 [5, 2, 8, 8], replicated, may hold values from -1.5 to 1.5
Outputs:
- grid_potential: float32 [8, 384, 4096], P(None, None, ('strip', 'sect'))
- segment_potential: float32 [32768], P(('strip', 'sect'))
The draws below stay inside these ranges and needn't reach their ends.
Inputs may be any that keep to these rules, and one draw needn't show every extreme that they name: `brick_dest`: among the 256 bricks of one section at most 96 name the same owner section. `brick_tile`: tile t covers cells across track (t // 8) * 8 onward and along track (t % 8) * 16 onward within the owner's block; several bricks may share a tile. A section's live bricks are its first brick_count ones; the others carry no current and see zero potential.
All inputs are finite; a program needn't handle non-finite values.
Results may differ from the reference program's by a relative error of at most 0.00015.
Values sent between devices are 32-bit elements; how exact they have to be, the bound alone decides.
No kernel may reach another device: no remote copies, remote signals or barrier semaphores. Data moves between devices by JAX's collectives and lax.ppermute only.
A program may use at most 192 MiB of HBM per device.

```python
import math
import jax
import jax.numpy as jnp
import numpy as np
from jax import lax

PLANES = 8
NY = 384
CX = 128
LEVELS = 4
TAPS = 17
BX = 16
BY = 8
SLOTS = 4
NB_DEV = 256
C = 128
CAP = 96
TILES = 384
SECTIONS = 32
NBR = 8192
SEGS = 32768
NX = 4096
N_SECT = 4
DEVICES = 32


def draw_brick_count(key, part):
    first_key, second_key = jax.random.split(key)
    divisor = jax.random.randint(first_key, (SECTIONS,), 1, 5)
    counts = NB_DEV // divisor
    fullest = jax.random.randint(second_key, (), 0, SECTIONS)
    return jnp.where(jnp.arange(SECTIONS) == fullest, NB_DEV, counts).astype(jnp.int32)


def with_ends(result, stream_key, least, top_value):
    dims = result.shape
    spot = [jax.random.randint(jax.random.fold_in(stream_key, axis), (), 0, dims[axis]) for axis in range(len(dims))]
    result = result.at[tuple(spot)].set(least)
    longest = dims.index(max(dims))
    spot[longest] = (spot[longest] + 1) % dims[longest]
    return result.at[tuple(spot)].set(top_value)


def steps_of(key, shape, cuts, least, top_value):
    def one(dim, blocks):
        steps = jax.random.uniform(jax.random.fold_in(jax.random.fold_in(key, 6), dim), (blocks,), jnp.float32, least / len(cuts), top_value / len(cuts))
        return jnp.repeat(jnp.exp(steps), shape[dim] // blocks).reshape((-1,) + (1,) * (len(shape) - dim - 1))

    factor_of = one(*cuts[0])
    for cut in cuts[1:]:
        factor_of = factor_of * one(*cut)
    return factor_of


def routed_block(key, own, number, rows, count, top, most, slope):
    order = jax.random.permutation(key, count)
    crowded, usual = portions_of(count, rows * top, most, slope, True), portions_of(count, rows * top, most, slope, False)
    places = jnp.arange(count)

    def named(lengths, turn):
        used = int((lengths > 0).sum())
        fixed = max(1, used // 4)
        passed = fixed + (places - fixed + turn * (used - fixed)) % max(1, count - fixed)
        return jnp.zeros((count,), jnp.int32).at[order[jnp.where(places < fixed, places, passed)]].set(jnp.asarray(lengths, jnp.int32))

    lengths = jnp.where(number % 4 == 0, named(crowded, number // 4), named(usual, number - number // 4 - 1))
    mixed = jax.random.permutation(jax.random.fold_in(own, 3), count)
    source_of, sink = mixed[0:count // 2 * 2:2], mixed[1:count // 2 * 2:2]
    margin = jnp.minimum(lengths[source_of] - 1, most - lengths[sink]) // 2
    margin = jnp.where((source_of == order[0]) | (sink == order[0]) | (lengths[sink] == 0), 0, jnp.maximum(margin, 0))
    passed = jax.random.randint(jax.random.fold_in(own, 4), (count // 2,), 0, 1 << 20) % (margin + 1)
    lengths = lengths.at[source_of].add(-passed).at[sink].add(passed)
    items = jnp.searchsorted(jnp.cumsum(lengths), jnp.arange(rows * top), side="right").astype(jnp.int32)
    listing = items.reshape(top, rows).T
    listing = listing[jax.random.permutation(jax.random.fold_in(own, 1), rows)]
    turn = jax.random.randint(jax.random.fold_in(own, 2), (rows, 1), 0, top)
    return jnp.take_along_axis(listing, (jnp.arange(top)[None, :] + turn) % top, axis=1)


def portions_of(number_of, total, most, lean, full):
    portions = [(1 << 20) // math.isqrt(rank ** lean) + 1 for rank in range(1, number_of + 1)]
    largest = most if full else min(most, max(-(-total // number_of), total * portions[0] // sum(portions)))
    least = 1 if total - largest >= number_of - 1 else 0
    holding, rest = [largest] + [least] * (number_of - 1), total - largest - least * (number_of - 1)
    while rest > 0:
        candidates = [i for i in range(1, number_of) if holding[i] < largest] or [i for i in range(1, number_of) if holding[i] < most]
        whole, left = sum([portions[i] for i in candidates]), rest
        for i in candidates:
            addition = min(most - holding[i], max(1, left * portions[i] // whole), rest)
            holding[i] = holding[i] + addition
            rest = rest - addition
    return np.array(holding)


def bell_draw(stream_key, dims, spread, bound, shards=(), kind=jnp.bfloat16):
    values = spread * jax.random.normal(stream_key, dims, jnp.float32)
    if shards:
        values = values * steps_of(stream_key, dims, shards, -0.22, 0.18)
    return jnp.clip(values, -bound, bound).astype(kind)


def setup_inputs(seed: int = 0) -> dict:
    key_list = jax.random.split(jax.random.key(seed), 10)
    currents = bell_draw(key_list[0], (SEGS,), 1.0, 6.0, ((0, 32),), jnp.float32)
    plane_weights = jnp.clip(1.0 * jax.random.uniform(key_list[1], (PLANES, SEGS), jnp.float32) ** steps_of(key_list[1], (PLANES, SEGS), ((1, 32),), -0.2, 0.2), 0.0, 1.0)
    cell_weights = jnp.clip(1.0 * jax.random.uniform(key_list[2], (SEGS, C), jnp.float32) ** steps_of(key_list[2], (SEGS, C), ((0, 32),), -0.2, 0.2), 0.0, 1.0)
    brick_dest_keys = jax.random.split(jax.random.fold_in(key_list[3], 1), NBR // NB_DEV)
    brick_dest_turns = jax.random.permutation(jax.random.fold_in(key_list[3], 3), NBR // NB_DEV)
    brick_dest = jax.vmap(lambda own, number: routed_block(jax.random.fold_in(key_list[3], 2), own, number, NB_DEV, N_SECT, 1, CAP, 2))(brick_dest_keys, brick_dest_turns).reshape((NBR, 1))
    brick_tile = with_ends(jax.random.randint(key_list[4], (NBR,), 0, TILES), jax.random.fold_in(key_list[4], 1), 0, TILES - 1).astype(jnp.int32)
    brick_count = draw_brick_count(jax.random.fold_in(key_list[9], 71), 0)
    kern_across = bell_draw(key_list[6], (LEVELS + 1, 2, TAPS), 0.25, 1.5, (), jnp.float32)
    kern_along = bell_draw(key_list[7], (LEVELS + 1, 2, TAPS), 0.25, 1.5, (), jnp.float32)
    plane_mix = bell_draw(key_list[8], (LEVELS + 1, 2, PLANES, PLANES), (2 * PLANES) ** -0.5, 1.5, (), jnp.float32)
    return {"currents": currents, "plane_weights": plane_weights, "cell_weights": cell_weights, "brick_dest": brick_dest, "brick_tile": brick_tile, "brick_count": brick_count, "kern_across": kern_across, "kern_along": kern_along, "plane_mix": plane_mix}


precise = lax.Precision.HIGHEST


def across_ranks(charge_field, kernel):
    reach = kernel.shape[-1] // 2
    extent = charge_field.shape[1]
    padded = jnp.pad(charge_field, ((0, 0), (reach, reach), (0, 0)))
    summed = jnp.zeros((kernel.shape[0],) + charge_field.shape, jnp.float32)
    for offset in range(kernel.shape[-1]):
        summed = summed + kernel[:, offset][:, None, None, None] * padded[None, :, offset:offset + extent, :]
    return summed


def along_sum(ranked, kernel):
    reach = kernel.shape[-1] // 2
    extent = ranked.shape[3]
    padded = jnp.pad(ranked, ((0, 0), (0, 0), (0, 0), (reach, reach)))
    summed = jnp.zeros(ranked.shape, jnp.float32)
    for offset in range(kernel.shape[-1]):
        summed = summed + kernel[:, offset][:, None, None, None] * padded[:, :, :, offset:offset + extent]
    return summed


def level_term(charge_field, kern_y, kern_x, mixing):
    ranked = across_ranks(charge_field, kern_y)
    ranked = along_sum(ranked, kern_x)
    return jnp.einsum('rzw,rwyx->zyx', mixing, ranked, precision=precise)


def restrict(charge_field):
    planes, rows, columns = charge_field.shape
    return 0.5 * charge_field.reshape(planes, rows // 2, 2, columns // 2, 2).sum(axis=(2, 4))


def prolong(coarse):
    return 0.5 * jnp.repeat(jnp.repeat(coarse, 2, axis=1), 2, axis=2)


def reference(currents, plane_weights, cell_weights, brick_dest, brick_tile, brick_count, kern_across, kern_along, plane_mix):
    brick_ids = jnp.arange(NBR, dtype=jnp.int32)
    section = brick_ids // NB_DEV
    alive_mask = ((brick_ids % NB_DEV) < brick_count[section]).astype(jnp.float32)
    owner = (section // N_SECT) * N_SECT + brick_dest[:, 0]
    place = (owner * TILES + brick_tile).astype(jnp.int32)
    charge = plane_weights.reshape(PLANES, NBR, SLOTS).transpose(1, 2, 0) * (currents.reshape(NBR, SLOTS) * alive_mask[:, None])[:, :, None]
    cell_rows = cell_weights.reshape(NBR, SLOTS, C)
    brick = jnp.einsum('bsz,bsc->bzc', charge, cell_rows, precision=precise)
    tile_sum = jnp.zeros((DEVICES * TILES, PLANES, C), jnp.float32).at[place].add(brick)
    charge_grid = tile_sum.reshape(DEVICES, NY // BY, CX // BX, PLANES, BY, BX).transpose(3, 1, 4, 0, 2, 5).reshape(PLANES, NY, NX)
    charges = [charge_grid]
    for level_index in range(LEVELS):
        charges.append(restrict(charges[-1]))
    potential = level_term(charges[LEVELS], kern_across[LEVELS], kern_along[LEVELS], plane_mix[LEVELS])
    for level_index in range(LEVELS - 1, -1, -1):
        potential = level_term(charges[level_index], kern_across[level_index], kern_along[level_index], plane_mix[level_index]) + prolong(potential)
    pot_tiles = potential.reshape(PLANES, NY // BY, BY, DEVICES, CX // BX, BX).transpose(3, 1, 4, 0, 2, 5).reshape(DEVICES * TILES, PLANES, C)
    sampled = jnp.einsum('bzc,bsc->bsz', pot_tiles[place], cell_rows, precision=precise)
    weights_back = plane_weights.reshape(PLANES, NBR, SLOTS)
    segment_potential = jnp.einsum('bsz,zbs->bs', sampled, weights_back, precision=precise) * alive_mask[:, None]
    return potential, segment_potential.reshape(SEGS)
```

```python
import functools

import jax
import jax.numpy as jnp
from jax import lax
from jax.experimental import pallas as pl
from jax.experimental.pallas import tpu as pltpu
from jax.sharding import PartitionSpec as P

NY = 384
CX = 128
LEVELS = 4
TILES = 384
PLANES = 8
TAPS = 17
REACH = TAPS // 2
SLOTS = 4
BRICKS = 256
CAP = 96
PEERS = 4
CELLS = SLOTS * CAP
PACK = CAP // 2
ROWS = CELLS + PACK
SEGS = BRICKS * SLOTS
HEIGHTS = tuple(NY >> level for level in range(LEVELS + 1))
WIDTHS = tuple(CX >> level for level in range(LEVELS + 1))
LANE_OF = (0, 0, 64, 96, 112)
RIM_ROW = (0, 0, 192, 288, 336)
STEP = (384, 192, 96, 48, 32)
K_OF = (0, 768, 1152, 1344, 1440)
DEPTH = 1536
F32 = jnp.float32
BF16 = jnp.bfloat16


def split(value):
    high = value.astype(BF16)
    return high, (value - high.astype(F32)).astype(BF16)


def dot(left, right):
    return jnp.dot(left, right, preferred_element_type=F32)


def iota(shape, dim):
    return lax.broadcasted_iota(jnp.int32, shape, dim)


def swap_groups(value):
    count = value.shape[0] // 8
    value = value.reshape(count, 8, CX)
    row, group = iota((1, 8, CX), 1), iota((1, 8, CX), 2) // 16
    for bit in range(3):
        step = 1 << bit
        row_bit, group_bit = (row >> bit) & 1, (group >> bit) & 1
        ahead = pltpu.roll(pltpu.roll(value, 8 - step, 1), 16 * step, 2)
        if step == 4:
            behind = ahead
        else:
            behind = pltpu.roll(pltpu.roll(value, step, 1), CX - 16 * step, 2)
        value = jnp.where(row_bit == group_bit, value, jnp.where(group_bit == 1, ahead, behind))
    return value.reshape(count * 8, CX)


def route_kernel(
    count_ref, currents_ref, planes_ref, cells_ref, dest_ref, tile_ref, *refs
):
    outs, slot_ref, feature = refs[:PEERS], refs[PEERS], refs[PEERS + 1]
    me = lax.axis_index("sect")
    turn = dest_ref[...] ^ me
    onehot = iota((16, BRICKS), 0) == turn
    onehot_f = onehot.astype(F32)
    before = (iota((BRICKS, BRICKS), 0) < iota((BRICKS, BRICKS), 1)).astype(F32).astype(BF16)
    earlier = dot(onehot_f.astype(BF16), before)
    base = (iota((16, BRICKS), 0) * CAP).astype(F32)
    slot = jnp.sum(onehot_f * (earlier + base), axis=0, keepdims=True)
    slot_ref[...] = jnp.broadcast_to(slot, slot_ref.shape)
    choose = (iota((PEERS * CAP, BRICKS), 0).astype(F32) == slot).astype(F32).astype(BF16)
    alive = (iota((1, SEGS), 1) // SLOTS < count_ref[0]).astype(F32)
    currents = currents_ref[...] * alive
    lines = jnp.concatenate(
        [planes_ref[...], currents, jnp.zeros((CX - PLANES - 1, SEGS), F32)], axis=0
    )
    for part in range(SEGS // CX):
        feature[part * CX : (part + 1) * CX, :] = lines[:, part * CX : (part + 1) * CX].T
    meta = jnp.zeros((BRICKS, CX), F32)
    for s in range(SLOTS):
        rows = feature[pl.ds(s, BRICKS, stride=SLOTS), :]
        meta = meta + (pltpu.roll(rows, 16 * s, 1) if s else rows)
    tiles = jnp.concatenate(
        [tile_ref[...].astype(F32), jnp.zeros((CX - 1, BRICKS), F32)], axis=0
    )
    tiles = jnp.concatenate([tiles[:, :CX].T, tiles[:, CX:].T], axis=0)
    meta = meta + pltpu.roll(tiles, 9, 1)
    both = dot(choose, jnp.concatenate(split(meta), axis=1))
    both = both[:, :CX] + both[:, CX:]
    for k in range(PEERS):
        lower = both[k * CAP : k * CAP + PACK]
        upper = both[k * CAP + PACK : (k + 1) * CAP]
        outs[k][CELLS:, :] = lower + pltpu.roll(upper, CX // 2, 1)
    for s in range(SLOTS):
        high, low = split(cells_ref[pl.ds(s, BRICKS, stride=SLOTS), :])
        moved = dot(choose, jnp.concatenate([high, low], axis=1))
        moved = moved[:, :CX] + moved[:, CX:]
        for k in range(PEERS):
            outs[k][s * CAP : (s + 1) * CAP, :] = moved[k * CAP : (k + 1) * CAP]


def prep_kernel(across_ref, along_ref, along_high, along_low, across_high, across_low):
    for level in range(LEVELS + 1):
        lane, width = LANE_OF[level], WIDTHS[level]
        row = iota((2 * CX, 1), 0)
        own = row - lane
        own = jnp.where((row < CX) & (own >= 0) & (own < width), own, 4 * NY)
        first, second = row - CX, row - CX - CX // 2
        before = first if level == 0 else second
        after = second if level == 0 else first
        place = jnp.where((before >= 0) & (before < REACH), before - REACH, own)
        place = jnp.where((after >= 0) & (after < REACH), after + width, place)
        shift = place - (iota((2 * CX, CX), 1) >> level) + REACH
        for r in range(2):
            taps = jnp.zeros((2 * CX, CX), F32)
            for t in range(TAPS):
                taps = jnp.where(shift == t, along_ref[level, r, t], taps)
            high, low = split(taps * (0.5**level))
            along_high[level, :, r * CX : (r + 1) * CX] = high
            along_low[level, :, r * CX : (r + 1) * CX] = low
    for part in range(DEPTH // CX):
        column = iota((1, CX), 1) + part * CX
        pieces = []
        for level in range(LEVELS + 1):
            for r in range(2):
                start = K_OF[level] + r * STEP[level]
                if start < (part + 1) * CX and start + HEIGHTS[level] > part * CX:
                    pieces.append((level, r, start))
        held = []
        far = jnp.full((1, CX), 4 * NY, jnp.int32)
        offset, levels = far, jnp.zeros((1, CX), jnp.int32)
        for level, r, start in pieces:
            inside = (column >= start) & (column < start + HEIGHTS[level])
            held.append(inside)
            offset = jnp.where(inside, column - start + REACH, offset)
            levels = jnp.where(inside, level, levels)
        shift = offset - (iota((NY, CX), 0) >> jnp.broadcast_to(levels, (NY, CX)))
        taps = jnp.zeros((NY, CX), F32)
        for t in range(TAPS):
            line = jnp.zeros((1, CX), F32)
            for (level, r, start), inside in zip(pieces, held):
                line = jnp.where(inside, across_ref[level, r, t], line)
            taps = jnp.where(shift == t, line, taps)
        high, low = split(taps)
        across_high[:, part * CX : (part + 1) * CX] = high
        across_low[:, part * CX : (part + 1) * CX] = low


def unpack_meta(ref):
    packed = ref[CELLS:, :]
    return jnp.concatenate([packed, pltpu.roll(packed, CX // 2, 1)], axis=0)


def charge_kernel(r0, r1, r2, r3, q0, s1, s2, s3, s4, to_right, to_left, hot, bricks, narrow):
    half = PLANES * CX
    for j, ref in enumerate((r0, r1, r2, r3)):
        meta = unpack_meta(ref)
        charged = [
            ref[s * CAP : (s + 1) * CAP, :] * meta[:, 16 * s + 8 : 16 * s + 9] for s in range(SLOTS)
        ]
        for z in range(PLANES):
            total = charged[0] * meta[:, z : z + 1]
            for s in range(1, SLOTS):
                total = total + charged[s] * meta[:, 16 * s + z : 16 * s + z + 1]
            high, low = split(total)
            bricks[j * CX : j * CX + CAP, z * CX : (z + 1) * CX] = high
            bricks[j * CX : j * CX + CAP, half + z * CX : half + (z + 1) * CX] = low
        bricks[j * CX + CAP : (j + 1) * CX, :] = jnp.zeros((CX - CAP, 2 * half), BF16)
        whole = jnp.concatenate([meta, jnp.zeros((CX - CAP, CX), F32)], axis=0)
        names = whole.T[9:10, :]
        names = jnp.where(iota((1, CX), 1) < CAP, names, -1.0)
        match = (iota((TILES, CX), 0).astype(F32) == names).astype(F32).astype(BF16)
        hot[:, j * CX : (j + 1) * CX] = match
    lane, row = iota((CX, CX), 1), iota((CX, CX), 0)
    fold = jnp.zeros((CX, CX), F32)
    for level in range(1, LEVELS + 1):
        start = LANE_OF[level]
        mine = (lane >= start) & (lane < start + WIDTHS[level]) & ((row >> level) == lane - start)
        fold = jnp.where(mine, 0.5**level, fold)
    fold = fold.astype(BF16)
    fold = jnp.concatenate([fold, fold], axis=0)
    for z in range(PLANES):
        found = dot(hot[...], bricks[:, z * CX : (z + 1) * CX]) + dot(
            hot[...], bricks[:, half + z * CX : half + (z + 1) * CX]
        )
        field = swap_groups(found)
        q0[z] = field
        narrow[z * NY : (z + 1) * NY, :] = dot(jnp.concatenate(split(field), axis=1), fold)
    source = narrow
    for target in (s1, s2, s3, s4):
        size = target.shape[0]
        target[...] = source[pl.ds(0, size, stride=2), :] + source[pl.ds(1, size, stride=2), :]
        source = target
    lanes = iota((1, CX), 1)
    right = jnp.zeros((NY, CX), F32)
    left = jnp.zeros((NY, CX), F32)
    for z in range(PLANES):
        field = q0[z]
        low = (lanes >= 8 * z) & (lanes < 8 * z + 8)
        high = (lanes >= 64 + 8 * z) & (lanes < 72 + 8 * z)
        right = jnp.where(low, pltpu.roll(field, (8 * z - (CX - REACH)) % CX, 1), right)
        left = jnp.where(high, pltpu.roll(field, (64 + 8 * z) % CX, 1), left)
    to_right[...] = right
    to_left[...] = left
    for level, source in zip(range(1, LEVELS + 1), (s1, s2, s3, s4)):
        size, start, width = HEIGHTS[level], LANE_OF[level], WIDTHS[level]
        rows = slice(RIM_ROW[level], RIM_ROW[level] + size)
        right, left = to_right[rows, :], to_left[rows, :]
        for z in range(PLANES):
            field = source[z * size : (z + 1) * size, :]
            low = (lanes >= 8 * z) & (lanes < 8 * z + 8)
            high = (lanes >= 64 + 8 * z) & (lanes < 72 + 8 * z)
            right = jnp.where(
                high, pltpu.roll(field, (64 + 8 * z - (start + width - REACH)) % CX, 1), right
            )
            left = jnp.where(low, pltpu.roll(field, (8 * z - start) % CX, 1), left)
        to_right[rows, :] = right
        to_left[rows, :] = left


def field_kernel(
    mix_ref, q0, s1, s2, s3, s4, from_left, from_right, along_high, along_low, across_high,
    across_low, r0, r1, r2, r3, grid_ref, b0, b1, b2, b3, ranked, high_ref, low_ref, tiles, picked
):
    half = PLANES * CX
    lanes = iota((1, CX), 1)
    sources = (q0, s1, s2, s3, s4)
    for level in range(LEVELS + 1):
        size, step = HEIGHTS[level], STEP[level]
        if level == 0:
            rims = jnp.where(lanes < CX // 2, from_left[...], from_right[...])
        else:
            rows = slice(RIM_ROW[level], RIM_ROW[level] + size)
            rims = jnp.where(lanes < CX // 2, from_right[rows, :], from_left[rows, :])
        for z in range(PLANES):
            own = q0[z] if level == 0 else sources[level][z * size : (z + 1) * size, :]
            turned = pltpu.roll(rims, (CX - 8 * z) % CX, 1) if z else rims
            high, low = split(jnp.concatenate([own, turned], axis=1))
            ranked[z, :size, :] = (
                dot(high, along_high[level]) + dot(low, along_high[level])
                + dot(high, along_low[level])
            )
        chunk = {384: 32, 192: 32, 96: 32, 48: 16, 24: 24}[size]

        def mixed(index, carry, level=level, chunk=chunk, step=step):
            start = index * chunk
            if chunk % 8 == 0 and not isinstance(start, int):
                start = pl.multiple_of(start, chunk)
            for r in range(2):
                parts = [
                    ranked[w, pl.ds(start, chunk), r * CX : (r + 1) * CX] for w in range(PLANES)
                ]
                for z in range(PLANES):
                    total = parts[0] * mix_ref[level, r, z, 0]
                    for w in range(1, PLANES):
                        total = total + parts[w] * mix_ref[level, r, z, w]
                    if chunk == 24:
                        total = jnp.concatenate([total, jnp.zeros((8, CX), F32)], axis=0)
                    high, low = split(total)
                    length = 32 if chunk == 24 else chunk
                    place = K_OF[level] + r * step + start
                    high_ref[pl.ds(place, length), z * CX : (z + 1) * CX] = high
                    low_ref[pl.ds(place, length), z * CX : (z + 1) * CX] = low
            return carry

        if size // chunk == 1:
            mixed(0, 0)
        else:
            lax.fori_loop(0, size // chunk, mixed, 0)
    spare = K_OF[LEVELS] + 2 * STEP[LEVELS]
    high_ref[spare:, :] = jnp.zeros((DEPTH - spare, half), BF16)
    low_ref[spare:, :] = jnp.zeros((DEPTH - spare, half), BF16)
    for pair in range(PLANES // 2):
        part = slice(pair * 2 * CX, (pair + 1) * 2 * CX)
        total = dot(across_high[...], high_ref[:, part]) + dot(across_high[...], low_ref[:, part])
        total = total + dot(across_low[...], high_ref[:, part])
        for i in range(2):
            z = 2 * pair + i
            plane = total[:, i * CX : (i + 1) * CX]
            grid_ref[z] = plane
            high, low = split(swap_groups(plane))
            tiles[:, z * CX : (z + 1) * CX] = high
            tiles[:, half + z * CX : half + (z + 1) * CX] = low
    for ref, out in zip((r0, r1, r2, r3), (b0, b1, b2, b3)):
        meta = unpack_meta(ref)
        match = (iota((CAP, TILES), 1).astype(F32) == meta[:, 9:10]).astype(F32).astype(BF16)
        picked[...] = dot(match, tiles[:, :half]) + dot(match, tiles[:, half:])
        values = jnp.zeros((CAP, CX), F32)
        for s in range(SLOTS):
            total = picked[:, :CX] * meta[:, 16 * s : 16 * s + 1]
            for z in range(1, PLANES):
                total = total + picked[:, z * CX : (z + 1) * CX] * meta[:, 16 * s + z : 16 * s + z + 1]
            total = jnp.sum(total * ref[s * CAP : (s + 1) * CAP, :], axis=1, keepdims=True)
            values = jnp.where(lanes == s, total, values)
        values = jnp.concatenate([values, jnp.zeros((CX - CAP, CX), F32)], axis=0)
        out[...] = values.T[:8, :]


def pick_kernel(count_ref, slot_ref, b0, b1, b2, b3, out_ref):
    slot = slot_ref[0:1, :]
    turn = jnp.floor((slot + 0.5) * (1.0 / CAP))
    place = slot + turn * (CX - CAP)
    match = (iota((PEERS * CX, BRICKS), 0).astype(F32) == place).astype(F32).astype(BF16)
    held = jnp.concatenate([b0[...], b1[...], b2[...], b3[...]], axis=1)
    high, low = split(held)
    value = dot(jnp.concatenate([high, low], axis=0), match)
    value = value[:8] + value[8:]
    spread = (iota((BRICKS, SEGS), 1) // SLOTS == iota((BRICKS, SEGS), 0)).astype(F32).astype(BF16)
    high, low = split(value)
    value = dot(jnp.concatenate([high, low], axis=0), spread)
    value = value[:8] + value[8:]
    lane = iota((8, SEGS), 1)
    mine = (lane % SLOTS == iota((8, SEGS), 0)) & (lane // SLOTS < count_ref[0])
    out_ref[...] = jnp.sum(jnp.where(mine, value, 0.0), axis=0, keepdims=True)


VMEM = pl.BlockSpec(memory_space=pltpu.VMEM)
SMEM = pl.BlockSpec(memory_space=pltpu.SMEM)


def shape(*dims, kind=F32):
    return jax.ShapeDtypeStruct(dims, kind)


def call(kernel, inputs, outputs, scratch=(), megabytes=32):
    return pl.pallas_call(
        kernel,
        in_specs=list(inputs),
        out_specs=[VMEM] * len(outputs),
        out_shape=list(outputs),
        scratch_shapes=list(scratch),
        compiler_params=pltpu.CompilerParams(vmem_limit_bytes=megabytes << 20),
    )


def body(
    currents, plane_weights, cell_weights, brick_dest, brick_tile, brick_count, kern_across,
    kern_along, plane_mix,
):
    *sends, slots = call(
        route_kernel,
        [SMEM] + [VMEM] * 5,
        [shape(ROWS, CX)] * PEERS + [shape(8, BRICKS)],
        [pltpu.VMEM((SEGS, CX), F32)],
    )(
        brick_count,
        currents.reshape(1, SEGS),
        plane_weights,
        cell_weights,
        brick_dest.reshape(1, BRICKS),
        brick_tile.reshape(1, BRICKS),
    )
    swaps = [[(i, i ^ k) for i in range(PEERS)] for k in range(PEERS)]
    held = [sends[0]] + [lax.ppermute(sends[k], "sect", swaps[k]) for k in range(1, PEERS)]
    along_high, along_low, across_high, across_low = call(
        prep_kernel,
        [SMEM, SMEM],
        [shape(LEVELS + 1, 2 * CX, 2 * CX, kind=BF16)] * 2 + [shape(NY, DEPTH, kind=BF16)] * 2,
    )(kern_across, kern_along)
    *fields, to_right, to_left = call(
        charge_kernel,
        [VMEM] * 4,
        [shape(PLANES, NY, CX)]
        + [shape(PLANES * HEIGHTS[level], CX) for level in range(1, LEVELS + 1)]
        + [shape(NY, CX)] * 2,
        [
            pltpu.VMEM((TILES, PEERS * CX), BF16),
            pltpu.VMEM((PEERS * CX, 2 * PLANES * CX), BF16),
            pltpu.VMEM((PLANES * NY, CX), F32),
        ],
    )(*held)
    axes = ("strip", "sect")
    devices = lax.axis_size(axes)
    up = [(i, i + 1) for i in range(devices - 1)]
    down = [(i + 1, i) for i in range(devices - 1)]
    from_left = lax.ppermute(to_right, axes, up)
    from_right = lax.ppermute(to_left, axes, down)
    grid, *samples = call(
        field_kernel,
        [SMEM] + [VMEM] * 15,
        [shape(PLANES, NY, CX)] + [shape(8, CX)] * PEERS,
        [
            pltpu.VMEM((PLANES, NY, 2 * CX), F32),
            pltpu.VMEM((DEPTH, PLANES * CX), BF16),
            pltpu.VMEM((DEPTH, PLANES * CX), BF16),
            pltpu.VMEM((TILES, 2 * PLANES * CX), BF16),
            pltpu.VMEM((CAP, PLANES * CX), F32),
        ],
        megabytes=56,
    )(
        plane_mix, *fields, from_left, from_right, along_high, along_low, across_high, across_low,
        *held,
    )
    back = [samples[0]] + [lax.ppermute(samples[k], "sect", swaps[k]) for k in range(1, PEERS)]
    (segments,) = call(
        pick_kernel, [SMEM] + [VMEM] * 5, [shape(1, SEGS)]
    )(brick_count, slots, *back)
    return grid, segments.reshape(SEGS)


def solution(mesh):
    flat = ("strip", "sect")
    placed = (
        P(flat), P(None, flat), P(flat, None), P(flat, None), P(flat), P(flat), P(), P(), P(),
    )
    return jax.shard_map(
        body,
        mesh=mesh,
        in_specs=placed,
        out_specs=(P(None, None, flat), P(flat)),
        check_vma=False,
    )
```

```python
import jax
import jax.numpy as jnp
from jax import lax
from jax.experimental import pallas as pl
from jax.experimental.pallas import tpu as pltpu
from jax.sharding import PartitionSpec as P

NY = 384
CX = 128
LEVELS = 4
TILES = 384
PLANES = 8
TAPS = 17
REACH = TAPS // 2
SLOTS = 4
BRICKS = 256
CAP = 96
PEERS = 4
CELLS = SLOTS * CAP
PACK = CAP // 2
ROWS = CELLS + PACK
SEGS = BRICKS * SLOTS
BAND = NY // 8
HALF = PLANES * CX
HEIGHTS = tuple(NY >> level for level in range(LEVELS + 1))
WIDTHS = tuple(CX >> level for level in range(LEVELS + 1))
STEP = (384, 192, 96, 48, 32)
ROW_OF = (0, 384, 576, 672, 720)
ALL_ROWS = 752
K_OF = (0, 768, 1152, 1344, 1440)
ALL_K = 1504
RIM_ROW = (0, 0, 192, 288, 384)
RIM_ROWS = NY + HEIGHTS[LEVELS]
F32 = jnp.float32
BF16 = jnp.bfloat16


def split(value):
    high = value.astype(BF16)
    return high, (value - high.astype(F32)).astype(BF16)


def dot(left, right):
    return jnp.dot(left, right, preferred_element_type=F32)


def iota(shape, dim):
    return lax.broadcasted_iota(jnp.int32, shape, dim)


def flags(condition):
    return condition.astype(F32).astype(BF16)


def turn(value, amount):
    amount = amount % CX
    return pltpu.roll(value, amount, 1) if amount else value


def swap_groups(bands):
    group = iota((1, CX), 1) // 16
    for bit in range(3):
        step = 1 << bit
        upper = ((group >> bit) & 1) == 1
        fresh = []
        for i in range(8):
            other = bands[i ^ step]
            if i & step:
                fresh.append(jnp.where(upper, bands[i], turn(other, -16 * step)))
            else:
                fresh.append(jnp.where(upper, turn(other, 16 * step), bands[i]))
        bands = fresh
    return bands


def route_kernel(
    count_ref, currents_hbm, planes_hbm, cells_hbm, dest_hbm, tile_hbm, *refs
):
    outs, slot_ref = refs[:PEERS], refs[PEERS]
    feature, currents_ref, planes_ref, cells_ref, dest_ref, tile_ref, sems = refs[PEERS + 1 :]
    pairs = (
        (dest_hbm, dest_ref), (tile_hbm, tile_ref), (currents_hbm, currents_ref),
        (planes_hbm, planes_ref), (cells_hbm, cells_ref),
    )
    copies = [pltpu.make_async_copy(a, b, sems.at[i]) for i, (a, b) in enumerate(pairs)]
    for copy in copies:
        copy.start()
    for copy in copies[:4]:
        copy.wait()
    me = lax.axis_index("sect")
    away = dest_ref[...] ^ me
    onehot = (iota((16, BRICKS), 0) == away).astype(F32)
    before = flags(iota((BRICKS, BRICKS), 0) < iota((BRICKS, BRICKS), 1))
    earlier = dot(onehot.astype(BF16), before)
    base = (iota((16, BRICKS), 0) * CAP).astype(F32)
    slot = jnp.sum(onehot * (earlier + base), axis=0, keepdims=True)
    slot_ref[...] = jnp.broadcast_to(slot, slot_ref.shape)
    choose = flags(iota((PEERS * CAP, BRICKS), 0).astype(F32) == slot)
    alive = (iota((1, SEGS), 1) // SLOTS < count_ref[0]).astype(F32)
    currents = currents_ref[...] * alive
    lines = jnp.concatenate(
        [planes_ref[...], currents, jnp.zeros((CX - PLANES - 1, SEGS), F32)], axis=0
    )
    for part in range(SEGS // CX):
        feature[part * CX : (part + 1) * CX, :] = lines[:, part * CX : (part + 1) * CX].T
    meta = jnp.zeros((BRICKS, CX), F32)
    for s in range(SLOTS):
        meta = meta + turn(feature[pl.ds(s, BRICKS, stride=SLOTS), :], 16 * s)
    tile = tile_ref[...]
    tile = (tile & 7) * BAND + (tile >> 3)
    tiles = jnp.concatenate([tile.astype(F32), jnp.zeros((CX - 1, BRICKS), F32)], axis=0)
    tiles = jnp.concatenate([tiles[:, :CX].T, tiles[:, CX:].T], axis=0)
    meta = meta + turn(tiles, 9)
    both = dot(choose, jnp.concatenate(split(meta), axis=1))
    both = both[:, :CX] + both[:, CX:]
    for k in range(PEERS):
        lower = both[k * CAP : k * CAP + PACK]
        upper = both[k * CAP + PACK : (k + 1) * CAP]
        outs[k][CELLS:, :] = lower + turn(upper, CX // 2)
    copies[4].wait()
    for s in range(SLOTS):
        high, low = split(cells_ref[pl.ds(s, BRICKS, stride=SLOTS), :])
        moved = dot(choose, jnp.concatenate([high, low], axis=1))
        moved = moved[:, :CX] + moved[:, CX:]
        for k in range(PEERS):
            outs[k][s * CAP : (s + 1) * CAP, :] = moved[k * CAP : (k + 1) * CAP]


def height_of(place, level):
    if level == LEVELS:
        return place
    band = (place * 1366) >> 16
    return (place - band * BAND) * (8 >> level) + band


def rim_of(lane, level):
    if level == LEVELS:
        j, rest = lane >> 4, lane & 15
        return rest & 7, jnp.where(rest < 8, j - REACH, j + WIDTHS[level])
    spot = lane if level == 0 else lane ^ (CX // 2)
    log = level + 3
    rest = spot & ((8 << level) - 1)
    j, offset = rest >> level, rest & ((1 << level) - 1)
    first = spot < CX // 2
    block = jnp.where(first, spot >> log, (CX - 1 - spot) >> log)
    return (block << level) + offset, jnp.where(first, j + WIDTHS[level], j - REACH)


def prep_kernel(
    across_ref, along_ref, mix_ref, own_ref, own_low_ref, across_high, across_low, blend_high,
    blend_low, rim_high, rim_low
):
    exact = lax.Precision.HIGHEST
    for level in range(LEVELS + 1):
        scale = 0.25**level
        row = iota((CX, 1), 0)
        mark = jnp.where((row & ((1 << level) - 1)) == 0, row >> level, 4 * NY)
        lane_z, lane_place = rim_of(row, level)
        line_z, line_place = rim_of(iota((1, CX), 1), level)
        column = iota((CX, CX), 1) >> level
        shift = mark - column + REACH
        rim_shift = lane_place - column + REACH
        same = lane_place == line_place
        pick = (lane_z == iota((CX, 8), 1)).astype(F32)
        pick_t = (line_z == iota((8, CX), 0)).astype(F32)
        for r in range(2):
            part = slice(r * CX, (r + 1) * CX)
            taps = jnp.zeros((CX, CX), F32)
            rims = jnp.zeros((CX, CX), F32)
            for t in range(TAPS):
                tap = along_ref[level, r, t]
                taps = jnp.where(shift == t, tap, taps)
                rims = jnp.where(rim_shift == t, tap, rims)
            high, low = split(taps * scale)
            own_ref[level, :CX, part] = high
            own_ref[level, CX:, part] = high
            own_low_ref[level, :, part] = low
            high, low = split(rims * scale)
            for z in range(PLANES):
                mine = jnp.broadcast_to((lane_z == z).astype(F32), (CX, CX)).astype(BF16)
                rim_high[level, part, z * CX : (z + 1) * CX] = high * mine
                rim_low[level, part, z * CX : (z + 1) * CX] = low * mine
            mixes = lax.dot_general(
                pick, mix_ref[level, r], (((1,), (1,)), ((), ())), precision=exact,
                preferred_element_type=F32,
            )
            mixes = jnp.dot(mixes, pick_t, precision=exact, preferred_element_type=F32)
            high, low = split(jnp.where(same, mixes, 0.0))
            blend_high[level, :, part] = high
            blend_low[level, :, part] = low
        size, step = HEIGHTS[level], STEP[level]
        rows = slice(ROW_OF[level], ROW_OF[level] + size)
        mine = height_of(iota((size, 1), 0), level)
        for start in range(0, 2 * step, CX):
            lanes = min(CX, 2 * step - start)
            place = iota((1, lanes), 1) + start
            second = place >= step
            place = jnp.where(second, place - step, place)
            other = jnp.where(place < size, height_of(place, level), 4 * NY)
            shift = other - mine + REACH
            taps = jnp.zeros((size, lanes), F32)
            for t in range(TAPS):
                tap = jnp.where(second, across_ref[level, 1, t], across_ref[level, 0, t])
                taps = jnp.where(shift == t, tap, taps)
            high, low = split(taps)
            across_high[rows, start : start + lanes] = high
            across_low[rows, start : start + lanes] = low


def brick_kernel(ref, bricks, hot, match, weights):
    packed = ref[CELLS:, :]
    meta = jnp.concatenate([packed, turn(packed, CX // 2)], axis=0)
    cells = [ref[s * CAP : (s + 1) * CAP, :] for s in range(SLOTS)]
    totals = [None] * PLANES
    for s in range(SLOTS):
        current = meta[:, 16 * s + 8 : 16 * s + 9]
        for z in range(PLANES):
            piece = cells[s] * meta[:, 16 * s + z : 16 * s + z + 1]
            weights[s * PLANES + z] = piece
            piece = piece * current
            totals[z] = piece if s == 0 else totals[z] + piece
    for z in range(PLANES):
        high, low = split(totals[z])
        bricks[:CAP, z * CX : (z + 1) * CX] = high
        bricks[:CAP, HALF + z * CX : HALF + (z + 1) * CX] = low
    bricks[CAP:, :] = jnp.zeros((CX - CAP, 2 * HALF), BF16)
    whole = jnp.concatenate([meta, jnp.zeros((CX - CAP, CX), F32)], axis=0)
    names = jnp.where(iota((1, CX), 1) < CAP, whole.T[9:10, :], -1.0)
    hot[...] = flags(iota((TILES, CX), 0).astype(F32) == names)
    match[...] = flags(iota((CAP, TILES), 1).astype(F32) == meta[:, 9:10])


def charge_kernel(*refs):
    bricks, hots = refs[:PEERS], refs[PEERS : 2 * PEERS]
    q0, s1, s2, s3, s4, to_right, to_left = refs[2 * PEERS + 1 : -4]
    rims = refs[-4:]
    hot = jnp.concatenate([ref[...] for ref in hots], axis=1)
    lanes = iota((1, CX), 1)
    for pair in range(PLANES // 2):
        part = slice(pair * 2 * CX, (pair + 1) * 2 * CX)
        lower = slice(HALF + pair * 2 * CX, HALF + (pair + 1) * 2 * CX)
        found = dot(hot, jnp.concatenate([ref[:, part] for ref in bricks], axis=0)) + dot(
            hot, jnp.concatenate([ref[:, lower] for ref in bricks], axis=0)
        )
        for i in range(2):
            z = 2 * pair + i
            plane = found[:, i * CX : (i + 1) * CX]
            bands = swap_groups([plane[b * BAND : (b + 1) * BAND] for b in range(8)])
            level = 0
            while True:
                size, log = HEIGHTS[level], level + 3
                target = (q0, s1, s2, s3)[level]
                for b, band in enumerate(bands):
                    rows = slice(b * BAND, (b + 1) * BAND)
                    target[z, rows, :] = band
                    block, offset = z >> level, z & ((1 << level) - 1)
                    first = turn(band, (block << log) + offset)
                    last = turn(band, offset - (block << log)) if block else first
                    mine = (lanes & ((1 << level) - 1)) == offset
                    left = mine & ((lanes >> log) == block) & (lanes < CX // 2)
                    right = mine & (((CX - 1 - lanes) >> log) == block) & (lanes >= CX // 2)
                    held = rims[level][rows, :] if z else jnp.zeros((BAND, CX), F32)
                    held = jnp.where(left, first, jnp.where(right, last, held))
                    rims[level][rows, :] = held
                if level == 3:
                    break
                sums = [bands[2 * b] + bands[2 * b + 1] for b in range(len(bands) // 2)]
                bands = [value + turn(value, -(1 << level)) for value in sums]
                level += 1
    size = HEIGHTS[LEVELS]
    coarse = jnp.zeros((size, CX), F32)
    for z in range(PLANES):
        value = s3[z, pl.ds(0, size, stride=2), :] + s3[z, pl.ds(1, size, stride=2), :]
        value = value + turn(value, -8)
        s4[z] = value
        coarse = jnp.where((lanes & 15) == z, turn(value, z), coarse)
    to_right[NY:, :] = coarse
    to_left[NY:, :] = coarse
    to_right[RIM_ROW[3] + HEIGHTS[3] : NY, :] = rims[0][RIM_ROW[3] + HEIGHTS[3] : NY, :]
    to_left[RIM_ROW[3] + HEIGHTS[3] : NY, :] = rims[0][RIM_ROW[3] + HEIGHTS[3] : NY, :]
    for level in range(1, LEVELS):
        rows = slice(RIM_ROW[level], RIM_ROW[level] + HEIGHTS[level])
        other = turn(rims[level][...], CX // 2)
        to_right[rows, :] = jnp.where(lanes < CX // 2, other, rims[0][rows, :])
        to_left[rows, :] = jnp.where(lanes < CX // 2, rims[0][rows, :], other)


def inner_kernel(
    mix_ref, q0, s1, s2, s3, s4, own_ref, own_low_ref, across_high, across_low, out_ref, ranked,
    high_ref, low_ref
):
    for level, source in enumerate((q0, s1, s2, s3, s4)):
        size, step = HEIGHTS[level], STEP[level]
        for z in range(PLANES):
            high, low = split(source[z])
            ranked[z, :size, :] = dot(
                jnp.concatenate([high, low], axis=1), own_ref[level]
            ) + dot(high, own_low_ref[level])
        chunk = {384: 32, 192: 32, 96: 32, 48: 16, 24: 24}[size]

        def mixed(index, carry, level=level, chunk=chunk, step=step):
            start = index * chunk
            if not isinstance(start, int):
                start = pl.multiple_of(start, chunk)
            for r in range(2):
                parts = [
                    ranked[w, pl.ds(start, chunk), r * CX : (r + 1) * CX] for w in range(PLANES)
                ]
                for z in range(PLANES):
                    total = parts[0] * mix_ref[level, r, z, 0]
                    for w in range(1, PLANES):
                        total = total + parts[w] * mix_ref[level, r, z, w]
                    if chunk == 24:
                        total = jnp.concatenate([total, jnp.zeros((8, CX), F32)], axis=0)
                    high, low = split(total)
                    place = pl.ds(r * step + start, high.shape[0])
                    high_ref[place, z * CX : (z + 1) * CX] = high
                    low_ref[place, z * CX : (z + 1) * CX] = low
            return carry

        if size == chunk:
            mixed(0, 0)
        else:
            lax.fori_loop(0, size // chunk, mixed, 0)
        rows = slice(ROW_OF[level], ROW_OF[level] + size)
        heavy, light = across_high[rows, : 2 * step], across_low[rows, : 2 * step]
        for pair in range(PLANES // 2):
            part = slice(pair * 2 * CX, (pair + 1) * 2 * CX)
            high = high_ref[: 2 * step, part]
            out_ref[rows, part] = (
                dot(heavy, high) + dot(heavy, low_ref[: 2 * step, part]) + dot(light, high)
            )


def outer_kernel(*refs):
    inner, from_left, from_right, across_high, across_low = refs[:5]
    blend_high, blend_low, rim_high, rim_low = refs[5:9]
    matches, weights = refs[9 : 9 + PEERS], refs[9 + PEERS : 9 + 2 * PEERS]
    grid_ref = refs[9 + 2 * PEERS]
    outs = refs[10 + 2 * PEERS : 10 + 3 * PEERS]
    high_ref, low_ref, tiles, picked, doubled = refs[10 + 3 * PEERS :]
    lanes = iota((1, CX), 1)
    high_ref[...] = jnp.zeros((ALL_K, 2 * CX), BF16)
    low_ref[...] = jnp.zeros((ALL_K, 2 * CX), BF16)
    sums = []
    for level in range(LEVELS + 1):
        size, step = HEIGHTS[level], STEP[level]
        rows = slice(RIM_ROW[level], RIM_ROW[level] + size)
        if level == 0:
            rims = jnp.where(lanes < CX // 2, from_right[rows, :], from_left[rows, :])
        elif level < LEVELS:
            rims = jnp.where(lanes < CX // 2, from_left[rows, :], from_right[rows, :])
        else:
            rims = jnp.where((lanes & 15) < 8, from_left[rows, :], turn(from_right[rows, :], 8))
        high, low = split(rims)
        mixed = dot(high, blend_high[level]) + dot(low, blend_high[level])
        mixed = mixed + dot(high, blend_low[level])
        if size < step:
            mixed = jnp.concatenate([mixed, jnp.zeros((step - size, 2 * CX), F32)], axis=0)
        high, low = split(mixed)
        for r in range(2):
            part = slice(r * CX, (r + 1) * CX)
            place = slice(K_OF[level] + r * step, K_OF[level] + (r + 1) * step)
            high_ref[place, part] = high[:, part]
            low_ref[place, part] = low[:, part]
        rows = slice(ROW_OF[level], ROW_OF[level] + size)
        place = slice(K_OF[level], K_OF[level] + 2 * step)
        heavy, light = across_high[rows, : 2 * step], across_low[rows, : 2 * step]
        total = dot(heavy, high_ref[place, :]) + dot(heavy, low_ref[place, :])
        sums.append(split(total + dot(light, high_ref[place, :])))
    for pair in range(PLANES // 2):
        part = slice(pair * 2 * CX, (pair + 1) * 2 * CX)
        above = None
        for level in range(LEVELS, -1, -1):
            high, low = sums[level]
            heavy, light = rim_high[level, :, part], rim_low[level, :, part]
            value = dot(high, heavy) + dot(low, heavy) + dot(high, light)
            value = value + inner[ROW_OF[level] : ROW_OF[level] + HEIGHTS[level], part]
            if level == LEVELS:
                doubled[pl.ds(0, HEIGHTS[level], stride=2), :] = value[:, :CX]
                doubled[pl.ds(1, HEIGHTS[level], stride=2), :] = value[:, :CX]
                doubled[pl.ds(BAND, HEIGHTS[level], stride=2), :] = value[:, CX:]
                doubled[pl.ds(BAND + 1, HEIGHTS[level], stride=2), :] = value[:, CX:]
                above = [jnp.concatenate([doubled[:BAND, :], doubled[BAND:, :]], axis=1)]
                continue
            bands = 8 >> level
            fresh = []
            for b in range(bands):
                fresh.append(value[b * BAND : (b + 1) * BAND] + above[b * len(above) // bands])
            above = fresh
        for i in range(2):
            z = 2 * pair + i
            planes = [band[:, i * CX : (i + 1) * CX] for band in above]
            for b in range(8):
                grid_ref[z, pl.ds(b, BAND, stride=8), :] = planes[b]
            for b, band in enumerate(swap_groups(planes)):
                high, low = split(band)
                rows = slice(b * BAND, (b + 1) * BAND)
                tiles[rows, z * CX : (z + 1) * CX] = high
                tiles[rows, HALF + z * CX : HALF + (z + 1) * CX] = low
    for j in range(PEERS):
        match = matches[j][...]
        for pair in range(PLANES // 2):
            part = slice(pair * 2 * CX, (pair + 1) * 2 * CX)
            lower = slice(HALF + pair * 2 * CX, HALF + (pair + 1) * 2 * CX)
            picked[:, part] = dot(match, tiles[:, part]) + dot(match, tiles[:, lower])
        values = jnp.zeros((CAP, CX), F32)
        for s in range(SLOTS):
            total = picked[:, :CX] * weights[j][s * PLANES]
            for z in range(1, PLANES):
                total = total + picked[:, z * CX : (z + 1) * CX] * weights[j][s * PLANES + z]
            values = jnp.where(lanes == s, jnp.sum(total, axis=1, keepdims=True), values)
        values = jnp.concatenate([values, jnp.zeros((CX - CAP, CX), F32)], axis=0)
        outs[j][...] = values.T[:8, :]


def pick_kernel(count_ref, slot_ref, b0, b1, b2, b3, out_ref):
    slot = slot_ref[0:1, :]
    away = jnp.floor((slot + 0.5) * (1.0 / CAP))
    place = slot + away * (CX - CAP)
    match = (iota((PEERS * CX, BRICKS), 0).astype(F32) == place).astype(F32).astype(BF16)
    held = jnp.concatenate([b0[...], b1[...], b2[...], b3[...]], axis=1)
    high, low = split(held)
    value = dot(jnp.concatenate([high, low], axis=0), match)
    value = value[:8] + value[8:]
    spread = (iota((BRICKS, SEGS), 1) // SLOTS == iota((BRICKS, SEGS), 0)).astype(F32).astype(BF16)
    high, low = split(value)
    value = dot(jnp.concatenate([high, low], axis=0), spread)
    value = value[:8] + value[8:]
    lane = iota((8, SEGS), 1)
    mine = (lane % SLOTS == iota((8, SEGS), 0)) & (lane // SLOTS < count_ref[0])
    out_ref[...] = jnp.sum(jnp.where(mine, value, 0.0), axis=0, keepdims=True)


VMEM = pl.BlockSpec(memory_space=pltpu.VMEM)
SMEM = pl.BlockSpec(memory_space=pltpu.SMEM)
ANY = pl.BlockSpec(memory_space=pl.ANY)


def shape(*dims, kind=F32):
    return jax.ShapeDtypeStruct(dims, kind)


def call(kernel, inputs, outputs, scratch=(), megabytes=16):
    return pl.pallas_call(
        kernel,
        in_specs=list(inputs),
        out_specs=[VMEM] * len(outputs),
        out_shape=list(outputs),
        scratch_shapes=list(scratch),
        compiler_params=pltpu.CompilerParams(vmem_limit_bytes=megabytes << 20),
    )


def body(
    currents, plane_weights, cell_weights, brick_dest, brick_tile, brick_count, kern_across,
    kern_along, plane_mix,
):
    *sends, slots = call(
        route_kernel,
        [SMEM] + [ANY] * 5,
        [shape(ROWS, CX)] * PEERS + [shape(8, BRICKS)],
        [
            pltpu.VMEM((SEGS, CX), F32),
            pltpu.VMEM((1, SEGS), F32),
            pltpu.VMEM((PLANES, SEGS), F32),
            pltpu.VMEM((SEGS, CX), F32),
            pltpu.VMEM((1, BRICKS), jnp.int32),
            pltpu.VMEM((1, BRICKS), jnp.int32),
            pltpu.SemaphoreType.DMA((5,)),
        ],
    )(
        brick_count,
        currents.reshape(1, SEGS),
        plane_weights,
        cell_weights,
        brick_dest.reshape(1, BRICKS),
        brick_tile.reshape(1, BRICKS),
    )
    swaps = [[(i, i ^ k) for i in range(PEERS)] for k in range(PEERS)]
    held = [sends[0]] + [lax.ppermute(sends[k], "sect", swaps[k]) for k in range(1, PEERS)]
    prepared = call(
        prep_kernel,
        [SMEM, SMEM, VMEM],
        [
            shape(LEVELS + 1, 2 * CX, 2 * CX, kind=BF16),
            shape(LEVELS + 1, CX, 2 * CX, kind=BF16),
            shape(ALL_ROWS, 2 * NY, kind=BF16),
            shape(ALL_ROWS, 2 * NY, kind=BF16),
            shape(LEVELS + 1, CX, 2 * CX, kind=BF16),
            shape(LEVELS + 1, CX, 2 * CX, kind=BF16),
            shape(LEVELS + 1, 2 * CX, HALF, kind=BF16),
            shape(LEVELS + 1, 2 * CX, HALF, kind=BF16),
        ],
    )(kern_across, kern_along, plane_mix)
    own, own_low, across_high, across_low, *outer = prepared
    parts = [
        call(
            brick_kernel,
            [VMEM],
            [
                shape(CX, 2 * HALF, kind=BF16),
                shape(TILES, CX, kind=BF16),
                shape(CAP, TILES, kind=BF16),
                shape(SLOTS * PLANES, CAP, CX),
            ],
        )(value)
        for value in held
    ]
    bricks, hots, matches, weights = zip(*parts)
    *fields, to_right, to_left = call(
        charge_kernel,
        [VMEM] * 8 + [ANY],
        [shape(PLANES, size, CX) for size in HEIGHTS] + [shape(RIM_ROWS, CX)] * 2,
        [pltpu.VMEM((size, CX), F32) for size in HEIGHTS[:LEVELS]],
    )(*bricks, *hots, own)
    axes = ("strip", "sect")
    devices = lax.axis_size(axes)
    up = [(i, i + 1) for i in range(devices - 1)]
    down = [(i + 1, i) for i in range(devices - 1)]
    from_left = lax.ppermute(to_right, axes, up)
    from_right = lax.ppermute(to_left, axes, down)
    (inner,) = call(
        inner_kernel,
        [SMEM] + [VMEM] * 9,
        [shape(ALL_ROWS, HALF)],
        [
            pltpu.VMEM((PLANES, NY, 2 * CX), F32),
            pltpu.VMEM((2 * NY, HALF), BF16),
            pltpu.VMEM((2 * NY, HALF), BF16),
        ],
    )(plane_mix, *fields, own, own_low, across_high, across_low)
    grid, *samples = call(
        outer_kernel,
        [VMEM] * (9 + 2 * PEERS),
        [shape(PLANES, NY, CX)] + [shape(8, CX)] * PEERS,
        [
            pltpu.VMEM((ALL_K, 2 * CX), BF16),
            pltpu.VMEM((ALL_K, 2 * CX), BF16),
            pltpu.VMEM((TILES, 2 * HALF), BF16),
            pltpu.VMEM((CAP, HALF), F32),
            pltpu.VMEM((2 * BAND, CX), F32),
        ],
    )(inner, from_left, from_right, across_high, across_low, *outer, *matches, *weights)
    back = [samples[0]] + [lax.ppermute(samples[k], "sect", swaps[k]) for k in range(1, PEERS)]
    (segments,) = call(
        pick_kernel, [SMEM] + [VMEM] * 5, [shape(1, SEGS)]
    )(brick_count, slots, *back)
    return grid, segments.reshape(SEGS)


def solution(mesh):
    flat = ("strip", "sect")
    placed = (
        P(flat), P(None, flat), P(flat, None), P(flat, None), P(flat), P(flat), P(), P(), P(),
    )
    return jax.shard_map(
        body,
        mesh=mesh,
        in_specs=placed,
        out_specs=(P(None, None, flat), P(flat)),
        check_vma=False,
    )
```

```python
import jax
import jax.numpy as jnp
from jax import lax
from jax.experimental import pallas as pl
from jax.experimental.pallas import tpu as pltpu
from jax.sharding import PartitionSpec as P

NY = 384
CX = 128
LEVELS = 4
TILES = 384
PLANES = 8
TAPS = 17
REACH = TAPS // 2
SLOTS = 4
BRICKS = 256
CAP = 96
PEERS = 4
CELLS = SLOTS * CAP
PACK = CAP // 2
ROWS = CELLS + PACK
SEGS = BRICKS * SLOTS
BAND = NY // 8
HALF = PLANES * CX
HEIGHTS = tuple(NY >> level for level in range(LEVELS + 1))
WIDTHS = tuple(CX >> level for level in range(LEVELS + 1))
STEP = (384, 192, 96, 48, 32)
ROW_OF = (0, 384, 576, 672, 720)
ALL_ROWS = 752
K_OF = (0, 768, 1152, 1344, 1440)
ALL_K = 1504
RIM_ROW = (0, 0, 192, 288, 384)
RIM_ROWS = NY + HEIGHTS[LEVELS]
F32 = jnp.float32
BF16 = jnp.bfloat16


def split(value):
    high = value.astype(BF16)
    return high, (value - high.astype(F32)).astype(BF16)


def dot(left, right):
    return jnp.dot(left, right, preferred_element_type=F32)


def iota(shape, dim):
    return lax.broadcasted_iota(jnp.int32, shape, dim)


def flags(condition):
    return condition.astype(F32).astype(BF16)


def turn(value, amount):
    amount = amount % CX
    return pltpu.roll(value, amount, 1) if amount else value


def swap_groups(bands):
    group = iota((1, CX), 1) // 16
    for bit in range(3):
        step = 1 << bit
        upper = ((group >> bit) & 1) == 1
        fresh = []
        for i in range(8):
            other = bands[i ^ step]
            if i & step:
                fresh.append(jnp.where(upper, bands[i], turn(other, -16 * step)))
            else:
                fresh.append(jnp.where(upper, turn(other, 16 * step), bands[i]))
        bands = fresh
    return bands


def route_kernel(
    count_ref, currents_hbm, planes_hbm, cells_hbm, dest_hbm, tile_hbm, *refs
):
    outs, slot_ref = refs[:PEERS], refs[PEERS]
    feature, currents_ref, planes_ref, cells_ref, dest_ref, tile_ref, sems = refs[PEERS + 1 :]
    pairs = (
        (dest_hbm, dest_ref), (tile_hbm, tile_ref), (currents_hbm, currents_ref),
        (planes_hbm, planes_ref), (cells_hbm, cells_ref),
    )
    copies = [pltpu.make_async_copy(a, b, sems.at[i]) for i, (a, b) in enumerate(pairs)]
    for copy in copies:
        copy.start()
    for copy in copies[:4]:
        copy.wait()
    me = lax.axis_index("sect")
    away = dest_ref[...] ^ me
    onehot = (iota((16, BRICKS), 0) == away).astype(F32)
    before = flags(iota((BRICKS, BRICKS), 0) < iota((BRICKS, BRICKS), 1))
    earlier = dot(onehot.astype(BF16), before)
    base = (iota((16, BRICKS), 0) * CAP).astype(F32)
    slot = jnp.sum(onehot * (earlier + base), axis=0, keepdims=True)
    slot_ref[...] = jnp.broadcast_to(slot, slot_ref.shape)
    choose = flags(iota((PEERS * CAP, BRICKS), 0).astype(F32) == slot)
    alive = (iota((1, SEGS), 1) // SLOTS < count_ref[0]).astype(F32)
    currents = currents_ref[...] * alive
    lines = jnp.concatenate(
        [planes_ref[...], currents, jnp.zeros((CX - PLANES - 1, SEGS), F32)], axis=0
    )
    for part in range(SEGS // CX):
        feature[part * CX : (part + 1) * CX, :] = lines[:, part * CX : (part + 1) * CX].T
    meta = jnp.zeros((BRICKS, CX), F32)
    for s in range(SLOTS):
        meta = meta + turn(feature[pl.ds(s, BRICKS, stride=SLOTS), :], 16 * s)
    tile = tile_ref[...]
    tile = (tile & 7) * BAND + (tile >> 3)
    tiles = jnp.concatenate([tile.astype(F32), jnp.zeros((CX - 1, BRICKS), F32)], axis=0)
    tiles = jnp.concatenate([tiles[:, :CX].T, tiles[:, CX:].T], axis=0)
    meta = meta + turn(tiles, 9)
    both = dot(choose, jnp.concatenate(split(meta), axis=1))
    both = both[:, :CX] + both[:, CX:]
    for k in range(PEERS):
        lower = both[k * CAP : k * CAP + PACK]
        upper = both[k * CAP + PACK : (k + 1) * CAP]
        outs[k][CELLS:, :] = lower + turn(upper, CX // 2)
    copies[4].wait()
    for s in range(SLOTS):
        high, low = split(cells_ref[pl.ds(s, BRICKS, stride=SLOTS), :])
        moved = dot(choose, jnp.concatenate([high, low], axis=1))
        moved = moved[:, :CX] + moved[:, CX:]
        for k in range(PEERS):
            outs[k][s * CAP : (s + 1) * CAP, :] = moved[k * CAP : (k + 1) * CAP]


def height_of(place, level):
    if level == LEVELS:
        return place
    band = (place * 1366) >> 16
    return (place - band * BAND) * (8 >> level) + band


def rim_of(lane, level):
    if level == LEVELS:
        j, rest = lane >> 4, lane & 15
        return rest & 7, jnp.where(rest < 8, j - REACH, j + WIDTHS[level])
    spot = lane if level == 0 else lane ^ (CX // 2)
    log = level + 3
    rest = spot & ((8 << level) - 1)
    j, offset = rest >> level, rest & ((1 << level) - 1)
    first = spot < CX // 2
    block = jnp.where(first, spot >> log, (CX - 1 - spot) >> log)
    return (block << level) + offset, jnp.where(first, j + WIDTHS[level], j - REACH)


def taps_at(table, shift):
    spot = jnp.where((shift >= 0) & (shift < TAPS), shift, CX - 1)
    return jnp.take_along_axis(jnp.broadcast_to(table, spot.shape), spot, axis=1)


def prep_kernel(
    across_ref, along_ref, mix_ref, own_ref, own_low_ref, across_high, across_low, blend_high,
    blend_low, rim_high, rim_low, table
):
    exact = lax.Precision.HIGHEST
    table[...] = jnp.zeros(table.shape, F32)
    for level in range(LEVELS + 1):
        for r in range(2):
            line = 4 * level + r
            table[line : line + 1, :TAPS] = along_ref[level, r : r + 1, :]
            table[line + 2 : line + 3, :TAPS] = across_ref[level, r : r + 1, :]
    for level in range(LEVELS + 1):
        scale = 0.25**level
        row = iota((CX, 1), 0)
        mark = jnp.where((row & ((1 << level) - 1)) == 0, row >> level, 4 * NY)
        lane_z, lane_place = rim_of(row, level)
        line_z, line_place = rim_of(iota((1, CX), 1), level)
        column = iota((CX, CX), 1) >> level
        shift = mark - column + REACH
        rim_shift = lane_place - column + REACH
        same = lane_place == line_place
        pick = (lane_z == iota((CX, 8), 1)).astype(F32)
        pick_t = (line_z == iota((8, CX), 0)).astype(F32)
        masks = [
            jnp.broadcast_to((lane_z == z).astype(F32), (CX, CX)).astype(BF16)
            for z in range(PLANES)
        ]
        for r in range(2):
            part = slice(r * CX, (r + 1) * CX)
            line = table[4 * level + r : 4 * level + r + 1, :]
            high, low = split(taps_at(line, shift) * scale)
            own_ref[level, :CX, part] = high
            own_ref[level, CX:, part] = high
            own_low_ref[level, :, part] = low
            high, low = split(taps_at(line, rim_shift) * scale)
            for z in range(PLANES):
                rim_high[level, part, z * CX : (z + 1) * CX] = high * masks[z]
                rim_low[level, part, z * CX : (z + 1) * CX] = low * masks[z]
            mixes = lax.dot_general(
                pick, mix_ref[level, r], (((1,), (1,)), ((), ())), precision=exact,
                preferred_element_type=F32,
            )
            mixes = jnp.dot(mixes, pick_t, precision=exact, preferred_element_type=F32)
            high, low = split(jnp.where(same, mixes, 0.0))
            blend_high[level, :, part] = high
            blend_low[level, :, part] = low
        size, step = HEIGHTS[level], STEP[level]
        rows = slice(ROW_OF[level], ROW_OF[level] + size)
        mine = height_of(iota((size, 1), 0), level)
        first = table[4 * level + 2 : 4 * level + 3, :]
        both = first + turn(table[4 * level + 3 : 4 * level + 4, :], 32)
        for start in range(0, 2 * step, CX):
            lanes = min(CX, 2 * step - start)
            place = iota((1, CX), 1) + start
            second = place >= step
            place = jnp.where(second, place - step, place)
            other = jnp.where(place < size, height_of(place, level), 4 * NY)
            shift = other - mine + REACH
            spot = jnp.where(
                (shift >= 0) & (shift < TAPS), shift + jnp.where(second, 32, 0), CX - 1
            )
            taps = jnp.take_along_axis(jnp.broadcast_to(both, spot.shape), spot, axis=1)
            high, low = split(taps[:, :lanes])
            across_high[rows, start : start + lanes] = high
            across_low[rows, start : start + lanes] = low


def brick_kernel(ref, bricks, hot, match, weights):
    packed = ref[CELLS:, :]
    meta = jnp.concatenate([packed, turn(packed, CX // 2)], axis=0)
    cells = [ref[s * CAP : (s + 1) * CAP, :] for s in range(SLOTS)]
    totals = [None] * PLANES
    for s in range(SLOTS):
        current = meta[:, 16 * s + 8 : 16 * s + 9]
        for z in range(PLANES):
            piece = cells[s] * meta[:, 16 * s + z : 16 * s + z + 1]
            weights[s * PLANES + z] = piece
            piece = piece * current
            totals[z] = piece if s == 0 else totals[z] + piece
    for z in range(PLANES):
        high, low = split(totals[z])
        bricks[:CAP, z * CX : (z + 1) * CX] = high
        bricks[:CAP, HALF + z * CX : HALF + (z + 1) * CX] = low
    bricks[CAP:, :] = jnp.zeros((CX - CAP, 2 * HALF), BF16)
    whole = jnp.concatenate([meta, jnp.zeros((CX - CAP, CX), F32)], axis=0)
    names = jnp.where(iota((1, CX), 1) < CAP, whole.T[9:10, :], -1.0)
    hot[...] = flags(iota((TILES, CX), 0).astype(F32) == names)
    match[...] = flags(iota((CAP, TILES), 1).astype(F32) == meta[:, 9:10])


def charge_kernel(*refs):
    bricks, hots = refs[:PEERS], refs[PEERS : 2 * PEERS]
    q0, s1, s2, s3, s4, to_pair, to_next = refs[2 * PEERS + 1 : -4]
    rims = refs[-4:]
    hot = jnp.concatenate([ref[...] for ref in hots], axis=1)
    lanes = iota((1, CX), 1)
    for pair in range(PLANES // 2):
        part = slice(pair * 2 * CX, (pair + 1) * 2 * CX)
        lower = slice(HALF + pair * 2 * CX, HALF + (pair + 1) * 2 * CX)
        found = dot(hot, jnp.concatenate([ref[:, part] for ref in bricks], axis=0)) + dot(
            hot, jnp.concatenate([ref[:, lower] for ref in bricks], axis=0)
        )
        for i in range(2):
            z = 2 * pair + i
            plane = found[:, i * CX : (i + 1) * CX]
            bands = swap_groups([plane[b * BAND : (b + 1) * BAND] for b in range(8)])
            level = 0
            while True:
                size, log = HEIGHTS[level], level + 3
                target = (q0, s1, s2, s3)[level]
                for b, band in enumerate(bands):
                    rows = slice(b * BAND, (b + 1) * BAND)
                    target[z, rows, :] = band
                    block, offset = z >> level, z & ((1 << level) - 1)
                    first = turn(band, (block << log) + offset)
                    last = turn(band, offset - (block << log)) if block else first
                    mine = (lanes & ((1 << level) - 1)) == offset
                    left = mine & ((lanes >> log) == block) & (lanes < CX // 2)
                    right = mine & (((CX - 1 - lanes) >> log) == block) & (lanes >= CX // 2)
                    held = rims[level][rows, :] if z else jnp.zeros((BAND, CX), F32)
                    held = jnp.where(left, first, jnp.where(right, last, held))
                    rims[level][rows, :] = held
                if level == 3:
                    break
                sums = [bands[2 * b] + bands[2 * b + 1] for b in range(len(bands) // 2)]
                bands = [value + turn(value, -(1 << level)) for value in sums]
                level += 1
    size = HEIGHTS[LEVELS]
    coarse = jnp.zeros((size, CX), F32)
    for z in range(PLANES):
        value = s3[z, pl.ds(0, size, stride=2), :] + s3[z, pl.ds(1, size, stride=2), :]
        value = value + turn(value, -8)
        s4[z] = value
        coarse = jnp.where((lanes & 15) == z, turn(value, z), coarse)
    even = (lax.axis_index("sect") & 1) == 0
    to_pair[NY:, :] = coarse
    to_next[NY:, :] = coarse
    for level in range(1, LEVELS + 1):
        if level < LEVELS:
            rows = slice(RIM_ROW[level], RIM_ROW[level] + HEIGHTS[level])
            other = turn(rims[level][...], CX // 2)
        else:
            rows = slice(RIM_ROW[3] + HEIGHTS[3], NY)
            other = jnp.zeros((NY - RIM_ROW[3] - HEIGHTS[3], CX), F32)
        right = jnp.where(lanes < CX // 2, other, rims[0][rows, :])
        left = jnp.where(lanes < CX // 2, rims[0][rows, :], other)
        to_pair[rows, :] = jnp.where(even, right, left)
        to_next[rows, :] = jnp.where(even, left, right)


def inner_kernel(
    mix_ref, q0, s1, s2, s3, s4, own_ref, own_low_ref, across_high, across_low, out_ref, ranked,
    high_ref, low_ref
):
    for level, source in enumerate((q0, s1, s2, s3, s4)):
        size, step = HEIGHTS[level], STEP[level]
        for z in range(PLANES):
            high, low = split(source[z])
            ranked[z, :size, :] = dot(
                jnp.concatenate([high, low], axis=1), own_ref[level]
            ) + dot(high, own_low_ref[level])
        chunk = {384: 64, 192: 64, 96: 48, 48: 48, 24: 24}[size]
        rows = slice(ROW_OF[level], ROW_OF[level] + size)
        heavy, light = across_high[rows, : 2 * step], across_low[rows, : 2 * step]
        for pair in range(PLANES // 2):
            for r in range(2):
                weights = [
                    [mix_ref[level, r, 2 * pair + i, w] for w in range(PLANES)] for i in range(2)
                ]
                for start in range(0, size, chunk):
                    for i in range(2):
                        total = None
                        for w in range(PLANES):
                            part = ranked[w, start : start + chunk, r * CX : (r + 1) * CX]
                            part = part * weights[i][w]
                            total = part if w == 0 else total + part
                        if chunk == 24:
                            total = jnp.concatenate([total, jnp.zeros((8, CX), F32)], axis=0)
                        high, low = split(total)
                        place = slice(r * step + start, r * step + start + high.shape[0])
                        column = slice((2 * pair + i) * CX, (2 * pair + i + 1) * CX)
                        high_ref[place, column] = high
                        low_ref[place, column] = low
            part = slice(pair * 2 * CX, (pair + 1) * 2 * CX)
            high = high_ref[: 2 * step, part]
            out_ref[rows, part] = (
                dot(heavy, high) + dot(heavy, low_ref[: 2 * step, part]) + dot(light, high)
            )


def outer_kernel(*refs):
    inner, by_pair, by_next, across_high, across_low = refs[:5]
    blend_high, blend_low, rim_high, rim_low = refs[5:9]
    matches, weights = refs[9 : 9 + PEERS], refs[9 + PEERS : 9 + 2 * PEERS]
    grid_ref = refs[9 + 2 * PEERS]
    outs = refs[10 + 2 * PEERS : 10 + 3 * PEERS]
    high_ref, low_ref, tiles, picked, doubled = refs[10 + 3 * PEERS :]
    lanes = iota((1, CX), 1)
    even = (lax.axis_index("sect") & 1) == 0
    high_ref[...] = jnp.zeros((ALL_K, 2 * CX), BF16)
    low_ref[...] = jnp.zeros((ALL_K, 2 * CX), BF16)
    sums = []
    for level in range(LEVELS + 1):
        size, step = HEIGHTS[level], STEP[level]
        rows = slice(RIM_ROW[level], RIM_ROW[level] + size)
        from_left = jnp.where(even, by_next[rows, :], by_pair[rows, :])
        from_right = jnp.where(even, by_pair[rows, :], by_next[rows, :])
        if level == 0:
            rims = jnp.where(lanes < CX // 2, from_right, from_left)
        elif level < LEVELS:
            rims = jnp.where(lanes < CX // 2, from_left, from_right)
        else:
            rims = jnp.where((lanes & 15) < 8, from_left, turn(from_right, 8))
        high, low = split(rims)
        mixed = dot(high, blend_high[level]) + dot(low, blend_high[level])
        mixed = mixed + dot(high, blend_low[level])
        if size < step:
            mixed = jnp.concatenate([mixed, jnp.zeros((step - size, 2 * CX), F32)], axis=0)
        high, low = split(mixed)
        for r in range(2):
            part = slice(r * CX, (r + 1) * CX)
            place = slice(K_OF[level] + r * step, K_OF[level] + (r + 1) * step)
            high_ref[place, part] = high[:, part]
            low_ref[place, part] = low[:, part]
        rows = slice(ROW_OF[level], ROW_OF[level] + size)
        place = slice(K_OF[level], K_OF[level] + 2 * step)
        heavy, light = across_high[rows, : 2 * step], across_low[rows, : 2 * step]
        total = dot(heavy, high_ref[place, :]) + dot(heavy, low_ref[place, :])
        sums.append(split(total + dot(light, high_ref[place, :])))
    for pair in range(PLANES // 2):
        part = slice(pair * 2 * CX, (pair + 1) * 2 * CX)
        above = None
        for level in range(LEVELS, -1, -1):
            high, low = sums[level]
            heavy, light = rim_high[level, :, part], rim_low[level, :, part]
            value = dot(high, heavy) + dot(low, heavy) + dot(high, light)
            value = value + inner[ROW_OF[level] : ROW_OF[level] + HEIGHTS[level], part]
            if level == LEVELS:
                doubled[pl.ds(0, HEIGHTS[level], stride=2), :] = value[:, :CX]
                doubled[pl.ds(1, HEIGHTS[level], stride=2), :] = value[:, :CX]
                doubled[pl.ds(BAND, HEIGHTS[level], stride=2), :] = value[:, CX:]
                doubled[pl.ds(BAND + 1, HEIGHTS[level], stride=2), :] = value[:, CX:]
                above = [jnp.concatenate([doubled[:BAND, :], doubled[BAND:, :]], axis=1)]
                continue
            bands = 8 >> level
            fresh = []
            for b in range(bands):
                fresh.append(value[b * BAND : (b + 1) * BAND] + above[b * len(above) // bands])
            above = fresh
        for i in range(2):
            z = 2 * pair + i
            planes = [band[:, i * CX : (i + 1) * CX] for band in above]
            for b in range(8):
                grid_ref[z, pl.ds(b, BAND, stride=8), :] = planes[b]
            for b, band in enumerate(swap_groups(planes)):
                high, low = split(band)
                rows = slice(b * BAND, (b + 1) * BAND)
                tiles[rows, z * CX : (z + 1) * CX] = high
                tiles[rows, HALF + z * CX : HALF + (z + 1) * CX] = low
    for j in range(PEERS):
        match = matches[j][...]
        for pair in range(PLANES // 2):
            part = slice(pair * 2 * CX, (pair + 1) * 2 * CX)
            lower = slice(HALF + pair * 2 * CX, HALF + (pair + 1) * 2 * CX)
            picked[:, part] = dot(match, tiles[:, part]) + dot(match, tiles[:, lower])
        values = jnp.zeros((CAP, CX), F32)
        for s in range(SLOTS):
            total = picked[:, :CX] * weights[j][s * PLANES]
            for z in range(1, PLANES):
                total = total + picked[:, z * CX : (z + 1) * CX] * weights[j][s * PLANES + z]
            values = jnp.where(lanes == s, jnp.sum(total, axis=1, keepdims=True), values)
        values = jnp.concatenate([values, jnp.zeros((CX - CAP, CX), F32)], axis=0)
        outs[j][...] = values.T[:8, :]


def pick_kernel(count_ref, slot_ref, b0, b1, b2, b3, out_ref):
    slot = slot_ref[0:1, :]
    away = jnp.floor((slot + 0.5) * (1.0 / CAP))
    place = slot + away * (CX - CAP)
    match = (iota((PEERS * CX, BRICKS), 0).astype(F32) == place).astype(F32).astype(BF16)
    held = jnp.concatenate([b0[...], b1[...], b2[...], b3[...]], axis=1)
    high, low = split(held)
    value = dot(jnp.concatenate([high, low], axis=0), match)
    value = value[:8] + value[8:]
    spread = (iota((BRICKS, SEGS), 1) // SLOTS == iota((BRICKS, SEGS), 0)).astype(F32).astype(BF16)
    high, low = split(value)
    value = dot(jnp.concatenate([high, low], axis=0), spread)
    value = value[:8] + value[8:]
    lane = iota((8, SEGS), 1)
    mine = (lane % SLOTS == iota((8, SEGS), 0)) & (lane // SLOTS < count_ref[0])
    out_ref[...] = jnp.sum(jnp.where(mine, value, 0.0), axis=0, keepdims=True)


VMEM = pl.BlockSpec(memory_space=pltpu.VMEM)
SMEM = pl.BlockSpec(memory_space=pltpu.SMEM)
ANY = pl.BlockSpec(memory_space=pl.ANY)
HBM = pl.BlockSpec(memory_space=pltpu.HBM)


def shape(*dims, kind=F32):
    return jax.ShapeDtypeStruct(dims, kind)


def call(kernel, inputs, outputs, scratch=(), megabytes=16):
    return pl.pallas_call(
        kernel,
        in_specs=list(inputs),
        out_specs=[VMEM] * len(outputs),
        out_shape=list(outputs),
        scratch_shapes=list(scratch),
        compiler_params=pltpu.CompilerParams(vmem_limit_bytes=megabytes << 20),
    )


def body(
    currents, plane_weights, cell_weights, brick_dest, brick_tile, brick_count, kern_across,
    kern_along, plane_mix,
):
    *sends, slots = call(
        route_kernel,
        [SMEM] + [HBM] * 5,
        [shape(ROWS, CX)] * PEERS + [shape(8, BRICKS)],
        [
            pltpu.VMEM((SEGS, CX), F32),
            pltpu.VMEM((1, SEGS), F32),
            pltpu.VMEM((PLANES, SEGS), F32),
            pltpu.VMEM((SEGS, CX), F32),
            pltpu.VMEM((1, BRICKS), jnp.int32),
            pltpu.VMEM((1, BRICKS), jnp.int32),
            pltpu.SemaphoreType.DMA((5,)),
        ],
    )(
        brick_count,
        currents.reshape(1, SEGS),
        plane_weights,
        cell_weights,
        brick_dest.reshape(1, BRICKS),
        brick_tile.reshape(1, BRICKS),
    )
    swaps = [[(i, i ^ k) for i in range(PEERS)] for k in range(PEERS)]
    held = [sends[0]] + [lax.ppermute(sends[k], "sect", swaps[k]) for k in range(1, PEERS)]
    prepared = call(
        prep_kernel,
        [VMEM, VMEM, VMEM],
        [
            shape(LEVELS + 1, 2 * CX, 2 * CX, kind=BF16),
            shape(LEVELS + 1, CX, 2 * CX, kind=BF16),
            shape(ALL_ROWS, 2 * NY, kind=BF16),
            shape(ALL_ROWS, 2 * NY, kind=BF16),
            shape(LEVELS + 1, CX, 2 * CX, kind=BF16),
            shape(LEVELS + 1, CX, 2 * CX, kind=BF16),
            shape(LEVELS + 1, 2 * CX, HALF, kind=BF16),
            shape(LEVELS + 1, 2 * CX, HALF, kind=BF16),
        ],
        [pltpu.VMEM((24, CX), F32)],
    )(kern_across, kern_along, plane_mix)
    own, own_low, across_high, across_low, *outer = prepared
    parts = [
        call(
            brick_kernel,
            [VMEM],
            [
                shape(CX, 2 * HALF, kind=BF16),
                shape(TILES, CX, kind=BF16),
                shape(CAP, TILES, kind=BF16),
                shape(SLOTS * PLANES, CAP, CX),
            ],
        )(value)
        for value in held
    ]
    bricks, hots, matches, weights = zip(*parts)
    *fields, to_pair, to_next = call(
        charge_kernel,
        [VMEM] * 8 + [ANY],
        [shape(PLANES, size, CX) for size in HEIGHTS] + [shape(RIM_ROWS, CX)] * 2,
        [pltpu.VMEM((size, CX), F32) for size in HEIGHTS[:LEVELS]],
    )(*bricks, *hots, own)
    axes = ("strip", "sect")
    devices = lax.axis_size(axes)
    paired = [(i, i ^ 1) for i in range(devices)]
    crossed = [(i, ((i + 1) ^ 1) - 1) for i in range(1, devices - 1)]
    by_pair = lax.ppermute(to_pair, axes, paired)
    by_next = lax.ppermute(to_next, axes, crossed)
    (inner,) = call(
        inner_kernel,
        [SMEM] + [VMEM] * 9,
        [shape(ALL_ROWS, HALF)],
        [
            pltpu.VMEM((PLANES, NY, 2 * CX), F32),
            pltpu.VMEM((2 * NY, HALF), BF16),
            pltpu.VMEM((2 * NY, HALF), BF16),
        ],
    )(plane_mix, *fields, own, own_low, across_high, across_low)
    grid, *samples = call(
        outer_kernel,
        [VMEM] * (9 + 2 * PEERS),
        [shape(PLANES, NY, CX)] + [shape(8, CX)] * PEERS,
        [
            pltpu.VMEM((ALL_K, 2 * CX), BF16),
            pltpu.VMEM((ALL_K, 2 * CX), BF16),
            pltpu.VMEM((TILES, 2 * HALF), BF16),
            pltpu.VMEM((CAP, HALF), F32),
            pltpu.VMEM((2 * BAND, CX), F32),
        ],
    )(inner, by_pair, by_next, across_high, across_low, *outer, *matches, *weights)
    back = [samples[0]] + [lax.ppermute(samples[k], "sect", swaps[k]) for k in range(1, PEERS)]
    (segments,) = call(
        pick_kernel, [SMEM] + [VMEM] * 5, [shape(1, SEGS)]
    )(brick_count, slots, *back)
    return grid, segments.reshape(SEGS)


def solution(mesh):
    flat = ("strip", "sect")
    placed = (
        P(flat), P(None, flat), P(flat, None), P(flat, None), P(flat), P(flat), P(), P(), P(),
    )
    return jax.shard_map(
        body,
        mesh=mesh,
        in_specs=placed,
        out_specs=(P(None, None, flat), P(flat)),
        check_vma=False,
    )
```

```python
import jax
import jax.numpy as jnp
from jax import lax
from jax.experimental import pallas as pl
from jax.experimental.pallas import tpu as pltpu
from jax.sharding import PartitionSpec as P

NY = 384
CX = 128
LEVELS = 4
TILES = 384
PLANES = 8
TAPS = 17
REACH = TAPS // 2
SLOTS = 4
BRICKS = 256
CAP = 96
PEERS = 4
CELLS = SLOTS * CAP
PACK = CAP // 2
ROWS = CELLS + PACK
SEGS = BRICKS * SLOTS
BAND = NY // 8
HALF = PLANES * CX
HEIGHTS = tuple(NY >> level for level in range(LEVELS + 1))
WIDTHS = tuple(CX >> level for level in range(LEVELS + 1))
STEP = (384, 192, 96, 48, 32)
ROW_OF = (0, 384, 576, 672, 720)
ALL_ROWS = 752
TAP_ROW = (0, 768, 1152, 1344, 1440)
K_OF = (0, 768, 1152, 1344, 1440)
ALL_K = 1504
RIM_ROW = (0, 0, 192, 288, 336)
MIX_ROW = tuple(PLANES * sum(HEIGHTS[:level]) for level in range(LEVELS + 1))
MIX_ROWS = PLANES * sum(HEIGHTS)
F32 = jnp.float32
BF16 = jnp.bfloat16


def split(value):
    high = value.astype(BF16)
    return high, (value - high.astype(F32)).astype(BF16)


def dot(left, right):
    return jnp.dot(left, right, preferred_element_type=F32)


def iota(shape, dim):
    return lax.broadcasted_iota(jnp.int32, shape, dim)


def flags(condition):
    return condition.astype(F32).astype(BF16)


def turn(value, amount):
    amount = amount % CX
    return pltpu.roll(value, amount, 1) if amount else value


def swap_groups(bands):
    group = iota((1, CX), 1) // 16
    bands = [turn(band, 16 * i) for i, band in enumerate(bands)]
    for bit in range(3):
        upper = ((group >> bit) & 1) == 1
        bands = [jnp.where(upper, bands[(i + (1 << bit)) % 8], bands[i]) for i in range(8)]
    return [turn(bands[-i % 8], -16 * i) for i in range(8)]


def route_kernel(
    count_ref, currents_hbm, planes_hbm, cells_hbm, dest_hbm, tile_hbm, *refs
):
    outs, slot_ref = refs[:PEERS], refs[PEERS]
    feature, currents_ref, planes_ref, cells_ref, dest_ref, tile_ref, sems = refs[PEERS + 1 :]
    pairs = (
        (dest_hbm, dest_ref), (tile_hbm, tile_ref), (currents_hbm, currents_ref),
        (planes_hbm, planes_ref), (cells_hbm, cells_ref),
    )
    copies = [pltpu.make_async_copy(a, b, sems.at[i]) for i, (a, b) in enumerate(pairs)]
    for copy in copies:
        copy.start()
    for copy in copies[:4]:
        copy.wait()
    me = lax.axis_index("sect")
    away = dest_ref[...] ^ me
    onehot = (iota((16, BRICKS), 0) == away).astype(F32)
    before = flags(iota((BRICKS, BRICKS), 0) < iota((BRICKS, BRICKS), 1))
    earlier = dot(onehot.astype(BF16), before)
    base = (iota((16, BRICKS), 0) * CAP).astype(F32)
    slot = jnp.sum(onehot * (earlier + base), axis=0, keepdims=True)
    slot_ref[...] = jnp.broadcast_to(slot, slot_ref.shape)
    choose = flags(iota((PEERS * CAP, BRICKS), 0).astype(F32) == slot)
    alive = (iota((1, SEGS), 1) // SLOTS < count_ref[0]).astype(F32)
    currents = currents_ref[...] * alive
    lines = jnp.concatenate(
        [planes_ref[...], currents, jnp.zeros((CX - PLANES - 1, SEGS), F32)], axis=0
    )
    for part in range(SEGS // CX):
        feature[part * CX : (part + 1) * CX, :] = lines[:, part * CX : (part + 1) * CX].T
    meta = jnp.zeros((BRICKS, CX), F32)
    for s in range(SLOTS):
        meta = meta + turn(feature[pl.ds(s, BRICKS, stride=SLOTS), :], 16 * s)
    tile = tile_ref[...]
    tile = (tile & 7) * BAND + (tile >> 3)
    tiles = jnp.concatenate([tile.astype(F32), jnp.zeros((CX - 1, BRICKS), F32)], axis=0)
    tiles = jnp.concatenate([tiles[:, :CX].T, tiles[:, CX:].T], axis=0)
    meta = meta + turn(tiles, 9)
    both = dot(choose, jnp.concatenate(split(meta), axis=1))
    both = both[:, :CX] + both[:, CX:]
    for k in range(PEERS):
        lower = both[k * CAP : k * CAP + PACK]
        upper = both[k * CAP + PACK : (k + 1) * CAP]
        outs[k][CELLS:, :] = lower + turn(upper, CX // 2)
    copies[4].wait()
    for s in range(SLOTS):
        high, low = split(cells_ref[pl.ds(s, BRICKS, stride=SLOTS), :])
        moved = dot(choose, jnp.concatenate([high, low], axis=1))
        moved = moved[:, :CX] + moved[:, CX:]
        for k in range(PEERS):
            outs[k][s * CAP : (s + 1) * CAP, :] = moved[k * CAP : (k + 1) * CAP]


def height_of(place, level):
    if level == LEVELS:
        return place
    band = (place * 1366) >> 16
    return (place - band * BAND) * (8 >> level) + band


def rim_of(lane, level):
    j = lane & 7
    before = (lane < CX // 2) == (level == 0)
    return (lane >> 3) & 7, jnp.where(before, j - REACH, j + WIDTHS[level])


def taps_at(table, shift):
    spot = jnp.where((shift >= 0) & (shift < TAPS), shift, CX - 1)
    return jnp.take_along_axis(jnp.broadcast_to(table, spot.shape), spot, axis=1)


def prep_kernel(
    across_ref, along_ref, mix_ref, own_ref, own_low_ref, across, blend_high, blend_low,
    rim_high, rim_low, gather, table
):
    exact = lax.Precision.HIGHEST
    table[...] = jnp.zeros(table.shape, F32)
    for level in range(LEVELS + 1):
        for r in range(2):
            line = 4 * level + r
            table[line : line + 1, :TAPS] = along_ref[level, r : r + 1, :]
            table[line + 2 : line + 3, :TAPS] = across_ref[level, r : r + 1, :]
    for level in range(LEVELS + 1):
        scale = 0.25**level
        row = iota((CX, 1), 0)
        mark = row >> level
        lane_z, lane_place = rim_of(row, level)
        line_z, line_place = rim_of(iota((1, CX), 1), level)
        column = iota((CX, CX), 1) >> level
        shift = mark - column + REACH
        rim_shift = lane_place - column + REACH
        same = lane_place == line_place
        edge = jnp.where(line_place < 0, line_place + WIDTHS[level], line_place - WIDTHS[level])
        for z in range(PLANES):
            chosen = flags((mark == edge) & (line_z == z))
            gather[level * PLANES + z, :CX, :] = chosen
            gather[level * PLANES + z, CX:, :] = chosen
        pick = (lane_z == iota((CX, 8), 1)).astype(F32)
        pick_t = (line_z == iota((8, CX), 0)).astype(F32)
        masks = [
            jnp.broadcast_to((lane_z == z).astype(F32), (CX, CX)).astype(BF16)
            for z in range(PLANES)
        ]
        for r in range(2):
            part = slice(r * CX, (r + 1) * CX)
            line = table[4 * level + r : 4 * level + r + 1, :]
            high, low = split(taps_at(line, shift) * scale)
            own_ref[level, :CX, part] = high
            own_ref[level, CX:, part] = high
            own_low_ref[level, :, part] = low
            high, low = split(taps_at(line, rim_shift) * scale)
            for z in range(PLANES):
                rim_high[level, part, z * CX : (z + 1) * CX] = high * masks[z]
                rim_low[level, part, z * CX : (z + 1) * CX] = low * masks[z]
            mixes = lax.dot_general(
                pick, mix_ref[level, r], (((1,), (1,)), ((), ())), precision=exact,
                preferred_element_type=F32,
            )
            mixes = jnp.dot(mixes, pick_t, precision=exact, preferred_element_type=F32)
            high, low = split(jnp.where(same, mixes, 0.0))
            blend_high[level, :, part] = high
            blend_low[level, :, part] = low
        size, step = HEIGHTS[level], STEP[level]
        upper = slice(TAP_ROW[level], TAP_ROW[level] + size)
        lower = slice(TAP_ROW[level] + step, TAP_ROW[level] + step + size)
        mine = height_of(iota((size, 1), 0), level)
        first = table[4 * level + 2 : 4 * level + 3, :]
        both = first + turn(table[4 * level + 3 : 4 * level + 4, :], 32)
        for start in range(0, 2 * step, CX):
            lanes = min(CX, 2 * step - start)
            place = iota((1, CX), 1) + start
            second = place >= step
            place = jnp.where(second, place - step, place)
            other = jnp.where(place < size, height_of(place, level), 4 * NY)
            shift = other - mine + REACH
            spot = jnp.where(
                (shift >= 0) & (shift < TAPS), shift + jnp.where(second, 32, 0), CX - 1
            )
            taps = jnp.take_along_axis(jnp.broadcast_to(both, spot.shape), spot, axis=1)
            high, low = split(taps[:, :lanes])
            across[upper, start : start + lanes] = high
            across[lower, start : start + lanes] = low


def brick_products(ref, match, weights, bricks):
    packed = ref[CELLS:, :]
    meta = jnp.concatenate([packed, turn(packed, CX // 2)], axis=0)
    cells = [ref[s * CAP : (s + 1) * CAP, :] for s in range(SLOTS)]
    totals = [None] * PLANES
    for s in range(SLOTS):
        current = meta[:, 16 * s + 8 : 16 * s + 9]
        for z in range(PLANES):
            piece = cells[s] * meta[:, 16 * s + z : 16 * s + z + 1]
            weights[s * PLANES + z] = piece
            piece = piece * current
            totals[z] = piece if s == 0 else totals[z] + piece
    blank = jnp.zeros((CX - CAP, HALF), BF16)
    bricks[CAP:CX, :] = blank
    bricks[CX + CAP :, :] = blank
    for z in range(PLANES):
        high, low = split(totals[z])
        bricks[:CAP, z * CX : (z + 1) * CX] = high
        bricks[CX : CX + CAP, z * CX : (z + 1) * CX] = low
    whole = jnp.concatenate([meta, jnp.zeros((CX - CAP, CX), F32)], axis=0)
    names = jnp.where(iota((1, CX), 1) < CAP, whole.T[9:10, :], -1.0)
    match[...] = flags(iota((CAP, TILES), 1).astype(F32) == meta[:, 9:10])
    hot = flags(iota((TILES, CX), 0).astype(F32) == names)
    return jnp.concatenate([hot, hot], axis=1)


def brick_kernel(ref, *refs):
    match, weights, total, bricks = refs[-4:]
    hot = brick_products(ref, match, weights, bricks)
    for pair in range(PLANES // 2):
        part = slice(pair * 2 * CX, (pair + 1) * 2 * CX)
        found = dot(hot, bricks[:, part])
        total[:, part] = refs[0][:, part] + found if len(refs) > 4 else found


def charge_kernel(
    ref, partial, gather, match, weights, q0, s1, s2, s3, s4, to_pair, to_next, bricks, *rims
):
    hot = brick_products(ref, match, weights, bricks)
    lanes = iota((1, CX), 1)
    for pair in range(PLANES // 2):
        part = slice(pair * 2 * CX, (pair + 1) * 2 * CX)
        found = partial[:, part] + dot(hot, bricks[:, part])
        for i in range(2):
            z = 2 * pair + i
            plane = found[:, i * CX : (i + 1) * CX]
            bands = swap_groups([plane[b * BAND : (b + 1) * BAND] for b in range(8)])
            for level in range(LEVELS):
                plain = jnp.concatenate(bands, axis=0)
                (q0, s1, s2, s3)[level][z] = plain
                found_rims = dot(
                    jnp.concatenate(split(plain), axis=1), gather[level * PLANES + z]
                )
                rims[level][...] = rims[level][...] + found_rims if z else found_rims
                bands = [bands[2 * b] + bands[2 * b + 1] for b in range(len(bands) // 2)]
    size = HEIGHTS[LEVELS]
    coarse = jnp.zeros((size, CX), F32)
    for z in range(PLANES):
        value = s3[z, pl.ds(0, size, stride=2), :] + s3[z, pl.ds(1, size, stride=2), :]
        s4[z] = value
        coarse = coarse + dot(
            jnp.concatenate(split(value), axis=1), gather[LEVELS * PLANES + z]
        )
    even = (lax.axis_index("sect") & 1) == 0
    for level in range(1, LEVELS + 2):
        if level < LEVELS:
            rows = slice(RIM_ROW[level], RIM_ROW[level] + HEIGHTS[level])
            other = rims[level][...]
        elif level == LEVELS:
            rows, other = slice(RIM_ROW[level], RIM_ROW[level] + size), coarse
        else:
            rows = slice(RIM_ROW[LEVELS] + size, NY)
            other = jnp.zeros((NY - RIM_ROW[LEVELS] - size, CX), F32)
        right = jnp.where(lanes < CX // 2, rims[0][rows, :], other)
        left = jnp.where(lanes < CX // 2, other, rims[0][rows, :])
        to_pair[rows, :] = jnp.where(even, right, left)
        to_next[rows, :] = jnp.where(even, left, right)


def inner_kernel(
    mix_ref, q0, s1, s2, s3, s4, own_ref, own_low_ref, across, out_ref, ranked, high_ref, low_ref
):
    sources = (q0, s1, s2, s3, s4)

    def along(level):
        size = HEIGHTS[level]
        for z in range(PLANES):
            high, low = split(sources[level][z])
            found = dot(jnp.concatenate([high, low], axis=1), own_ref[level])
            rows = slice(MIX_ROW[level] + z * size, MIX_ROW[level] + (z + 1) * size)
            ranked[rows, :] = found + dot(high, own_low_ref[level])

    def blend(level, r):
        size, step = HEIGHTS[level], STEP[level]
        chunk = 24 if size < 32 else (48 if size == 48 else 32)
        chunk = 16 if chunk == 48 else chunk
        for start in range(0, size, chunk):
            parts = []
            for w in range(PLANES):
                line = MIX_ROW[level] + w * size + start
                parts.append(ranked[line : line + chunk, r * CX : (r + 1) * CX])
            for z in range(PLANES):
                total = parts[0] * mix_ref[level, r, z, 0]
                for w in range(1, PLANES):
                    total = total + parts[w] * mix_ref[level, r, z, w]
                if chunk == 24:
                    total = jnp.concatenate([total, jnp.zeros((8, CX), F32)], axis=0)
                high, low = split(total)
                line = TAP_ROW[level] + r * step + start
                high_ref[line : line + high.shape[0], z * CX : (z + 1) * CX] = high
                low_ref[line : line + high.shape[0], z * CX : (z + 1) * CX] = low

    def combine(level):
        size, step = HEIGHTS[level], STEP[level]
        rows = slice(ROW_OF[level], ROW_OF[level] + size)
        lines = slice(TAP_ROW[level], TAP_ROW[level] + 2 * step)
        taps = across[lines, : 2 * step]
        for pair in range(PLANES // 2):
            part = slice(pair * 2 * CX, (pair + 1) * 2 * CX)
            found = dot(taps, high_ref[lines, part])
            found = found[:size] + found[step : step + size]
            out_ref[rows, part] = found + dot(taps[:step], low_ref[lines, part])[:size]

    along(0)
    blend(0, 0)
    blend(0, 1)
    for level in range(1, LEVELS + 1):
        along(level)
    combine(0)
    for level in range(1, LEVELS + 1):
        blend(level, 0)
        blend(level, 1)
    for level in range(1, LEVELS + 1):
        combine(level)


def outer_kernel(*refs):
    inner, by_pair, by_next, across = refs[:4]
    blend_high, blend_low, rim_high, rim_low = refs[4:8]
    matches, weights = refs[8 : 8 + PEERS], refs[8 + PEERS : 8 + 2 * PEERS]
    grid_ref = refs[8 + 2 * PEERS]
    outs = refs[9 + 2 * PEERS : 9 + 3 * PEERS]
    high_ref, low_ref, tiles, picked, doubled = refs[9 + 3 * PEERS :]
    lanes = iota((1, CX), 1)
    even = (lax.axis_index("sect") & 1) == 0
    high_ref[...] = jnp.zeros((ALL_K, 2 * CX), BF16)
    low_ref[...] = jnp.zeros((ALL_K, 2 * CX), BF16)
    sums = []
    for level in range(LEVELS + 1):
        size, step = HEIGHTS[level], STEP[level]
        rows = slice(RIM_ROW[level], RIM_ROW[level] + size)
        from_left = jnp.where(even, by_next[rows, :], by_pair[rows, :])
        from_right = jnp.where(even, by_pair[rows, :], by_next[rows, :])
        if level == 0:
            rims = jnp.where(lanes < CX // 2, from_left, from_right)
        else:
            rims = jnp.where(lanes < CX // 2, from_right, from_left)
        high, low = split(rims)
        mixed = dot(high, blend_high[level]) + dot(low, blend_high[level])
        mixed = mixed + dot(high, blend_low[level])
        if size < step:
            mixed = jnp.concatenate([mixed, jnp.zeros((step - size, 2 * CX), F32)], axis=0)
        high, low = split(mixed)
        for r in range(2):
            part = slice(r * CX, (r + 1) * CX)
            place = slice(K_OF[level] + r * step, K_OF[level] + (r + 1) * step)
            high_ref[place, part] = high[:, part]
            low_ref[place, part] = low[:, part]
        place = slice(K_OF[level], K_OF[level] + 2 * step)
        taps = across[TAP_ROW[level] : TAP_ROW[level] + 2 * step, : 2 * step]
        found = dot(taps, high_ref[place, :])
        found = found[:step] + found[step:] + dot(taps[:step], low_ref[place, :])
        sums.append(jnp.concatenate(split(found), axis=0))
    for pair in range(PLANES // 2):
        part = slice(pair * 2 * CX, (pair + 1) * 2 * CX)
        above = None
        for level in range(LEVELS, -1, -1):
            size, step = HEIGHTS[level], STEP[level]
            value = dot(sums[level], rim_high[level, :, part])
            value = value[:size] + value[step : step + size]
            value = value + dot(sums[level][:step], rim_low[level, :, part])[:size]
            value = value + inner[ROW_OF[level] : ROW_OF[level] + HEIGHTS[level], part]
            if level == LEVELS:
                doubled[pl.ds(0, HEIGHTS[level], stride=2), :] = value[:, :CX]
                doubled[pl.ds(1, HEIGHTS[level], stride=2), :] = value[:, :CX]
                doubled[pl.ds(BAND, HEIGHTS[level], stride=2), :] = value[:, CX:]
                doubled[pl.ds(BAND + 1, HEIGHTS[level], stride=2), :] = value[:, CX:]
                above = [jnp.concatenate([doubled[:BAND, :], doubled[BAND:, :]], axis=1)]
                continue
            bands = 8 >> level
            fresh = []
            for b in range(bands):
                fresh.append(value[b * BAND : (b + 1) * BAND] + above[b * len(above) // bands])
            above = fresh
        for i in range(2):
            z = 2 * pair + i
            planes = [band[:, i * CX : (i + 1) * CX] for band in above]
            for b in range(8):
                grid_ref[z, pl.ds(b, BAND, stride=8), :] = planes[b]
            for b, band in enumerate(swap_groups(planes)):
                high, low = split(band)
                rows = slice(b * BAND, (b + 1) * BAND)
                tiles[rows, z * CX : (z + 1) * CX] = high
                tiles[rows, HALF + z * CX : HALF + (z + 1) * CX] = low
    match = jnp.concatenate([ref[...] for ref in matches], axis=0)
    for pair in range(PLANES // 2):
        part = slice(pair * 2 * CX, (pair + 1) * 2 * CX)
        lower = slice(HALF + pair * 2 * CX, HALF + (pair + 1) * 2 * CX)
        picked[:, part] = dot(match, tiles[:, part]) + dot(match, tiles[:, lower])
    for j in range(PEERS):
        mine = slice(j * CAP, (j + 1) * CAP)
        values = jnp.zeros((CAP, CX), F32)
        for s in range(SLOTS):
            total = picked[mine, :CX] * weights[j][s * PLANES]
            for z in range(1, PLANES):
                total = total + picked[mine, z * CX : (z + 1) * CX] * weights[j][s * PLANES + z]
            values = jnp.where(lanes == s, jnp.sum(total, axis=1, keepdims=True), values)
        values = jnp.concatenate([values, jnp.zeros((CX - CAP, CX), F32)], axis=0)
        outs[j][...] = values.T[:8, :]


def pick_kernel(count_ref, slot_ref, b0, b1, b2, b3, out_ref):
    slot = slot_ref[0:1, :]
    away = jnp.floor((slot + 0.5) * (1.0 / CAP))
    place = slot + away * (CX - CAP)
    match = (iota((PEERS * CX, BRICKS), 0).astype(F32) == place).astype(F32).astype(BF16)
    held = jnp.concatenate([b0[...], b1[...], b2[...], b3[...]], axis=1)
    high, low = split(held)
    value = dot(jnp.concatenate([high, low], axis=0), match)
    value = value[:8] + value[8:]
    spread = (iota((BRICKS, SEGS), 1) // SLOTS == iota((BRICKS, SEGS), 0)).astype(F32).astype(BF16)
    high, low = split(value)
    value = dot(jnp.concatenate([high, low], axis=0), spread)
    value = value[:8] + value[8:]
    lane = iota((8, SEGS), 1)
    mine = (lane % SLOTS == iota((8, SEGS), 0)) & (lane // SLOTS < count_ref[0])
    out_ref[...] = jnp.sum(jnp.where(mine, value, 0.0), axis=0, keepdims=True)


VMEM = pl.BlockSpec(memory_space=pltpu.VMEM)
SMEM = pl.BlockSpec(memory_space=pltpu.SMEM)
ANY = pl.BlockSpec(memory_space=pl.ANY)
HBM = pl.BlockSpec(memory_space=pltpu.HBM)


def shape(*dims, kind=F32):
    return jax.ShapeDtypeStruct(dims, kind)


def call(kernel, inputs, outputs, scratch=(), megabytes=16):
    return pl.pallas_call(
        kernel,
        in_specs=list(inputs),
        out_specs=[VMEM] * len(outputs),
        out_shape=list(outputs),
        scratch_shapes=list(scratch),
        compiler_params=pltpu.CompilerParams(vmem_limit_bytes=megabytes << 20),
    )


def body(
    currents, plane_weights, cell_weights, brick_dest, brick_tile, brick_count, kern_across,
    kern_along, plane_mix,
):
    *sends, slots = call(
        route_kernel,
        [SMEM] + [HBM] * 5,
        [shape(ROWS, CX)] * PEERS + [shape(8, BRICKS)],
        [
            pltpu.VMEM((SEGS, CX), F32),
            pltpu.VMEM((1, SEGS), F32),
            pltpu.VMEM((PLANES, SEGS), F32),
            pltpu.VMEM((SEGS, CX), F32),
            pltpu.VMEM((1, BRICKS), jnp.int32),
            pltpu.VMEM((1, BRICKS), jnp.int32),
            pltpu.SemaphoreType.DMA((5,)),
        ],
    )(
        brick_count,
        currents.reshape(1, SEGS),
        plane_weights,
        cell_weights,
        brick_dest.reshape(1, BRICKS),
        brick_tile.reshape(1, BRICKS),
    )
    swaps = [[(i, i ^ k) for i in range(PEERS)] for k in range(PEERS)]
    held = [sends[0]] + [lax.ppermute(sends[k], "sect", swaps[k]) for k in range(1, PEERS)]
    prepared = call(
        prep_kernel,
        [VMEM, VMEM, VMEM],
        [
            shape(LEVELS + 1, 2 * CX, 2 * CX, kind=BF16),
            shape(LEVELS + 1, CX, 2 * CX, kind=BF16),
            shape(ALL_K, 2 * NY, kind=BF16),
            shape(LEVELS + 1, CX, 2 * CX, kind=BF16),
            shape(LEVELS + 1, CX, 2 * CX, kind=BF16),
            shape(LEVELS + 1, 2 * CX, HALF, kind=BF16),
            shape(LEVELS + 1, 2 * CX, HALF, kind=BF16),
            shape((LEVELS + 1) * PLANES, 2 * CX, CX, kind=BF16),
        ],
        [pltpu.VMEM((24, CX), F32)],
    )(kern_across, kern_along, plane_mix)
    own, own_low, across, *outer, gather = prepared
    kept = [shape(CAP, TILES, kind=BF16), shape(SLOTS * PLANES, CAP, CX)]
    products = pltpu.VMEM((2 * CX, HALF), BF16)
    matches, weights, total = [], [], []
    for value in held[:-1]:
        match, weight, partial = call(
            brick_kernel,
            [VMEM] * (1 + len(total)),
            kept + [shape(TILES, HALF)],
            [products],
        )(value, *total)
        matches.append(match)
        weights.append(weight)
        total = [partial]
    match, weight, *fields, to_pair, to_next = call(
        charge_kernel,
        [VMEM] * 3,
        kept + [shape(PLANES, size, CX) for size in HEIGHTS] + [shape(NY, CX)] * 2,
        [products] + [pltpu.VMEM((size, CX), F32) for size in HEIGHTS[:LEVELS]],
    )(held[-1], *total, gather)
    matches.append(match)
    weights.append(weight)
    axes = ("strip", "sect")
    devices = lax.axis_size(axes)
    paired = [(i, i ^ 1) for i in range(devices)]
    crossed = [(i, ((i + 1) ^ 1) - 1) for i in range(1, devices - 1)]
    by_pair = lax.ppermute(to_pair, axes, paired)
    by_next = lax.ppermute(to_next, axes, crossed)
    (inner,) = call(
        inner_kernel,
        [SMEM] + [VMEM] * 8,
        [shape(ALL_ROWS, HALF)],
        [
            pltpu.VMEM((MIX_ROWS, 2 * CX), F32),
            pltpu.VMEM((ALL_K, HALF), BF16),
            pltpu.VMEM((ALL_K, HALF), BF16),
        ],
        megabytes=24,
    )(plane_mix, *fields, own, own_low, across)
    grid, *samples = call(
        outer_kernel,
        [VMEM] * (8 + 2 * PEERS),
        [shape(PLANES, NY, CX)] + [shape(8, CX)] * PEERS,
        [
            pltpu.VMEM((ALL_K, 2 * CX), BF16),
            pltpu.VMEM((ALL_K, 2 * CX), BF16),
            pltpu.VMEM((TILES, 2 * HALF), BF16),
            pltpu.VMEM((PEERS * CAP, HALF), F32),
            pltpu.VMEM((2 * BAND, CX), F32),
        ],
    )(inner, by_pair, by_next, across, *outer, *matches, *weights)
    back = [samples[0]] + [lax.ppermute(samples[k], "sect", swaps[k]) for k in range(1, PEERS)]
    (segments,) = call(
        pick_kernel, [SMEM] + [VMEM] * 5, [shape(1, SEGS)]
    )(brick_count, slots, *back)
    return grid, segments.reshape(SEGS)


def solution(mesh):
    flat = ("strip", "sect")
    placed = (
        P(flat), P(None, flat), P(flat, None), P(flat, None), P(flat), P(flat), P(), P(), P(),
    )
    return jax.shard_map(
        body,
        mesh=mesh,
        in_specs=placed,
        out_specs=(P(None, None, flat), P(flat)),
        check_vma=False,
    )
```

```python
import jax
import jax.numpy as jnp
from jax import lax
from jax.experimental import pallas as pl
from jax.experimental.pallas import tpu as pltpu
from jax.sharding import PartitionSpec as P

NY = 384
CX = 128
LEVELS = 4
TILES = 384
PLANES = 8
TAPS = 17
REACH = TAPS // 2
SLOTS = 4
BRICKS = 256
CAP = 96
PEERS = 4
CELLS = SLOTS * CAP
PACK = CAP // 2
ROWS = CELLS + PACK
SEGS = BRICKS * SLOTS
BAND = NY // 8
HALF = PLANES * CX
HEIGHTS = tuple(NY >> level for level in range(LEVELS + 1))
WIDTHS = tuple(CX >> level for level in range(LEVELS + 1))
STEP = (384, 192, 96, 48, 32)
ROW_OF = (0, 384, 576, 672, 720)
ALL_ROWS = 752
TAP_ROW = (0, 768, 1152, 1344, 1440)
K_OF = (0, 768, 1152, 1344, 1440)
ALL_K = 1504
RIM_ROW = (0, 0, 192, 288, 336)
MIX_ROW = tuple(PLANES * sum(HEIGHTS[:level]) for level in range(LEVELS + 1))
MIX_ROWS = PLANES * sum(HEIGHTS)
F32 = jnp.float32
BF16 = jnp.bfloat16


def split(value):
    high = value.astype(BF16)
    return high, (value - high.astype(F32)).astype(BF16)


def dot(left, right):
    return jnp.dot(left, right, preferred_element_type=F32)


def iota(shape, dim):
    return lax.broadcasted_iota(jnp.int32, shape, dim)


def flags(condition):
    return condition.astype(F32).astype(BF16)


def turn(value, amount):
    amount = amount % CX
    return pltpu.roll(value, amount, 1) if amount else value


def swap_groups(bands):
    group = iota((1, CX), 1) // 16
    bands = [turn(band, 16 * i) for i, band in enumerate(bands)]
    for bit in range(3):
        upper = ((group >> bit) & 1) == 1
        bands = [jnp.where(upper, bands[(i + (1 << bit)) % 8], bands[i]) for i in range(8)]
    return [turn(bands[-i % 8], -16 * i) for i in range(8)]


def route_kernel(
    count_ref, currents_hbm, planes_hbm, cells_hbm, dest_hbm, tile_hbm, *refs
):
    outs, slot_ref = refs[:PEERS], refs[PEERS]
    feature, currents_ref, planes_ref, cells_ref, dest_ref, tile_ref, sems = refs[PEERS + 1 :]
    pairs = (
        (dest_hbm, dest_ref), (tile_hbm, tile_ref), (currents_hbm, currents_ref),
        (planes_hbm, planes_ref), (cells_hbm, cells_ref),
    )
    copies = [pltpu.make_async_copy(a, b, sems.at[i]) for i, (a, b) in enumerate(pairs)]
    for copy in copies:
        copy.start()
    for copy in copies[:4]:
        copy.wait()
    me = lax.axis_index("sect")
    away = dest_ref[...] ^ me
    onehot = (iota((16, BRICKS), 0) == away).astype(F32)
    before = flags(iota((BRICKS, BRICKS), 0) < iota((BRICKS, BRICKS), 1))
    earlier = dot(onehot.astype(BF16), before)
    base = (iota((16, BRICKS), 0) * CAP).astype(F32)
    slot = jnp.sum(onehot * (earlier + base), axis=0, keepdims=True)
    slot_ref[...] = jnp.broadcast_to(slot, slot_ref.shape)
    choose = flags(iota((PEERS * CAP, BRICKS), 0).astype(F32) == slot)
    alive = (iota((1, SEGS), 1) // SLOTS < count_ref[0]).astype(F32)
    currents = currents_ref[...] * alive
    lines = jnp.concatenate(
        [planes_ref[...], currents, jnp.zeros((CX - PLANES - 1, SEGS), F32)], axis=0
    )
    for part in range(SEGS // CX):
        feature[part * CX : (part + 1) * CX, :] = lines[:, part * CX : (part + 1) * CX].T
    meta = jnp.zeros((BRICKS, CX), F32)
    for s in range(SLOTS):
        meta = meta + turn(feature[pl.ds(s, BRICKS, stride=SLOTS), :], 16 * s)
    tile = tile_ref[...]
    tile = (tile & 7) * BAND + (tile >> 3)
    tiles = jnp.concatenate([tile.astype(F32), jnp.zeros((CX - 1, BRICKS), F32)], axis=0)
    tiles = jnp.concatenate([tiles[:, :CX].T, tiles[:, CX:].T], axis=0)
    meta = meta + turn(tiles, 9)
    both = dot(choose, jnp.concatenate(split(meta), axis=1))
    both = both[:, :CX] + both[:, CX:]
    for k in range(PEERS):
        lower = both[k * CAP : k * CAP + PACK]
        upper = both[k * CAP + PACK : (k + 1) * CAP]
        outs[k][CELLS:, :] = lower + turn(upper, CX // 2)
    copies[4].wait()
    for s in range(SLOTS):
        high, low = split(cells_ref[pl.ds(s, BRICKS, stride=SLOTS), :])
        moved = dot(choose, jnp.concatenate([high, low], axis=1))
        moved = moved[:, :CX] + moved[:, CX:]
        for k in range(PEERS):
            outs[k][s * CAP : (s + 1) * CAP, :] = moved[k * CAP : (k + 1) * CAP]


def height_of(place, level):
    if level == LEVELS:
        return place
    band = (place * 1366) >> 16
    return (place - band * BAND) * (8 >> level) + band


def rim_of(lane, level):
    j = lane & 7
    before = (lane < CX // 2) == (level == 0)
    return (lane >> 3) & 7, jnp.where(before, j - REACH, j + WIDTHS[level])


def taps_at(table, shift):
    spot = jnp.where((shift >= 0) & (shift < TAPS), shift, CX - 1)
    return jnp.take_along_axis(jnp.broadcast_to(table, spot.shape), spot, axis=1)


def prep_kernel(
    across_ref, along_ref, mix_ref, own_ref, own_low_ref, across, blend_high, blend_low,
    rim_high, rim_low, gather, table
):
    exact = lax.Precision.HIGHEST
    table[...] = jnp.zeros(table.shape, F32)
    for level in range(LEVELS + 1):
        for r in range(2):
            line = 4 * level + r
            table[line : line + 1, :TAPS] = along_ref[level, r : r + 1, :]
            table[line + 2 : line + 3, :TAPS] = across_ref[level, r : r + 1, :]
    for level in range(LEVELS + 1):
        scale = 0.25**level
        row = iota((CX, 1), 0)
        mark = row >> level
        lane_z, lane_place = rim_of(row, level)
        line_z, line_place = rim_of(iota((1, CX), 1), level)
        column = iota((CX, CX), 1) >> level
        shift = mark - column + REACH
        rim_shift = lane_place - column + REACH
        same = lane_place == line_place
        edge = jnp.where(line_place < 0, line_place + WIDTHS[level], line_place - WIDTHS[level])
        for z in range(PLANES):
            chosen = flags((mark == edge) & (line_z == z))
            gather[level * PLANES + z, :CX, :] = chosen
            gather[level * PLANES + z, CX:, :] = chosen
        pick = (lane_z == iota((CX, 8), 1)).astype(F32)
        pick_t = (line_z == iota((8, CX), 0)).astype(F32)
        masks = [
            jnp.broadcast_to((lane_z == z).astype(F32), (CX, CX)).astype(BF16)
            for z in range(PLANES)
        ]
        for r in range(2):
            part = slice(r * CX, (r + 1) * CX)
            line = table[4 * level + r : 4 * level + r + 1, :]
            high, low = split(taps_at(line, shift) * scale)
            own_ref[level, :CX, part] = high
            own_ref[level, CX:, part] = high
            own_low_ref[level, :, part] = low
            high, low = split(taps_at(line, rim_shift) * scale)
            for z in range(PLANES):
                rim_high[level, part, z * CX : (z + 1) * CX] = high * masks[z]
                rim_low[level, part, z * CX : (z + 1) * CX] = low * masks[z]
            mixes = lax.dot_general(
                pick, mix_ref[level, r], (((1,), (1,)), ((), ())), precision=exact,
                preferred_element_type=F32,
            )
            mixes = jnp.dot(mixes, pick_t, precision=exact, preferred_element_type=F32)
            high, low = split(jnp.where(same, mixes, 0.0))
            blend_high[level, :, part] = high
            blend_low[level, :, part] = low
        size, step = HEIGHTS[level], STEP[level]
        upper = slice(TAP_ROW[level], TAP_ROW[level] + size)
        lower = slice(TAP_ROW[level] + step, TAP_ROW[level] + step + size)
        mine = height_of(iota((size, 1), 0), level)
        first = table[4 * level + 2 : 4 * level + 3, :]
        both = first + turn(table[4 * level + 3 : 4 * level + 4, :], 32)
        for start in range(0, 2 * step, CX):
            lanes = min(CX, 2 * step - start)
            place = iota((1, CX), 1) + start
            second = place >= step
            place = jnp.where(second, place - step, place)
            other = jnp.where(place < size, height_of(place, level), 4 * NY)
            shift = other - mine + REACH
            spot = jnp.where(
                (shift >= 0) & (shift < TAPS), shift + jnp.where(second, 32, 0), CX - 1
            )
            taps = jnp.take_along_axis(jnp.broadcast_to(both, spot.shape), spot, axis=1)
            high, low = split(taps[:, :lanes])
            across[upper, start : start + lanes] = high
            across[lower, start : start + lanes] = low


def brick_products(ref, match, weights, bricks):
    packed = ref[CELLS:, :]
    meta = jnp.concatenate([packed, turn(packed, CX // 2)], axis=0)
    cells = [ref[s * CAP : (s + 1) * CAP, :] for s in range(SLOTS)]
    totals = [None] * PLANES
    for s in range(SLOTS):
        current = meta[:, 16 * s + 8 : 16 * s + 9]
        for z in range(PLANES):
            piece = cells[s] * meta[:, 16 * s + z : 16 * s + z + 1]
            weights[s * PLANES + z] = piece
            piece = piece * current
            totals[z] = piece if s == 0 else totals[z] + piece
    blank = jnp.zeros((CX - CAP, HALF), BF16)
    bricks[CAP:CX, :] = blank
    bricks[CX + CAP :, :] = blank
    for z in range(PLANES):
        high, low = split(totals[z])
        bricks[:CAP, z * CX : (z + 1) * CX] = high
        bricks[CX : CX + CAP, z * CX : (z + 1) * CX] = low
    whole = jnp.concatenate([meta, jnp.zeros((CX - CAP, CX), F32)], axis=0)
    names = jnp.where(iota((1, CX), 1) < CAP, whole.T[9:10, :], -1.0)
    match[...] = flags(iota((CAP, TILES), 1).astype(F32) == meta[:, 9:10])
    hot = flags(iota((TILES, CX), 0).astype(F32) == names)
    return jnp.concatenate([hot, hot], axis=1)


def brick_kernel(ref, *refs):
    match, weights, total, bricks = refs[-4:]
    hot = brick_products(ref, match, weights, bricks)
    for pair in range(PLANES // 2):
        part = slice(pair * 2 * CX, (pair + 1) * 2 * CX)
        found = dot(hot, bricks[:, part])
        total[:, part] = refs[0][:, part] + found if len(refs) > 4 else found


def charge_kernel(
    ref, partial, gather, match, weights, q0, s1, s2, s3, s4, to_pair, to_next, bricks, *rims
):
    hot = brick_products(ref, match, weights, bricks)
    lanes = iota((1, CX), 1)
    for pair in range(PLANES // 2):
        part = slice(pair * 2 * CX, (pair + 1) * 2 * CX)
        found = partial[:, part] + dot(hot, bricks[:, part])
        for i in range(2):
            z = 2 * pair + i
            plane = found[:, i * CX : (i + 1) * CX]
            bands = swap_groups([plane[b * BAND : (b + 1) * BAND] for b in range(8)])
            for level in range(LEVELS):
                plain = jnp.concatenate(bands, axis=0)
                (q0, s1, s2, s3)[level][z] = plain
                found_rims = dot(
                    jnp.concatenate(split(plain), axis=1), gather[level * PLANES + z]
                )
                rims[level][...] = rims[level][...] + found_rims if z else found_rims
                bands = [bands[2 * b] + bands[2 * b + 1] for b in range(len(bands) // 2)]
    size = HEIGHTS[LEVELS]
    coarse = jnp.zeros((size, CX), F32)
    for z in range(PLANES):
        value = s3[z, pl.ds(0, size, stride=2), :] + s3[z, pl.ds(1, size, stride=2), :]
        s4[z] = value
        coarse = coarse + dot(
            jnp.concatenate(split(value), axis=1), gather[LEVELS * PLANES + z]
        )
    even = (lax.axis_index("sect") & 1) == 0
    for level in range(1, LEVELS + 2):
        if level < LEVELS:
            rows = slice(RIM_ROW[level], RIM_ROW[level] + HEIGHTS[level])
            other = rims[level][...]
        elif level == LEVELS:
            rows, other = slice(RIM_ROW[level], RIM_ROW[level] + size), coarse
        else:
            rows = slice(RIM_ROW[LEVELS] + size, NY)
            other = jnp.zeros((NY - RIM_ROW[LEVELS] - size, CX), F32)
        right = jnp.where(lanes < CX // 2, rims[0][rows, :], other)
        left = jnp.where(lanes < CX // 2, other, rims[0][rows, :])
        to_pair[rows, :] = jnp.where(even, right, left)
        to_next[rows, :] = jnp.where(even, left, right)


def inner_kernel(
    mix_ref, q0, s1, s2, s3, s4, own_ref, own_low_ref, across, out_ref, ranked, high_ref, low_ref
):
    sources = (q0, s1, s2, s3, s4)

    def along(level):
        size = HEIGHTS[level]
        for z in range(PLANES):
            high, low = split(sources[level][z])
            found = dot(jnp.concatenate([high, low], axis=1), own_ref[level])
            rows = slice(MIX_ROW[level] + z * size, MIX_ROW[level] + (z + 1) * size)
            ranked[rows, :] = found + dot(high, own_low_ref[level])

    def blend(level, r):
        size, step = HEIGHTS[level], STEP[level]
        chunk = 24 if size < 32 else (48 if size == 48 else 32)
        chunk = 16 if chunk == 48 else chunk
        for start in range(0, size, chunk):
            parts = []
            for w in range(PLANES):
                line = MIX_ROW[level] + w * size + start
                parts.append(ranked[line : line + chunk, r * CX : (r + 1) * CX])
            for z in range(PLANES):
                total = parts[0] * mix_ref[level, r, z, 0]
                for w in range(1, PLANES):
                    total = total + parts[w] * mix_ref[level, r, z, w]
                if chunk == 24:
                    total = jnp.concatenate([total, jnp.zeros((8, CX), F32)], axis=0)
                high, low = split(total)
                line = TAP_ROW[level] + r * step + start
                high_ref[line : line + high.shape[0], z * CX : (z + 1) * CX] = high
                low_ref[line : line + high.shape[0], z * CX : (z + 1) * CX] = low

    def combine(level):
        size, step = HEIGHTS[level], STEP[level]
        rows = slice(ROW_OF[level], ROW_OF[level] + size)
        lines = slice(TAP_ROW[level], TAP_ROW[level] + 2 * step)
        taps = across[lines, : 2 * step]
        for pair in range(PLANES // 2):
            part = slice(pair * 2 * CX, (pair + 1) * 2 * CX)
            found = dot(taps, high_ref[lines, part])
            found = found[:size] + found[step : step + size]
            out_ref[rows, part] = found + dot(taps[:step], low_ref[lines, part])[:size]

    along(0)
    blend(0, 0)
    blend(0, 1)
    for level in range(1, LEVELS + 1):
        along(level)
    combine(0)
    for level in range(1, LEVELS + 1):
        blend(level, 0)
        blend(level, 1)
    for level in range(1, LEVELS + 1):
        combine(level)


def outer_kernel(*refs):
    inner, by_pair, by_next, across = refs[:4]
    blend_high, blend_low, rim_high, rim_low = refs[4:8]
    matches, weights = refs[8 : 8 + PEERS], refs[8 + PEERS : 8 + 2 * PEERS]
    grid_ref = refs[8 + 2 * PEERS]
    outs = refs[9 + 2 * PEERS : 9 + 3 * PEERS]
    high_ref, low_ref, tiles, picked, doubled = refs[9 + 3 * PEERS :]
    lanes = iota((1, CX), 1)
    even = (lax.axis_index("sect") & 1) == 0
    high_ref[...] = jnp.zeros((ALL_K, 2 * CX), BF16)
    low_ref[...] = jnp.zeros((ALL_K, 2 * CX), BF16)
    sums = []
    for level in range(LEVELS + 1):
        size, step = HEIGHTS[level], STEP[level]
        rows = slice(RIM_ROW[level], RIM_ROW[level] + size)
        from_left = jnp.where(even, by_next[rows, :], by_pair[rows, :])
        from_right = jnp.where(even, by_pair[rows, :], by_next[rows, :])
        if level == 0:
            rims = jnp.where(lanes < CX // 2, from_left, from_right)
        else:
            rims = jnp.where(lanes < CX // 2, from_right, from_left)
        high, low = split(rims)
        mixed = dot(high, blend_high[level]) + dot(low, blend_high[level])
        mixed = mixed + dot(high, blend_low[level])
        if size < step:
            mixed = jnp.concatenate([mixed, jnp.zeros((step - size, 2 * CX), F32)], axis=0)
        high, low = split(mixed)
        for r in range(2):
            part = slice(r * CX, (r + 1) * CX)
            place = slice(K_OF[level] + r * step, K_OF[level] + (r + 1) * step)
            high_ref[place, part] = high[:, part]
            low_ref[place, part] = low[:, part]
        place = slice(K_OF[level], K_OF[level] + 2 * step)
        taps = across[TAP_ROW[level] : TAP_ROW[level] + 2 * step, : 2 * step]
        found = dot(taps, high_ref[place, :])
        found = found[:step] + found[step:] + dot(taps[:step], low_ref[place, :])
        sums.append(jnp.concatenate(split(found), axis=0))
    for pair in range(PLANES // 2):
        part = slice(pair * 2 * CX, (pair + 1) * 2 * CX)
        above = None
        for level in range(LEVELS, -1, -1):
            size, step = HEIGHTS[level], STEP[level]
            value = dot(sums[level], rim_high[level, :, part])
            value = value[:size] + value[step : step + size]
            value = value + dot(sums[level][:step], rim_low[level, :, part])[:size]
            value = value + inner[ROW_OF[level] : ROW_OF[level] + HEIGHTS[level], part]
            if level == LEVELS:
                doubled[pl.ds(0, HEIGHTS[level], stride=2), :] = value[:, :CX]
                doubled[pl.ds(1, HEIGHTS[level], stride=2), :] = value[:, :CX]
                doubled[pl.ds(BAND, HEIGHTS[level], stride=2), :] = value[:, CX:]
                doubled[pl.ds(BAND + 1, HEIGHTS[level], stride=2), :] = value[:, CX:]
                above = [jnp.concatenate([doubled[:BAND, :], doubled[BAND:, :]], axis=1)]
                continue
            bands = 8 >> level
            fresh = []
            for b in range(bands):
                fresh.append(value[b * BAND : (b + 1) * BAND] + above[b * len(above) // bands])
            above = fresh
        for i in range(2):
            z = 2 * pair + i
            planes = [band[:, i * CX : (i + 1) * CX] for band in above]
            for b in range(8):
                grid_ref[z, pl.ds(b, BAND, stride=8), :] = planes[b]
            for b, band in enumerate(swap_groups(planes)):
                high, low = split(band)
                rows = slice(b * BAND, (b + 1) * BAND)
                tiles[rows, z * CX : (z + 1) * CX] = high
                tiles[rows, HALF + z * CX : HALF + (z + 1) * CX] = low
    match = jnp.concatenate([ref[...] for ref in matches], axis=0)
    for pair in range(PLANES // 2):
        part = slice(pair * 2 * CX, (pair + 1) * 2 * CX)
        lower = slice(HALF + pair * 2 * CX, HALF + (pair + 1) * 2 * CX)
        picked[:, part] = dot(match, tiles[:, part]) + dot(match, tiles[:, lower])
    for j in range(PEERS):
        mine = slice(j * CAP, (j + 1) * CAP)
        values = jnp.zeros((CAP, CX), F32)
        for s in range(SLOTS):
            total = picked[mine, :CX] * weights[j][s * PLANES]
            for z in range(1, PLANES):
                total = total + picked[mine, z * CX : (z + 1) * CX] * weights[j][s * PLANES + z]
            values = jnp.where(lanes == s, jnp.sum(total, axis=1, keepdims=True), values)
        values = jnp.concatenate([values, jnp.zeros((CX - CAP, CX), F32)], axis=0)
        outs[j][...] = values.T[:8, :]


def pick_kernel(count_ref, slot_ref, b0, b1, b2, b3, out_ref):
    slot = slot_ref[0:1, :]
    away = jnp.floor((slot + 0.5) * (1.0 / CAP))
    place = slot + away * (CX - CAP)
    match = (iota((PEERS * CX, BRICKS), 0).astype(F32) == place).astype(F32).astype(BF16)
    held = jnp.concatenate([b0[...], b1[...], b2[...], b3[...]], axis=1)
    high, low = split(held)
    value = dot(jnp.concatenate([high, low], axis=0), match)
    value = value[:8] + value[8:]
    spread = (iota((BRICKS, SEGS), 1) // SLOTS == iota((BRICKS, SEGS), 0)).astype(F32).astype(BF16)
    high, low = split(value)
    value = dot(jnp.concatenate([high, low], axis=0), spread)
    value = value[:8] + value[8:]
    lane = iota((8, SEGS), 1)
    mine = (lane % SLOTS == iota((8, SEGS), 0)) & (lane // SLOTS < count_ref[0])
    out_ref[...] = jnp.sum(jnp.where(mine, value, 0.0), axis=0, keepdims=True)


VMEM = pl.BlockSpec(memory_space=pltpu.VMEM)
SMEM = pl.BlockSpec(memory_space=pltpu.SMEM)
ANY = pl.BlockSpec(memory_space=pl.ANY)
HBM = pl.BlockSpec(memory_space=pltpu.HBM)


def shape(*dims, kind=F32):
    return jax.ShapeDtypeStruct(dims, kind)


def call(kernel, inputs, outputs, scratch=(), megabytes=16):
    return pl.pallas_call(
        kernel,
        in_specs=list(inputs),
        out_specs=[VMEM] * len(outputs),
        out_shape=list(outputs),
        scratch_shapes=list(scratch),
        compiler_params=pltpu.CompilerParams(vmem_limit_bytes=megabytes << 20),
    )


def body(
    currents, plane_weights, cell_weights, brick_dest, brick_tile, brick_count, kern_across,
    kern_along, plane_mix,
):
    *sends, slots = call(
        route_kernel,
        [SMEM] + [HBM] * 5,
        [shape(ROWS, CX)] * PEERS + [shape(8, BRICKS)],
        [
            pltpu.VMEM((SEGS, CX), F32),
            pltpu.VMEM((1, SEGS), F32),
            pltpu.VMEM((PLANES, SEGS), F32),
            pltpu.VMEM((SEGS, CX), F32),
            pltpu.VMEM((1, BRICKS), jnp.int32),
            pltpu.VMEM((1, BRICKS), jnp.int32),
            pltpu.SemaphoreType.DMA((5,)),
        ],
        megabytes=63,
    )(
        brick_count,
        currents.reshape(1, SEGS),
        plane_weights,
        cell_weights,
        brick_dest.reshape(1, BRICKS),
        brick_tile.reshape(1, BRICKS),
    )
    swaps = [[(i, i ^ k) for i in range(PEERS)] for k in range(PEERS)]
    held = [sends[0]] + [lax.ppermute(sends[k], "sect", swaps[k]) for k in range(1, PEERS)]
    prepared = call(
        prep_kernel,
        [VMEM, VMEM, VMEM],
        [
            shape(LEVELS + 1, 2 * CX, 2 * CX, kind=BF16),
            shape(LEVELS + 1, CX, 2 * CX, kind=BF16),
            shape(ALL_K, 2 * NY, kind=BF16),
            shape(LEVELS + 1, CX, 2 * CX, kind=BF16),
            shape(LEVELS + 1, CX, 2 * CX, kind=BF16),
            shape(LEVELS + 1, 2 * CX, HALF, kind=BF16),
            shape(LEVELS + 1, 2 * CX, HALF, kind=BF16),
            shape((LEVELS + 1) * PLANES, 2 * CX, CX, kind=BF16),
        ],
        [pltpu.VMEM((24, CX), F32)],
    )(kern_across, kern_along, plane_mix)
    own, own_low, across, *outer, gather = prepared
    kept = [shape(CAP, TILES, kind=BF16), shape(SLOTS * PLANES, CAP, CX)]
    products = pltpu.VMEM((2 * CX, HALF), BF16)
    matches, weights, total = [], [], []
    for value in held[:-1]:
        match, weight, partial = call(
            brick_kernel,
            [VMEM] * (1 + len(total)),
            kept + [shape(TILES, HALF)],
            [products],
        )(value, *total)
        matches.append(match)
        weights.append(weight)
        total = [partial]
    match, weight, *fields, to_pair, to_next = call(
        charge_kernel,
        [VMEM] * 3,
        kept + [shape(PLANES, size, CX) for size in HEIGHTS] + [shape(NY, CX)] * 2,
        [products] + [pltpu.VMEM((size, CX), F32) for size in HEIGHTS[:LEVELS]],
    )(held[-1], *total, gather)
    matches.append(match)
    weights.append(weight)
    axes = ("strip", "sect")
    devices = lax.axis_size(axes)
    paired = [(i, i ^ 1) for i in range(devices)]
    crossed = [(i, ((i + 1) ^ 1) - 1) for i in range(1, devices - 1)]
    by_pair = lax.ppermute(to_pair, axes, paired)
    by_next = lax.ppermute(to_next, axes, crossed)
    (inner,) = call(
        inner_kernel,
        [SMEM] + [VMEM] * 8,
        [shape(ALL_ROWS, HALF)],
        [
            pltpu.VMEM((MIX_ROWS, 2 * CX), F32),
            pltpu.VMEM((ALL_K, HALF), BF16),
            pltpu.VMEM((ALL_K, HALF), BF16),
        ],
        megabytes=24,
    )(plane_mix, *fields, own, own_low, across)
    grid, *samples = call(
        outer_kernel,
        [VMEM] * (8 + 2 * PEERS),
        [shape(PLANES, NY, CX)] + [shape(8, CX)] * PEERS,
        [
            pltpu.VMEM((ALL_K, 2 * CX), BF16),
            pltpu.VMEM((ALL_K, 2 * CX), BF16),
            pltpu.VMEM((TILES, 2 * HALF), BF16),
            pltpu.VMEM((PEERS * CAP, HALF), F32),
            pltpu.VMEM((2 * BAND, CX), F32),
        ],
    )(inner, by_pair, by_next, across, *outer, *matches, *weights)
    back = [samples[0]] + [lax.ppermute(samples[k], "sect", swaps[k]) for k in range(1, PEERS)]
    (segments,) = call(
        pick_kernel, [SMEM] + [VMEM] * 5, [shape(1, SEGS)]
    )(brick_count, slots, *back)
    return grid, segments.reshape(SEGS)


def solution(mesh):
    flat = ("strip", "sect")
    placed = (
        P(flat), P(None, flat), P(flat, None), P(flat, None), P(flat), P(flat), P(), P(), P(),
    )
    return jax.shard_map(
        body,
        mesh=mesh,
        in_specs=placed,
        out_specs=(P(None, None, flat), P(flat)),
        check_vma=False,
    )
```

```python
import jax
import jax.numpy as jnp
from jax import lax
from jax.experimental import pallas as pl
from jax.experimental.pallas import tpu as pltpu
from jax.sharding import PartitionSpec as P

NY = 384
CX = 128
LEVELS = 4
TILES = 384
PLANES = 8
TAPS = 17
REACH = TAPS // 2
SLOTS = 4
BRICKS = 256
CAP = 96
PEERS = 4
CELLS = SLOTS * CAP
PACK = CAP // 3
SPAN = 10
WIDE = SPAN * SLOTS
ROWS = CELLS + PACK
SEGS = BRICKS * SLOTS
BAND = NY // 8
HALF = PLANES * CX
HEIGHTS = tuple(NY >> level for level in range(LEVELS + 1))
WIDTHS = tuple(CX >> level for level in range(LEVELS + 1))
STEP = (384, 192, 96, 48, 32)
ROW_OF = (0, 384, 576, 672, 720)
ALL_ROWS = 752
TAP_ROW = (0, 768, 1152, 1344, 1440)
K_OF = (0, 768, 1152, 1344, 1440)
ALL_K = 1504
RIM_ROW = (0, 0, 192, 288, 336)
MIX_ROW = tuple(PLANES * sum(HEIGHTS[:level]) for level in range(LEVELS + 1))
MIX_ROWS = PLANES * sum(HEIGHTS)
F32 = jnp.float32
BF16 = jnp.bfloat16


def split(value):
    high = value.astype(BF16)
    return high, (value - high.astype(F32)).astype(BF16)


def dot(left, right):
    return jnp.dot(left, right, preferred_element_type=F32)


def iota(shape, dim):
    return lax.broadcasted_iota(jnp.int32, shape, dim)


def flags(condition):
    return condition.astype(F32).astype(BF16)


def turn(value, amount):
    amount = amount % CX
    return pltpu.roll(value, amount, 1) if amount else value


def swap_groups(bands):
    group = iota((1, CX), 1) // 16
    bands = [turn(band, 16 * i) for i, band in enumerate(bands)]
    for bit in range(3):
        upper = ((group >> bit) & 1) == 1
        bands = [jnp.where(upper, bands[(i + (1 << bit)) % 8], bands[i]) for i in range(8)]
    return [turn(bands[-i % 8], -16 * i) for i in range(8)]


def route_kernel(
    count_ref, currents_hbm, planes_hbm, cells_hbm, dest_hbm, tile_hbm, *refs
):
    outs, slot_ref = refs[:PEERS], refs[PEERS]
    feature, currents_ref, planes_ref, cells_ref, dest_ref, tile_ref, sems = refs[PEERS + 1 :]
    pairs = (
        (dest_hbm, dest_ref), (tile_hbm, tile_ref), (currents_hbm, currents_ref),
        (planes_hbm, planes_ref), (cells_hbm, cells_ref),
    )
    copies = [pltpu.make_async_copy(a, b, sems.at[i]) for i, (a, b) in enumerate(pairs)]
    for copy in copies:
        copy.start()
    for copy in copies[:4]:
        copy.wait()
    me = lax.axis_index("sect")
    away = dest_ref[...] ^ me
    onehot = (iota((16, BRICKS), 0) == away).astype(F32)
    before = flags(iota((BRICKS, BRICKS), 0) < iota((BRICKS, BRICKS), 1))
    earlier = dot(onehot.astype(BF16), before)
    base = (iota((16, BRICKS), 0) * CAP).astype(F32)
    slot = jnp.sum(onehot * (earlier + base), axis=0, keepdims=True)
    slot_ref[...] = jnp.broadcast_to(slot, slot_ref.shape)
    choose = flags(iota((PEERS * CAP, BRICKS), 0).astype(F32) == slot)
    alive = (iota((1, SEGS), 1) // SLOTS < count_ref[0]).astype(F32)
    currents = currents_ref[...] * alive
    lines = jnp.concatenate(
        [planes_ref[...], currents, jnp.zeros((CX - PLANES - 1, SEGS), F32)], axis=0
    )
    for part in range(SEGS // CX):
        feature[part * CX : (part + 1) * CX, :] = lines[:, part * CX : (part + 1) * CX].T
    meta = jnp.zeros((BRICKS, CX), F32)
    for s in range(SLOTS):
        meta = meta + turn(feature[pl.ds(s, BRICKS, stride=SLOTS), :], SPAN * s)
    tile = tile_ref[...]
    tile = (tile & 7) * BAND + (tile >> 3)
    tiles = jnp.concatenate([tile.astype(F32), jnp.zeros((CX - 1, BRICKS), F32)], axis=0)
    tiles = jnp.concatenate([tiles[:, :CX].T, tiles[:, CX:].T], axis=0)
    meta = meta + turn(tiles, 9)
    both = dot(choose, jnp.concatenate(split(meta), axis=1))
    both = both[:, :CX] + both[:, CX:]
    for k in range(PEERS):
        packed = both[k * CAP : k * CAP + PACK]
        for i in range(1, 3):
            start = k * CAP + i * PACK
            packed = packed + turn(both[start : start + PACK], WIDE * i)
        outs[k][CELLS:, :] = packed
    copies[4].wait()
    for s in range(SLOTS):
        high, low = split(cells_ref[pl.ds(s, BRICKS, stride=SLOTS), :])
        moved = dot(choose, jnp.concatenate([high, low], axis=1))
        moved = moved[:, :CX] + moved[:, CX:]
        for k in range(PEERS):
            outs[k][s * CAP : (s + 1) * CAP, :] = moved[k * CAP : (k + 1) * CAP]


def height_of(place, level):
    if level == LEVELS:
        return place
    band = (place * 1366) >> 16
    return (place - band * BAND) * (8 >> level) + band


def rim_of(lane, level):
    j = lane & 7
    before = (lane < CX // 2) == (level == 0)
    return (lane >> 3) & 7, jnp.where(before, j - REACH, j + WIDTHS[level])


def taps_at(table, shift):
    spot = jnp.where((shift >= 0) & (shift < TAPS), shift, CX - 1)
    return jnp.take_along_axis(jnp.broadcast_to(table, spot.shape), spot, axis=1)


def prep_kernel(
    across_ref, along_ref, mix_ref, own_ref, own_low_ref, across, blend_high, blend_low,
    rim_high, rim_low, gather, table
):
    exact = lax.Precision.HIGHEST
    table[...] = jnp.zeros(table.shape, F32)
    for level in range(LEVELS + 1):
        for r in range(2):
            line = 4 * level + r
            table[line : line + 1, :TAPS] = along_ref[level, r : r + 1, :]
            table[line + 2 : line + 3, :TAPS] = across_ref[level, r : r + 1, :]
    for level in range(LEVELS + 1):
        scale = 0.25**level
        row = iota((CX, 1), 0)
        mark = row >> level
        lane_z, lane_place = rim_of(row, level)
        line_z, line_place = rim_of(iota((1, CX), 1), level)
        column = iota((CX, CX), 1) >> level
        shift = mark - column + REACH
        rim_shift = lane_place - column + REACH
        same = lane_place == line_place
        edge = jnp.where(line_place < 0, line_place + WIDTHS[level], line_place - WIDTHS[level])
        for z in range(PLANES):
            chosen = flags((mark == edge) & (line_z == z))
            gather[level * PLANES + z, :CX, :] = chosen
            gather[level * PLANES + z, CX:, :] = chosen
        pick = (lane_z == iota((CX, 8), 1)).astype(F32)
        pick_t = (line_z == iota((8, CX), 0)).astype(F32)
        masks = [
            jnp.broadcast_to((lane_z == z).astype(F32), (CX, CX)).astype(BF16)
            for z in range(PLANES)
        ]
        for r in range(2):
            part = slice(r * CX, (r + 1) * CX)
            line = table[4 * level + r : 4 * level + r + 1, :]
            high, low = split(taps_at(line, shift) * scale)
            own_ref[level, :CX, part] = high
            own_ref[level, CX:, part] = high
            own_low_ref[level, :, part] = low
            high, low = split(taps_at(line, rim_shift) * scale)
            for z in range(PLANES):
                rim_high[level, part, z * CX : (z + 1) * CX] = high * masks[z]
                rim_low[level, part, z * CX : (z + 1) * CX] = low * masks[z]
            mixes = lax.dot_general(
                pick, mix_ref[level, r], (((1,), (1,)), ((), ())), precision=exact,
                preferred_element_type=F32,
            )
            mixes = jnp.dot(mixes, pick_t, precision=exact, preferred_element_type=F32)
            high, low = split(jnp.where(same, mixes, 0.0))
            blend_high[level, :, part] = high
            blend_low[level, :, part] = low
        size, step = HEIGHTS[level], STEP[level]
        upper = slice(TAP_ROW[level], TAP_ROW[level] + size)
        lower = slice(TAP_ROW[level] + step, TAP_ROW[level] + step + size)
        mine = height_of(iota((size, 1), 0), level)
        first = table[4 * level + 2 : 4 * level + 3, :]
        both = first + turn(table[4 * level + 3 : 4 * level + 4, :], 32)
        for start in range(0, 2 * step, CX):
            lanes = min(CX, 2 * step - start)
            place = iota((1, CX), 1) + start
            second = place >= step
            place = jnp.where(second, place - step, place)
            other = jnp.where(place < size, height_of(place, level), 4 * NY)
            shift = other - mine + REACH
            spot = jnp.where(
                (shift >= 0) & (shift < TAPS), shift + jnp.where(second, 32, 0), CX - 1
            )
            taps = jnp.take_along_axis(jnp.broadcast_to(both, spot.shape), spot, axis=1)
            high, low = split(taps[:, :lanes])
            across[upper, start : start + lanes] = high
            across[lower, start : start + lanes] = low


def brick_products(ref, match, weights, bricks):
    packed = ref[CELLS:, :]
    meta = jnp.concatenate([packed, turn(packed, -WIDE), turn(packed, -2 * WIDE)], axis=0)
    cells = [ref[s * CAP : (s + 1) * CAP, :] for s in range(SLOTS)]
    totals = [None] * PLANES
    for s in range(SLOTS):
        current = meta[:, SPAN * s + 8 : SPAN * s + 9]
        for z in range(PLANES):
            piece = cells[s] * meta[:, SPAN * s + z : SPAN * s + z + 1]
            weights[s * PLANES + z] = piece
            piece = piece * current
            totals[z] = piece if s == 0 else totals[z] + piece
    blank = jnp.zeros((CX - CAP, HALF), BF16)
    bricks[CAP:CX, :] = blank
    bricks[CX + CAP :, :] = blank
    for z in range(PLANES):
        high, low = split(totals[z])
        bricks[:CAP, z * CX : (z + 1) * CX] = high
        bricks[CX : CX + CAP, z * CX : (z + 1) * CX] = low
    whole = jnp.concatenate([meta, jnp.zeros((CX - CAP, CX), F32)], axis=0)
    names = jnp.where(iota((1, CX), 1) < CAP, whole.T[9:10, :], -1.0)
    match[...] = flags(iota((CAP, TILES), 1).astype(F32) == meta[:, 9:10])
    hot = flags(iota((TILES, CX), 0).astype(F32) == names)
    return jnp.concatenate([hot, hot], axis=1)


def brick_kernel(ref, *refs):
    match, weights, total, bricks = refs[-4:]
    hot = brick_products(ref, match, weights, bricks)
    for pair in range(PLANES // 2):
        part = slice(pair * 2 * CX, (pair + 1) * 2 * CX)
        found = dot(hot, bricks[:, part])
        total[:, part] = refs[0][:, part] + found if len(refs) > 4 else found


def charge_kernel(
    ref, partial, gather, match, weights, q0, s1, s2, s3, s4, to_pair, to_next, bricks, *rims
):
    hot = brick_products(ref, match, weights, bricks)
    lanes = iota((1, CX), 1)
    for pair in range(PLANES // 2):
        part = slice(pair * 2 * CX, (pair + 1) * 2 * CX)
        found = partial[:, part] + dot(hot, bricks[:, part])
        for i in range(2):
            z = 2 * pair + i
            plane = found[:, i * CX : (i + 1) * CX]
            bands = swap_groups([plane[b * BAND : (b + 1) * BAND] for b in range(8)])
            for level in range(LEVELS):
                plain = jnp.concatenate(bands, axis=0)
                (q0, s1, s2, s3)[level][z] = plain
                found_rims = dot(
                    jnp.concatenate(split(plain), axis=1), gather[level * PLANES + z]
                )
                rims[level][...] = rims[level][...] + found_rims if z else found_rims
                bands = [bands[2 * b] + bands[2 * b + 1] for b in range(len(bands) // 2)]
    size = HEIGHTS[LEVELS]
    coarse = jnp.zeros((size, CX), F32)
    for z in range(PLANES):
        value = s3[z, pl.ds(0, size, stride=2), :] + s3[z, pl.ds(1, size, stride=2), :]
        s4[z] = value
        coarse = coarse + dot(
            jnp.concatenate(split(value), axis=1), gather[LEVELS * PLANES + z]
        )
    even = (lax.axis_index("sect") & 1) == 0
    for level in range(1, LEVELS + 2):
        if level < LEVELS:
            rows = slice(RIM_ROW[level], RIM_ROW[level] + HEIGHTS[level])
            other = rims[level][...]
        elif level == LEVELS:
            rows, other = slice(RIM_ROW[level], RIM_ROW[level] + size), coarse
        else:
            rows = slice(RIM_ROW[LEVELS] + size, NY)
            other = jnp.zeros((NY - RIM_ROW[LEVELS] - size, CX), F32)
        right = jnp.where(lanes < CX // 2, rims[0][rows, :], other)
        left = jnp.where(lanes < CX // 2, other, rims[0][rows, :])
        to_pair[rows, :] = jnp.where(even, right, left)
        to_next[rows, :] = jnp.where(even, left, right)


def inner_kernel(
    mix_ref, q0, s1, s2, s3, s4, own_ref, own_low_ref, across, out_ref, ranked, high_ref, low_ref
):
    sources = (q0, s1, s2, s3, s4)

    def along(level):
        size = HEIGHTS[level]
        for z in range(PLANES):
            high, low = split(sources[level][z])
            found = dot(jnp.concatenate([high, low], axis=1), own_ref[level])
            rows = slice(MIX_ROW[level] + z * size, MIX_ROW[level] + (z + 1) * size)
            ranked[rows, :] = found + dot(high, own_low_ref[level])

    def blend(level, r):
        size, step = HEIGHTS[level], STEP[level]
        chunk = 24 if size < 32 else (48 if size == 48 else 32)
        chunk = 16 if chunk == 48 else chunk
        for start in range(0, size, chunk):
            parts = []
            for w in range(PLANES):
                line = MIX_ROW[level] + w * size + start
                parts.append(ranked[line : line + chunk, r * CX : (r + 1) * CX])
            for z in range(PLANES):
                total = parts[0] * mix_ref[level, r, z, 0]
                for w in range(1, PLANES):
                    total = total + parts[w] * mix_ref[level, r, z, w]
                if chunk == 24:
                    total = jnp.concatenate([total, jnp.zeros((8, CX), F32)], axis=0)
                high, low = split(total)
                line = TAP_ROW[level] + r * step + start
                high_ref[line : line + high.shape[0], z * CX : (z + 1) * CX] = high
                low_ref[line : line + high.shape[0], z * CX : (z + 1) * CX] = low

    def combine(level):
        size, step = HEIGHTS[level], STEP[level]
        rows = slice(ROW_OF[level], ROW_OF[level] + size)
        lines = slice(TAP_ROW[level], TAP_ROW[level] + 2 * step)
        taps = across[lines, : 2 * step]
        for pair in range(PLANES // 2):
            part = slice(pair * 2 * CX, (pair + 1) * 2 * CX)
            found = dot(taps, high_ref[lines, part])
            found = found[:size] + found[step : step + size]
            out_ref[rows, part] = found + dot(taps[:step], low_ref[lines, part])[:size]

    along(0)
    blend(0, 0)
    blend(0, 1)
    for level in range(1, LEVELS + 1):
        along(level)
    combine(0)
    for level in range(1, LEVELS + 1):
        blend(level, 0)
        blend(level, 1)
    for level in range(1, LEVELS + 1):
        combine(level)


def outer_kernel(*refs):
    inner, by_pair, by_next, across = refs[:4]
    blend_high, blend_low, rim_high, rim_low = refs[4:8]
    matches, weights = refs[8 : 8 + PEERS], refs[8 + PEERS : 8 + 2 * PEERS]
    grid_ref = refs[8 + 2 * PEERS]
    outs = refs[9 + 2 * PEERS : 9 + 3 * PEERS]
    high_ref, low_ref, tiles, picked, doubled = refs[9 + 3 * PEERS :]
    lanes = iota((1, CX), 1)
    even = (lax.axis_index("sect") & 1) == 0
    high_ref[...] = jnp.zeros((ALL_K, 2 * CX), BF16)
    low_ref[...] = jnp.zeros((ALL_K, 2 * CX), BF16)
    sums = []
    for level in range(LEVELS + 1):
        size, step = HEIGHTS[level], STEP[level]
        rows = slice(RIM_ROW[level], RIM_ROW[level] + size)
        from_left = jnp.where(even, by_next[rows, :], by_pair[rows, :])
        from_right = jnp.where(even, by_pair[rows, :], by_next[rows, :])
        if level == 0:
            rims = jnp.where(lanes < CX // 2, from_left, from_right)
        else:
            rims = jnp.where(lanes < CX // 2, from_right, from_left)
        high, low = split(rims)
        mixed = dot(high, blend_high[level]) + dot(low, blend_high[level])
        mixed = mixed + dot(high, blend_low[level])
        if size < step:
            mixed = jnp.concatenate([mixed, jnp.zeros((step - size, 2 * CX), F32)], axis=0)
        high, low = split(mixed)
        for r in range(2):
            part = slice(r * CX, (r + 1) * CX)
            place = slice(K_OF[level] + r * step, K_OF[level] + (r + 1) * step)
            high_ref[place, part] = high[:, part]
            low_ref[place, part] = low[:, part]
        place = slice(K_OF[level], K_OF[level] + 2 * step)
        taps = across[TAP_ROW[level] : TAP_ROW[level] + 2 * step, : 2 * step]
        found = dot(taps, high_ref[place, :])
        found = found[:step] + found[step:] + dot(taps[:step], low_ref[place, :])
        sums.append(jnp.concatenate(split(found), axis=0))
    for pair in range(PLANES // 2):
        part = slice(pair * 2 * CX, (pair + 1) * 2 * CX)
        above = None
        for level in range(LEVELS, -1, -1):
            size, step = HEIGHTS[level], STEP[level]
            value = dot(sums[level], rim_high[level, :, part])
            value = value[:size] + value[step : step + size]
            value = value + dot(sums[level][:step], rim_low[level, :, part])[:size]
            value = value + inner[ROW_OF[level] : ROW_OF[level] + HEIGHTS[level], part]
            if level == LEVELS:
                doubled[pl.ds(0, HEIGHTS[level], stride=2), :] = value[:, :CX]
                doubled[pl.ds(1, HEIGHTS[level], stride=2), :] = value[:, :CX]
                doubled[pl.ds(BAND, HEIGHTS[level], stride=2), :] = value[:, CX:]
                doubled[pl.ds(BAND + 1, HEIGHTS[level], stride=2), :] = value[:, CX:]
                above = [jnp.concatenate([doubled[:BAND, :], doubled[BAND:, :]], axis=1)]
                continue
            bands = 8 >> level
            fresh = []
            for b in range(bands):
                fresh.append(value[b * BAND : (b + 1) * BAND] + above[b * len(above) // bands])
            above = fresh
        for i in range(2):
            z = 2 * pair + i
            planes = [band[:, i * CX : (i + 1) * CX] for band in above]
            for b in range(8):
                grid_ref[z, pl.ds(b, BAND, stride=8), :] = planes[b]
            for b, band in enumerate(swap_groups(planes)):
                high, low = split(band)
                rows = slice(b * BAND, (b + 1) * BAND)
                tiles[rows, z * CX : (z + 1) * CX] = high
                rows = slice(TILES + b * BAND, TILES + (b + 1) * BAND)
                tiles[rows, z * CX : (z + 1) * CX] = low
    match = jnp.concatenate([ref[...] for ref in matches], axis=0)
    match = jnp.concatenate([match, match], axis=1)
    for pair in range(PLANES // 2):
        part = slice(pair * 2 * CX, (pair + 1) * 2 * CX)
        picked[:, part] = dot(match, tiles[:, part])
    for j in range(PEERS):
        mine = slice(j * CAP, (j + 1) * CAP)
        values = jnp.zeros((CAP, CX), F32)
        for s in range(SLOTS):
            total = picked[mine, :CX] * weights[j][s * PLANES]
            for z in range(1, PLANES):
                total = total + picked[mine, z * CX : (z + 1) * CX] * weights[j][s * PLANES + z]
            values = jnp.where(lanes == s, jnp.sum(total, axis=1, keepdims=True), values)
        values = jnp.concatenate([values, jnp.zeros((CX - CAP, CX), F32)], axis=0)
        outs[j][...] = values.T[:8, :]


def spread_kernel(slot_ref, match_ref):
    slot = slot_ref[0:1, :]
    away = jnp.floor((slot + 0.5) * (1.0 / CAP))
    pieces = jnp.concatenate(
        [away, slot - away * CAP, jnp.zeros((14, BRICKS), F32)], axis=0
    )
    spread = flags(iota((BRICKS, SEGS), 1) // SLOTS == iota((BRICKS, SEGS), 0))
    pieces = dot(pieces.astype(BF16), spread)
    place = pieces[0:1] * CX + pieces[1:2]
    match_ref[...] = flags(iota((PEERS * CX, SEGS), 0).astype(F32) == place)


def pick_kernel(count_ref, match_ref, b0, b1, b2, b3, out_ref):
    held = jnp.concatenate([b0[...], b1[...], b2[...], b3[...]], axis=1)
    value = dot(jnp.concatenate(split(held), axis=0), match_ref[...])
    value = value[:8] + value[8:]
    lane = iota((8, SEGS), 1)
    mine = (lane % SLOTS == iota((8, SEGS), 0)) & (lane // SLOTS < count_ref[0])
    out_ref[...] = jnp.sum(jnp.where(mine, value, 0.0), axis=0, keepdims=True)


VMEM = pl.BlockSpec(memory_space=pltpu.VMEM)
SMEM = pl.BlockSpec(memory_space=pltpu.SMEM)
ANY = pl.BlockSpec(memory_space=pl.ANY)
HBM = pl.BlockSpec(memory_space=pltpu.HBM)


def shape(*dims, kind=F32):
    return jax.ShapeDtypeStruct(dims, kind)


def call(kernel, inputs, outputs, scratch=(), megabytes=16):
    return pl.pallas_call(
        kernel,
        in_specs=list(inputs),
        out_specs=[VMEM] * len(outputs),
        out_shape=list(outputs),
        scratch_shapes=list(scratch),
        compiler_params=pltpu.CompilerParams(vmem_limit_bytes=int(megabytes * (1 << 20))),
    )


def body(
    currents, plane_weights, cell_weights, brick_dest, brick_tile, brick_count, kern_across,
    kern_along, plane_mix,
):
    *sends, slots = call(
        route_kernel,
        [SMEM] + [HBM] * 5,
        [shape(ROWS, CX)] * PEERS + [shape(8, BRICKS)],
        [
            pltpu.VMEM((SEGS, CX), F32),
            pltpu.VMEM((1, SEGS), F32),
            pltpu.VMEM((PLANES, SEGS), F32),
            pltpu.VMEM((SEGS, CX), F32),
            pltpu.VMEM((1, BRICKS), jnp.int32),
            pltpu.VMEM((1, BRICKS), jnp.int32),
            pltpu.SemaphoreType.DMA((5,)),
        ],
        megabytes=63,
    )(
        brick_count,
        currents.reshape(1, SEGS),
        plane_weights,
        cell_weights,
        brick_dest.reshape(1, BRICKS),
        brick_tile.reshape(1, BRICKS),
    )
    swaps = [[(i, i ^ k) for i in range(PEERS)] for k in range(PEERS)]
    held = [sends[0]] + [lax.ppermute(sends[k], "sect", swaps[k]) for k in range(1, PEERS)]
    prepared = call(
        prep_kernel,
        [VMEM, VMEM, VMEM],
        [
            shape(LEVELS + 1, 2 * CX, 2 * CX, kind=BF16),
            shape(LEVELS + 1, CX, 2 * CX, kind=BF16),
            shape(ALL_K, 2 * NY, kind=BF16),
            shape(LEVELS + 1, CX, 2 * CX, kind=BF16),
            shape(LEVELS + 1, CX, 2 * CX, kind=BF16),
            shape(LEVELS + 1, 2 * CX, HALF, kind=BF16),
            shape(LEVELS + 1, 2 * CX, HALF, kind=BF16),
            shape((LEVELS + 1) * PLANES, 2 * CX, CX, kind=BF16),
        ],
        [pltpu.VMEM((24, CX), F32)],
    )(kern_across, kern_along, plane_mix)
    own, own_low, across, *outer, gather = prepared
    kept = [shape(CAP, TILES, kind=BF16), shape(SLOTS * PLANES, CAP, CX)]
    products = pltpu.VMEM((2 * CX, HALF), BF16)
    matches, weights, total = [], [], []
    for value in held[:-1]:
        match, weight, partial = call(
            brick_kernel,
            [VMEM] * (1 + len(total)),
            kept + [shape(TILES, HALF)],
            [products],
        )(value, *total)
        matches.append(match)
        weights.append(weight)
        total = [partial]
    match, weight, *fields, to_pair, to_next = call(
        charge_kernel,
        [VMEM] * 3,
        kept + [shape(PLANES, size, CX) for size in HEIGHTS] + [shape(NY, CX)] * 2,
        [products] + [pltpu.VMEM((size, CX), F32) for size in HEIGHTS[:LEVELS]],
    )(held[-1], *total, gather)
    matches.append(match)
    weights.append(weight)
    axes = ("strip", "sect")
    devices = lax.axis_size(axes)
    paired = [(i, i ^ 1) for i in range(devices)]
    crossed = [(i, ((i + 1) ^ 1) - 1) for i in range(1, devices - 1)]
    by_pair = lax.ppermute(to_pair, axes, paired)
    by_next = lax.ppermute(to_next, axes, crossed)
    (inner,) = call(
        inner_kernel,
        [SMEM] + [VMEM] * 8,
        [shape(ALL_ROWS, HALF)],
        [
            pltpu.VMEM((MIX_ROWS, 2 * CX), F32),
            pltpu.VMEM((ALL_K, HALF), BF16),
            pltpu.VMEM((ALL_K, HALF), BF16),
        ],
        megabytes=24,
    )(plane_mix, *fields, own, own_low, across)
    grid, *samples = call(
        outer_kernel,
        [VMEM] * (8 + 2 * PEERS),
        [shape(PLANES, NY, CX)] + [shape(8, CX)] * PEERS,
        [
            pltpu.VMEM((ALL_K, 2 * CX), BF16),
            pltpu.VMEM((ALL_K, 2 * CX), BF16),
            pltpu.VMEM((2 * TILES, HALF), BF16),
            pltpu.VMEM((PEERS * CAP, HALF), F32),
            pltpu.VMEM((2 * BAND, CX), F32),
        ],
    )(inner, by_pair, by_next, across, *outer, *matches, *weights)
    back = [samples[0]] + [lax.ppermute(samples[k], "sect", swaps[k]) for k in range(1, PEERS)]
    (match,) = call(spread_kernel, [VMEM], [shape(PEERS * CX, SEGS, kind=BF16)])(slots)
    (segments,) = call(
        pick_kernel, [SMEM] + [VMEM] * 5, [shape(1, SEGS)]
    )(brick_count, match, *back)
    return grid, segments.reshape(SEGS)


def solution(mesh):
    flat = ("strip", "sect")
    placed = (
        P(flat), P(None, flat), P(flat, None), P(flat, None), P(flat), P(flat), P(), P(), P(),
    )
    return jax.shard_map(
        body,
        mesh=mesh,
        in_specs=placed,
        out_specs=(P(None, None, flat), P(flat)),
        check_vma=False,
    )
```

```python
import jax
import jax.numpy as jnp
from jax import lax
from jax.experimental import pallas as pl
from jax.experimental.pallas import tpu as pltpu
from jax.sharding import PartitionSpec as P

NY = 384
CX = 128
LEVELS = 4
TILES = 384
PLANES = 8
TAPS = 17
REACH = TAPS // 2
SLOTS = 4
BRICKS = 256
CAP = 96
PEERS = 4
CELLS = SLOTS * CAP
PACK = CAP // 3
SPAN = 10
WIDE = SPAN * SLOTS
ROWS = CELLS + PACK
SEGS = BRICKS * SLOTS
BAND = NY // 8
HALF = PLANES * CX
HEIGHTS = tuple(NY >> level for level in range(LEVELS + 1))
WIDTHS = tuple(CX >> level for level in range(LEVELS + 1))
STEP = (384, 192, 96, 48, 32)
ROW_OF = (0, 384, 576, 672, 720)
ALL_ROWS = 752
TAP_ROW = (0, 768, 1152, 1344, 1440)
K_OF = (0, 768, 1152, 1344, 1440)
ALL_K = 1504
RIM_ROW = (0, 0, 192, 288, 336)
MIX_ROW = tuple(PLANES * sum(HEIGHTS[:level]) for level in range(LEVELS + 1))
MIX_ROWS = PLANES * sum(HEIGHTS)
F32 = jnp.float32
BF16 = jnp.bfloat16


def split(value):
    high = value.astype(BF16)
    return high, (value - high.astype(F32)).astype(BF16)


def dot(left, right):
    return jnp.dot(left, right, preferred_element_type=F32)


def iota(shape, dim):
    return lax.broadcasted_iota(jnp.int32, shape, dim)


def flags(condition):
    return condition.astype(F32).astype(BF16)


def turn(value, amount):
    amount = amount % CX
    return pltpu.roll(value, amount, 1) if amount else value


def swap_groups(bands):
    group = iota((1, CX), 1) // 16
    bands = [turn(band, 16 * i) for i, band in enumerate(bands)]
    for bit in range(3):
        upper = ((group >> bit) & 1) == 1
        bands = [jnp.where(upper, bands[(i + (1 << bit)) % 8], bands[i]) for i in range(8)]
    return [turn(bands[-i % 8], -16 * i) for i in range(8)]


def route_kernel(
    count_ref, currents_hbm, planes_hbm, cells_hbm, dest_hbm, tile_hbm, *refs
):
    outs, slot_ref = refs[:PEERS], refs[PEERS]
    feature, currents_ref, planes_ref, cells_ref, dest_ref, tile_ref, sems = refs[PEERS + 1 :]
    pairs = (
        (dest_hbm, dest_ref), (tile_hbm, tile_ref), (currents_hbm, currents_ref),
        (planes_hbm, planes_ref), (cells_hbm, cells_ref),
    )
    copies = [pltpu.make_async_copy(a, b, sems.at[i]) for i, (a, b) in enumerate(pairs)]
    for copy in copies:
        copy.start()
    for copy in copies[:4]:
        copy.wait()
    me = lax.axis_index("sect")
    away = dest_ref[...] ^ me
    onehot = (iota((16, BRICKS), 0) == away).astype(F32)
    before = flags(iota((BRICKS, BRICKS), 0) < iota((BRICKS, BRICKS), 1))
    earlier = dot(onehot.astype(BF16), before)
    base = (iota((16, BRICKS), 0) * CAP).astype(F32)
    slot = jnp.sum(onehot * (earlier + base), axis=0, keepdims=True)
    slot_ref[...] = jnp.broadcast_to(slot, slot_ref.shape)
    choose = flags(iota((PEERS * CAP, BRICKS), 0).astype(F32) == slot)
    alive = (iota((1, SEGS), 1) // SLOTS < count_ref[0]).astype(F32)
    currents = currents_ref[...] * alive
    lines = jnp.concatenate(
        [planes_ref[...], currents, jnp.zeros((CX - PLANES - 1, SEGS), F32)], axis=0
    )
    for part in range(SEGS // CX):
        feature[part * CX : (part + 1) * CX, :] = lines[:, part * CX : (part + 1) * CX].T
    meta = jnp.zeros((BRICKS, CX), F32)
    for s in range(SLOTS):
        meta = meta + turn(feature[pl.ds(s, BRICKS, stride=SLOTS), :], SPAN * s)
    tile = tile_ref[...]
    tile = (tile & 7) * BAND + (tile >> 3)
    tiles = jnp.concatenate([tile.astype(F32), jnp.zeros((CX - 1, BRICKS), F32)], axis=0)
    tiles = jnp.concatenate([tiles[:, :CX].T, tiles[:, CX:].T], axis=0)
    meta = meta + turn(tiles, 9)
    both = dot(choose, jnp.concatenate(split(meta), axis=1))
    both = both[:, :CX] + both[:, CX:]
    for k in range(PEERS):
        packed = both[k * CAP : k * CAP + PACK]
        for i in range(1, 3):
            start = k * CAP + i * PACK
            packed = packed + turn(both[start : start + PACK], WIDE * i)
        outs[k][CELLS:, :] = packed
    copies[4].wait()
    for s in range(SLOTS):
        high, low = split(cells_ref[pl.ds(s, BRICKS, stride=SLOTS), :])
        moved = dot(choose, jnp.concatenate([high, low], axis=1))
        moved = moved[:, :CX] + moved[:, CX:]
        for k in range(PEERS):
            outs[k][s * CAP : (s + 1) * CAP, :] = moved[k * CAP : (k + 1) * CAP]


def height_of(place, level):
    if level == LEVELS:
        return place
    band = (place * 1366) >> 16
    return (place - band * BAND) * (8 >> level) + band


def rim_of(lane, level):
    j = lane & 7
    before = (lane < CX // 2) == (level == 0)
    return (lane >> 3) & 7, jnp.where(before, j - REACH, j + WIDTHS[level])


def taps_at(table, shift):
    spot = jnp.where((shift >= 0) & (shift < TAPS), shift, CX - 1)
    return jnp.take_along_axis(jnp.broadcast_to(table, spot.shape), spot, axis=1)


def prep_kernel(
    across_ref, along_ref, mix_ref, own_ref, own_low_ref, across, blend_high, blend_low,
    rim_high, rim_low, gather, table
):
    exact = lax.Precision.HIGHEST
    table[...] = jnp.zeros(table.shape, F32)
    for level in range(LEVELS + 1):
        for r in range(2):
            line = 4 * level + r
            table[line : line + 1, :TAPS] = along_ref[level, r : r + 1, :]
            table[line + 2 : line + 3, :TAPS] = across_ref[level, r : r + 1, :]
    for level in range(LEVELS + 1):
        scale = 0.25**level
        row = iota((CX, 1), 0)
        mark = row >> level
        lane_z, lane_place = rim_of(row, level)
        line_z, line_place = rim_of(iota((1, CX), 1), level)
        column = iota((CX, CX), 1) >> level
        shift = mark - column + REACH
        rim_shift = lane_place - column + REACH
        same = lane_place == line_place
        edge = jnp.where(line_place < 0, line_place + WIDTHS[level], line_place - WIDTHS[level])
        for z in range(PLANES):
            chosen = flags((mark == edge) & (line_z == z))
            gather[level * PLANES + z, :CX, :] = chosen
            gather[level * PLANES + z, CX:, :] = chosen
        pick = (lane_z == iota((CX, 8), 1)).astype(F32)
        pick_t = (line_z == iota((8, CX), 0)).astype(F32)
        masks = [
            jnp.broadcast_to((lane_z == z).astype(F32), (CX, CX)).astype(BF16)
            for z in range(PLANES)
        ]
        for r in range(2):
            part = slice(r * CX, (r + 1) * CX)
            line = table[4 * level + r : 4 * level + r + 1, :]
            high, low = split(taps_at(line, shift) * scale)
            own_ref[level, :CX, part] = high
            own_ref[level, CX:, part] = high
            own_low_ref[level, :, part] = low
            high, low = split(taps_at(line, rim_shift) * scale)
            for z in range(PLANES):
                rim_high[level, part, z * CX : (z + 1) * CX] = high * masks[z]
                rim_low[level, part, z * CX : (z + 1) * CX] = low * masks[z]
            mixes = lax.dot_general(
                pick, mix_ref[level, r], (((1,), (1,)), ((), ())), precision=exact,
                preferred_element_type=F32,
            )
            mixes = jnp.dot(mixes, pick_t, precision=exact, preferred_element_type=F32)
            high, low = split(jnp.where(same, mixes, 0.0))
            blend_high[level, :, part] = high
            blend_low[level, :, part] = low
        size, step = HEIGHTS[level], STEP[level]
        upper = slice(TAP_ROW[level], TAP_ROW[level] + size)
        lower = slice(TAP_ROW[level] + step, TAP_ROW[level] + step + size)
        mine = height_of(iota((size, 1), 0), level)
        first = table[4 * level + 2 : 4 * level + 3, :]
        both = first + turn(table[4 * level + 3 : 4 * level + 4, :], 32)
        for start in range(0, 2 * step, CX):
            lanes = min(CX, 2 * step - start)
            place = iota((1, CX), 1) + start
            second = place >= step
            place = jnp.where(second, place - step, place)
            other = jnp.where(place < size, height_of(place, level), 4 * NY)
            shift = other - mine + REACH
            spot = jnp.where(
                (shift >= 0) & (shift < TAPS), shift + jnp.where(second, 32, 0), CX - 1
            )
            taps = jnp.take_along_axis(jnp.broadcast_to(both, spot.shape), spot, axis=1)
            high, low = split(taps[:, :lanes])
            across[upper, start : start + lanes] = high
            across[lower, start : start + lanes] = low


def brick_products(ref, match, weights, bricks):
    packed = ref[CELLS:, :]
    meta = jnp.concatenate([packed, turn(packed, -WIDE), turn(packed, -2 * WIDE)], axis=0)
    cells = [ref[s * CAP : (s + 1) * CAP, :] for s in range(SLOTS)]
    totals = [None] * PLANES
    for s in range(SLOTS):
        current = meta[:, SPAN * s + 8 : SPAN * s + 9]
        for z in range(PLANES):
            piece = cells[s] * meta[:, SPAN * s + z : SPAN * s + z + 1]
            weights[s * PLANES + z] = piece
            piece = piece * current
            totals[z] = piece if s == 0 else totals[z] + piece
    blank = jnp.zeros((CX - CAP, HALF), BF16)
    bricks[CAP:CX, :] = blank
    bricks[CX + CAP :, :] = blank
    for z in range(PLANES):
        high, low = split(totals[z])
        bricks[:CAP, z * CX : (z + 1) * CX] = high
        bricks[CX : CX + CAP, z * CX : (z + 1) * CX] = low
    whole = jnp.concatenate([meta, jnp.zeros((CX - CAP, CX), F32)], axis=0)
    names = jnp.where(iota((1, CX), 1) < CAP, whole.T[9:10, :], -1.0)
    match[...] = flags(iota((CAP, TILES), 1).astype(F32) == meta[:, 9:10])
    hot = flags(iota((TILES, CX), 0).astype(F32) == names)
    return jnp.concatenate([hot, hot], axis=1)


def brick_kernel(ref, *refs):
    match, weights, total, bricks = refs[-4:]
    hot = brick_products(ref, match, weights, bricks)
    for pair in range(PLANES // 2):
        part = slice(pair * 2 * CX, (pair + 1) * 2 * CX)
        found = dot(hot, bricks[:, part])
        total[:, part] = refs[0][:, part] + found if len(refs) > 4 else found


def charge_kernel(
    ref, partial, gather, match, weights, q0, s1, s2, s3, s4, to_pair, to_next, bricks, *rims
):
    hot = brick_products(ref, match, weights, bricks)
    lanes = iota((1, CX), 1)
    for pair in range(PLANES // 2):
        part = slice(pair * 2 * CX, (pair + 1) * 2 * CX)
        found = partial[:, part] + dot(hot, bricks[:, part])
        for i in range(2):
            z = 2 * pair + i
            plane = found[:, i * CX : (i + 1) * CX]
            bands = swap_groups([plane[b * BAND : (b + 1) * BAND] for b in range(8)])
            for level in range(LEVELS):
                plain = jnp.concatenate(bands, axis=0)
                (q0, s1, s2, s3)[level][z] = plain
                found_rims = dot(
                    jnp.concatenate(split(plain), axis=1), gather[level * PLANES + z]
                )
                rims[level][...] = rims[level][...] + found_rims if z else found_rims
                bands = [bands[2 * b] + bands[2 * b + 1] for b in range(len(bands) // 2)]
    size = HEIGHTS[LEVELS]
    coarse = jnp.zeros((size, CX), F32)
    for z in range(PLANES):
        value = s3[z, pl.ds(0, size, stride=2), :] + s3[z, pl.ds(1, size, stride=2), :]
        s4[z] = value
        coarse = coarse + dot(
            jnp.concatenate(split(value), axis=1), gather[LEVELS * PLANES + z]
        )
    even = (lax.axis_index("sect") & 1) == 0
    for level in range(1, LEVELS + 2):
        if level < LEVELS:
            rows = slice(RIM_ROW[level], RIM_ROW[level] + HEIGHTS[level])
            other = rims[level][...]
        elif level == LEVELS:
            rows, other = slice(RIM_ROW[level], RIM_ROW[level] + size), coarse
        else:
            rows = slice(RIM_ROW[LEVELS] + size, NY)
            other = jnp.zeros((NY - RIM_ROW[LEVELS] - size, CX), F32)
        right = jnp.where(lanes < CX // 2, rims[0][rows, :], other)
        left = jnp.where(lanes < CX // 2, other, rims[0][rows, :])
        to_pair[rows, :] = jnp.where(even, right, left)
        to_next[rows, :] = jnp.where(even, left, right)


def inner_kernel(
    mix_ref, q0, s1, s2, s3, s4, own_ref, own_low_ref, across, out_ref, ranked, high_ref, low_ref
):
    sources = (q0, s1, s2, s3, s4)

    def along(level):
        size = HEIGHTS[level]
        for z in range(PLANES):
            high, low = split(sources[level][z])
            found = dot(jnp.concatenate([high, low], axis=1), own_ref[level])
            rows = slice(MIX_ROW[level] + z * size, MIX_ROW[level] + (z + 1) * size)
            ranked[rows, :] = found + dot(high, own_low_ref[level])

    def blend(level, r):
        size, step = HEIGHTS[level], STEP[level]
        chunk = 24 if size < 32 else (48 if size == 48 else 32)
        chunk = 16 if chunk == 48 else chunk
        for start in range(0, size, chunk):
            parts = []
            for w in range(PLANES):
                line = MIX_ROW[level] + w * size + start
                parts.append(ranked[line : line + chunk, r * CX : (r + 1) * CX])
            for z in range(PLANES):
                terms = [parts[w] * mix_ref[level, r, z, w] for w in range(PLANES)]
                while len(terms) > 1:
                    terms = [terms[i] + terms[i + 1] for i in range(0, len(terms), 2)]
                total = terms[0]
                if chunk == 24:
                    total = jnp.concatenate([total, jnp.zeros((8, CX), F32)], axis=0)
                high, low = split(total)
                line = TAP_ROW[level] + r * step + start
                high_ref[line : line + high.shape[0], z * CX : (z + 1) * CX] = high
                low_ref[line : line + high.shape[0], z * CX : (z + 1) * CX] = low

    def combine(level):
        size, step = HEIGHTS[level], STEP[level]
        rows = slice(ROW_OF[level], ROW_OF[level] + size)
        lines = slice(TAP_ROW[level], TAP_ROW[level] + 2 * step)
        taps = across[lines, : 2 * step]
        for pair in range(PLANES // 2):
            part = slice(pair * 2 * CX, (pair + 1) * 2 * CX)
            high = high_ref[lines, part]
            stack = jnp.concatenate([high, low_ref[lines, part]], axis=0)
            double = jnp.concatenate([taps[:step], taps[:step]], axis=1)
            found = dot(double, stack) + dot(taps[step:], high)
            out_ref[rows, part] = found[:size]

    for level in range(LEVELS + 1):
        along(level)
    for level in range(LEVELS + 1):
        blend(level, 0)
        blend(level, 1)
    for level in range(LEVELS + 1):
        combine(level)


def outer_kernel(*refs):
    inner, by_pair, by_next, across = refs[:4]
    blend_high, blend_low, rim_high, rim_low = refs[4:8]
    matches, weights = refs[8 : 8 + PEERS], refs[8 + PEERS : 8 + 2 * PEERS]
    grid_ref = refs[8 + 2 * PEERS]
    outs = refs[9 + 2 * PEERS : 9 + 3 * PEERS]
    high_ref, low_ref, tiles, picked, doubled = refs[9 + 3 * PEERS :]
    lanes = iota((1, CX), 1)
    even = (lax.axis_index("sect") & 1) == 0
    high_ref[...] = jnp.zeros((ALL_K, 2 * CX), BF16)
    low_ref[...] = jnp.zeros((ALL_K, 2 * CX), BF16)
    sums = []
    for level in range(LEVELS + 1):
        size, step = HEIGHTS[level], STEP[level]
        rows = slice(RIM_ROW[level], RIM_ROW[level] + size)
        from_left = jnp.where(even, by_next[rows, :], by_pair[rows, :])
        from_right = jnp.where(even, by_pair[rows, :], by_next[rows, :])
        if level == 0:
            rims = jnp.where(lanes < CX // 2, from_left, from_right)
        else:
            rims = jnp.where(lanes < CX // 2, from_right, from_left)
        high, low = split(rims)
        mixed = dot(high, blend_high[level]) + dot(low, blend_high[level])
        mixed = mixed + dot(high, blend_low[level])
        if size < step:
            mixed = jnp.concatenate([mixed, jnp.zeros((step - size, 2 * CX), F32)], axis=0)
        high, low = split(mixed)
        for r in range(2):
            part = slice(r * CX, (r + 1) * CX)
            place = slice(K_OF[level] + r * step, K_OF[level] + (r + 1) * step)
            high_ref[place, part] = high[:, part]
            low_ref[place, part] = low[:, part]
    for level in range(LEVELS + 1):
        size, step = HEIGHTS[level], STEP[level]
        place = slice(K_OF[level], K_OF[level] + 2 * step)
        taps = across[TAP_ROW[level] : TAP_ROW[level] + 2 * step, : 2 * step]
        found = dot(taps, high_ref[place, :])
        found = found[:step] + found[step:] + dot(taps[:step], low_ref[place, :])
        sums.append(jnp.concatenate(split(found), axis=0))
    for pair in range(PLANES // 2):
        part = slice(pair * 2 * CX, (pair + 1) * 2 * CX)
        above = None
        for level in range(LEVELS, -1, -1):
            size, step = HEIGHTS[level], STEP[level]
            value = dot(sums[level], rim_high[level, :, part])
            value = value[:size] + value[step : step + size]
            value = value + dot(sums[level][:step], rim_low[level, :, part])[:size]
            value = value + inner[ROW_OF[level] : ROW_OF[level] + HEIGHTS[level], part]
            if level == LEVELS:
                doubled[pl.ds(0, HEIGHTS[level], stride=2), :] = value[:, :CX]
                doubled[pl.ds(1, HEIGHTS[level], stride=2), :] = value[:, :CX]
                doubled[pl.ds(BAND, HEIGHTS[level], stride=2), :] = value[:, CX:]
                doubled[pl.ds(BAND + 1, HEIGHTS[level], stride=2), :] = value[:, CX:]
                above = [jnp.concatenate([doubled[:BAND, :], doubled[BAND:, :]], axis=1)]
                continue
            bands = 8 >> level
            fresh = []
            for b in range(bands):
                fresh.append(value[b * BAND : (b + 1) * BAND] + above[b * len(above) // bands])
            above = fresh
        for i in range(2):
            z = 2 * pair + i
            planes = [band[:, i * CX : (i + 1) * CX] for band in above]
            for b in range(8):
                grid_ref[z, pl.ds(b, BAND, stride=8), :] = planes[b]
            for b, band in enumerate(swap_groups(planes)):
                high, low = split(band)
                rows = slice(b * BAND, (b + 1) * BAND)
                tiles[rows, z * CX : (z + 1) * CX] = high
                rows = slice(TILES + b * BAND, TILES + (b + 1) * BAND)
                tiles[rows, z * CX : (z + 1) * CX] = low
    match = jnp.concatenate([ref[...] for ref in matches], axis=0)
    match = jnp.concatenate([match, match], axis=1)
    for pair in range(PLANES // 2):
        part = slice(pair * 2 * CX, (pair + 1) * 2 * CX)
        picked[:, part] = dot(match, tiles[:, part])
    for j in range(PEERS):
        mine = slice(j * CAP, (j + 1) * CAP)
        values = jnp.zeros((CAP, CX), F32)
        for s in range(SLOTS):
            total = picked[mine, :CX] * weights[j][s * PLANES]
            for z in range(1, PLANES):
                total = total + picked[mine, z * CX : (z + 1) * CX] * weights[j][s * PLANES + z]
            values = jnp.where(lanes == s, jnp.sum(total, axis=1, keepdims=True), values)
        values = jnp.concatenate([values, jnp.zeros((CX - CAP, CX), F32)], axis=0)
        outs[j][...] = values.T[:8, :]


def spread_kernel(slot_ref, match_ref):
    slot = slot_ref[0:1, :]
    away = jnp.floor((slot + 0.5) * (1.0 / CAP))
    pieces = jnp.concatenate(
        [away, slot - away * CAP, jnp.zeros((14, BRICKS), F32)], axis=0
    )
    spread = flags(iota((BRICKS, SEGS), 1) // SLOTS == iota((BRICKS, SEGS), 0))
    pieces = dot(pieces.astype(BF16), spread)
    place = pieces[0:1] * CX + pieces[1:2]
    match_ref[...] = flags(iota((PEERS * CX, SEGS), 0).astype(F32) == place)


def pick_kernel(count_ref, match_ref, b0, b1, b2, b3, out_ref):
    held = jnp.concatenate([b0[...], b1[...], b2[...], b3[...]], axis=1)
    value = dot(jnp.concatenate(split(held), axis=0), match_ref[...])
    value = value[:8] + value[8:]
    lane = iota((8, SEGS), 1)
    mine = (lane % SLOTS == iota((8, SEGS), 0)) & (lane // SLOTS < count_ref[0])
    out_ref[...] = jnp.sum(jnp.where(mine, value, 0.0), axis=0, keepdims=True)


VMEM = pl.BlockSpec(memory_space=pltpu.VMEM)
SMEM = pl.BlockSpec(memory_space=pltpu.SMEM)
ANY = pl.BlockSpec(memory_space=pl.ANY)
HBM = pl.BlockSpec(memory_space=pltpu.HBM)


def shape(*dims, kind=F32):
    return jax.ShapeDtypeStruct(dims, kind)


def call(kernel, inputs, outputs, scratch=(), megabytes=16):
    return pl.pallas_call(
        kernel,
        in_specs=list(inputs),
        out_specs=[VMEM] * len(outputs),
        out_shape=list(outputs),
        scratch_shapes=list(scratch),
        compiler_params=pltpu.CompilerParams(vmem_limit_bytes=int(megabytes * (1 << 20))),
    )


def body(
    currents, plane_weights, cell_weights, brick_dest, brick_tile, brick_count, kern_across,
    kern_along, plane_mix,
):
    *sends, slots = call(
        route_kernel,
        [SMEM] + [HBM] * 5,
        [shape(ROWS, CX)] * PEERS + [shape(8, BRICKS)],
        [
            pltpu.VMEM((SEGS, CX), F32),
            pltpu.VMEM((1, SEGS), F32),
            pltpu.VMEM((PLANES, SEGS), F32),
            pltpu.VMEM((SEGS, CX), F32),
            pltpu.VMEM((1, BRICKS), jnp.int32),
            pltpu.VMEM((1, BRICKS), jnp.int32),
            pltpu.SemaphoreType.DMA((5,)),
        ],
        megabytes=63,
    )(
        brick_count,
        currents.reshape(1, SEGS),
        plane_weights,
        cell_weights,
        brick_dest.reshape(1, BRICKS),
        brick_tile.reshape(1, BRICKS),
    )
    swaps = [[(i, i ^ k) for i in range(PEERS)] for k in range(PEERS)]
    held = [sends[0]] + [lax.ppermute(sends[k], "sect", swaps[k]) for k in range(1, PEERS)]
    prepared = call(
        prep_kernel,
        [VMEM, VMEM, VMEM],
        [
            shape(LEVELS + 1, 2 * CX, 2 * CX, kind=BF16),
            shape(LEVELS + 1, CX, 2 * CX, kind=BF16),
            shape(ALL_K, 2 * NY, kind=BF16),
            shape(LEVELS + 1, CX, 2 * CX, kind=BF16),
            shape(LEVELS + 1, CX, 2 * CX, kind=BF16),
            shape(LEVELS + 1, 2 * CX, HALF, kind=BF16),
            shape(LEVELS + 1, 2 * CX, HALF, kind=BF16),
            shape((LEVELS + 1) * PLANES, 2 * CX, CX, kind=BF16),
        ],
        [pltpu.VMEM((24, CX), F32)],
    )(kern_across, kern_along, plane_mix)
    own, own_low, across, *outer, gather = prepared
    kept = [shape(CAP, TILES, kind=BF16), shape(SLOTS * PLANES, CAP, CX)]
    products = pltpu.VMEM((2 * CX, HALF), BF16)
    matches, weights, total = [], [], []
    for value in held[:-1]:
        match, weight, partial = call(
            brick_kernel,
            [VMEM] * (1 + len(total)),
            kept + [shape(TILES, HALF)],
            [products],
        )(value, *total)
        matches.append(match)
        weights.append(weight)
        total = [partial]
    match, weight, *fields, to_pair, to_next = call(
        charge_kernel,
        [VMEM] * 3,
        kept + [shape(PLANES, size, CX) for size in HEIGHTS] + [shape(NY, CX)] * 2,
        [products] + [pltpu.VMEM((size, CX), F32) for size in HEIGHTS[:LEVELS]],
    )(held[-1], *total, gather)
    matches.append(match)
    weights.append(weight)
    axes = ("strip", "sect")
    devices = lax.axis_size(axes)
    paired = [(i, i ^ 1) for i in range(devices)]
    crossed = [(i, ((i + 1) ^ 1) - 1) for i in range(1, devices - 1)]
    by_pair = lax.ppermute(to_pair, axes, paired)
    by_next = lax.ppermute(to_next, axes, crossed)
    (inner,) = call(
        inner_kernel,
        [SMEM] + [VMEM] * 8,
        [shape(ALL_ROWS, HALF)],
        [
            pltpu.VMEM((MIX_ROWS, 2 * CX), F32),
            pltpu.VMEM((ALL_K, HALF), BF16),
            pltpu.VMEM((ALL_K, HALF), BF16),
        ],
        megabytes=24,
    )(plane_mix, *fields, own, own_low, across)
    grid, *samples = call(
        outer_kernel,
        [VMEM] * (8 + 2 * PEERS),
        [shape(PLANES, NY, CX)] + [shape(8, CX)] * PEERS,
        [
            pltpu.VMEM((ALL_K, 2 * CX), BF16),
            pltpu.VMEM((ALL_K, 2 * CX), BF16),
            pltpu.VMEM((2 * TILES, HALF), BF16),
            pltpu.VMEM((PEERS * CAP, HALF), F32),
            pltpu.VMEM((2 * BAND, CX), F32),
        ],
    )(inner, by_pair, by_next, across, *outer, *matches, *weights)
    back = [samples[0]] + [lax.ppermute(samples[k], "sect", swaps[k]) for k in range(1, PEERS)]
    (match,) = call(spread_kernel, [VMEM], [shape(PEERS * CX, SEGS, kind=BF16)])(slots)
    (segments,) = call(
        pick_kernel, [SMEM] + [VMEM] * 5, [shape(1, SEGS)]
    )(brick_count, match, *back)
    return grid, segments.reshape(SEGS)


def solution(mesh):
    flat = ("strip", "sect")
    placed = (
        P(flat), P(None, flat), P(flat, None), P(flat, None), P(flat), P(flat), P(), P(), P(),
    )
    return jax.shard_map(
        body,
        mesh=mesh,
        in_specs=placed,
        out_specs=(P(None, None, flat), P(flat)),
        check_vma=False,
    )
```

```python
import jax
import jax.numpy as jnp
from jax import lax
from jax.experimental import pallas as pl
from jax.experimental.pallas import tpu as pltpu
from jax.sharding import PartitionSpec as P

NY = 384
CX = 128
LEVELS = 4
TILES = 384
PLANES = 8
TAPS = 17
REACH = TAPS // 2
SLOTS = 4
BRICKS = 256
CAP = 96
PEERS = 4
CELLS = SLOTS * CAP
PACK = CAP // 3
SPAN = 10
WIDE = SPAN * SLOTS
ROWS = CELLS + PACK
SEGS = BRICKS * SLOTS
BAND = NY // 8
HALF = PLANES * CX
HEIGHTS = tuple(NY >> level for level in range(LEVELS + 1))
WIDTHS = tuple(CX >> level for level in range(LEVELS + 1))
STEP = (384, 192, 96, 48, 32)
ROW_OF = (0, 384, 576, 672, 720)
ALL_ROWS = 752
TAP_ROW = (0, 768, 1152, 1344, 1440)
K_OF = (0, 768, 1152, 1344, 1440)
ALL_K = 1504
RIM_ROW = (0, 0, 192, 288, 336)
MIX_ROW = tuple(PLANES * sum(HEIGHTS[:level]) for level in range(LEVELS + 1))
MIX_ROWS = PLANES * sum(HEIGHTS)
F32 = jnp.float32
BF16 = jnp.bfloat16


def split(value):
    high = value.astype(BF16)
    return high, (value - high.astype(F32)).astype(BF16)


def dot(left, right):
    return jnp.dot(left, right, preferred_element_type=F32)


def iota(shape, dim):
    return lax.broadcasted_iota(jnp.int32, shape, dim)


def flags(condition):
    return condition.astype(F32).astype(BF16)


def turn(value, amount):
    amount = amount % CX
    return pltpu.roll(value, amount, 1) if amount else value


def swap_groups(bands):
    group = iota((1, CX), 1) // 16
    bands = [turn(band, 16 * i) for i, band in enumerate(bands)]
    for bit in range(3):
        upper = ((group >> bit) & 1) == 1
        bands = [jnp.where(upper, bands[(i + (1 << bit)) % 8], bands[i]) for i in range(8)]
    return [turn(bands[-i % 8], -16 * i) for i in range(8)]


def route_kernel(
    count_ref, currents_hbm, planes_hbm, cells_hbm, dest_hbm, tile_hbm, *refs
):
    outs, slot_ref = refs[:PEERS], refs[PEERS]
    feature, currents_ref, planes_ref, cells_ref, dest_ref, tile_ref, sems = refs[PEERS + 1 :]
    pairs = (
        (dest_hbm, dest_ref), (tile_hbm, tile_ref), (currents_hbm, currents_ref),
        (planes_hbm, planes_ref), (cells_hbm, cells_ref),
    )
    copies = [pltpu.make_async_copy(a, b, sems.at[i]) for i, (a, b) in enumerate(pairs)]
    for copy in copies:
        copy.start()
    for copy in copies[:4]:
        copy.wait()
    me = lax.axis_index("sect")
    away = dest_ref[...] ^ me
    onehot = (iota((16, BRICKS), 0) == away).astype(F32)
    before = flags(iota((BRICKS, BRICKS), 0) < iota((BRICKS, BRICKS), 1))
    earlier = dot(onehot.astype(BF16), before)
    base = (iota((16, BRICKS), 0) * CAP).astype(F32)
    slot = jnp.sum(onehot * (earlier + base), axis=0, keepdims=True)
    slot_ref[...] = jnp.broadcast_to(slot, slot_ref.shape)
    choose = flags(iota((PEERS * CAP, BRICKS), 0).astype(F32) == slot)
    alive = (iota((1, SEGS), 1) // SLOTS < count_ref[0]).astype(F32)
    currents = currents_ref[...] * alive
    lines = jnp.concatenate(
        [planes_ref[...], currents, jnp.zeros((CX - PLANES - 1, SEGS), F32)], axis=0
    )
    for part in range(SEGS // CX):
        feature[part * CX : (part + 1) * CX, :] = lines[:, part * CX : (part + 1) * CX].T
    meta = jnp.zeros((BRICKS, CX), F32)
    for s in range(SLOTS):
        meta = meta + turn(feature[pl.ds(s, BRICKS, stride=SLOTS), :], SPAN * s)
    tile = tile_ref[...]
    tile = (tile & 7) * BAND + (tile >> 3)
    tiles = jnp.concatenate([tile.astype(F32), jnp.zeros((CX - 1, BRICKS), F32)], axis=0)
    tiles = jnp.concatenate([tiles[:, :CX].T, tiles[:, CX:].T], axis=0)
    meta = meta + turn(tiles, 9)
    both = dot(choose, jnp.concatenate(split(meta), axis=1))
    both = both[:, :CX] + both[:, CX:]
    for k in range(PEERS):
        packed = both[k * CAP : k * CAP + PACK]
        for i in range(1, 3):
            start = k * CAP + i * PACK
            packed = packed + turn(both[start : start + PACK], WIDE * i)
        outs[k][CELLS:, :] = packed
    copies[4].wait()
    for s in range(SLOTS):
        high, low = split(cells_ref[pl.ds(s, BRICKS, stride=SLOTS), :])
        moved = dot(choose, jnp.concatenate([high, low], axis=1))
        moved = moved[:, :CX] + moved[:, CX:]
        for k in range(PEERS):
            outs[k][s * CAP : (s + 1) * CAP, :] = moved[k * CAP : (k + 1) * CAP]


def height_of(place, level):
    if level == LEVELS:
        return place
    band = (place * 1366) >> 16
    return (place - band * BAND) * (8 >> level) + band


def rim_of(lane, level):
    j = lane & 7
    before = (lane < CX // 2) == (level == 0)
    return (lane >> 3) & 7, jnp.where(before, j - REACH, j + WIDTHS[level])


def taps_at(table, shift):
    spot = jnp.where((shift >= 0) & (shift < TAPS), shift, CX - 1)
    return jnp.take_along_axis(jnp.broadcast_to(table, spot.shape), spot, axis=1)


def prep_kernel(
    across_ref, along_ref, mix_ref, own_ref, own_low_ref, across, blend_high, blend_low,
    rim_high, rim_low, gather, table
):
    exact = lax.Precision.HIGHEST
    table[...] = jnp.zeros(table.shape, F32)
    for level in range(LEVELS + 1):
        for r in range(2):
            line = 4 * level + r
            table[line : line + 1, :TAPS] = along_ref[level, r : r + 1, :]
            table[line + 2 : line + 3, :TAPS] = across_ref[level, r : r + 1, :]
    for level in range(LEVELS + 1):
        scale = 0.25**level
        row = iota((CX, 1), 0)
        mark = row >> level
        lane_z, lane_place = rim_of(row, level)
        line_z, line_place = rim_of(iota((1, CX), 1), level)
        column = iota((CX, CX), 1) >> level
        shift = mark - column + REACH
        rim_shift = lane_place - column + REACH
        same = lane_place == line_place
        edge = jnp.where(line_place < 0, line_place + WIDTHS[level], line_place - WIDTHS[level])
        for z in range(PLANES):
            chosen = flags((mark == edge) & (line_z == z))
            gather[level * PLANES + z, :CX, :] = chosen
            gather[level * PLANES + z, CX:, :] = chosen
        pick = (lane_z == iota((CX, 8), 1)).astype(F32)
        pick_t = (line_z == iota((8, CX), 0)).astype(F32)
        masks = [
            jnp.broadcast_to((lane_z == z).astype(F32), (CX, CX)).astype(BF16)
            for z in range(PLANES)
        ]
        for r in range(2):
            part = slice(r * CX, (r + 1) * CX)
            line = table[4 * level + r : 4 * level + r + 1, :]
            high, low = split(taps_at(line, shift) * scale)
            own_ref[level, :CX, part] = high
            own_ref[level, CX:, part] = high
            own_low_ref[level, :, part] = low
            high, low = split(taps_at(line, rim_shift) * scale)
            for z in range(PLANES):
                rim_high[level, part, z * CX : (z + 1) * CX] = high * masks[z]
                rim_low[level, part, z * CX : (z + 1) * CX] = low * masks[z]
            mixes = lax.dot_general(
                pick, mix_ref[level, r], (((1,), (1,)), ((), ())), precision=exact,
                preferred_element_type=F32,
            )
            mixes = jnp.dot(mixes, pick_t, precision=exact, preferred_element_type=F32)
            high, low = split(jnp.where(same, mixes, 0.0))
            blend_high[level, :, part] = high
            blend_low[level, :, part] = low
        size, step = HEIGHTS[level], STEP[level]
        upper = slice(TAP_ROW[level], TAP_ROW[level] + size)
        lower = slice(TAP_ROW[level] + step, TAP_ROW[level] + step + size)
        mine = height_of(iota((size, 1), 0), level)
        first = table[4 * level + 2 : 4 * level + 3, :]
        both = first + turn(table[4 * level + 3 : 4 * level + 4, :], 32)
        for start in range(0, 2 * step, CX):
            lanes = min(CX, 2 * step - start)
            place = iota((1, CX), 1) + start
            second = place >= step
            place = jnp.where(second, place - step, place)
            other = jnp.where(place < size, height_of(place, level), 4 * NY)
            shift = other - mine + REACH
            spot = jnp.where(
                (shift >= 0) & (shift < TAPS), shift + jnp.where(second, 32, 0), CX - 1
            )
            taps = jnp.take_along_axis(jnp.broadcast_to(both, spot.shape), spot, axis=1)
            high, low = split(taps[:, :lanes])
            across[upper, start : start + lanes] = high
            across[lower, start : start + lanes] = low


def brick_products(ref, match, weights, bricks):
    packed = ref[CELLS:, :]
    meta = jnp.concatenate([packed, turn(packed, -WIDE), turn(packed, -2 * WIDE)], axis=0)
    cells = [ref[s * CAP : (s + 1) * CAP, :] for s in range(SLOTS)]
    totals = [None] * PLANES
    for s in range(SLOTS):
        current = meta[:, SPAN * s + 8 : SPAN * s + 9]
        for z in range(PLANES):
            piece = cells[s] * meta[:, SPAN * s + z : SPAN * s + z + 1]
            weights[s * PLANES + z] = piece
            piece = piece * current
            totals[z] = piece if s == 0 else totals[z] + piece
    blank = jnp.zeros((CX - CAP, HALF), BF16)
    bricks[CAP:CX, :] = blank
    bricks[CX + CAP :, :] = blank
    for z in range(PLANES):
        high, low = split(totals[z])
        bricks[:CAP, z * CX : (z + 1) * CX] = high
        bricks[CX : CX + CAP, z * CX : (z + 1) * CX] = low
    whole = jnp.concatenate([meta, jnp.zeros((CX - CAP, CX), F32)], axis=0)
    names = jnp.where(iota((1, CX), 1) < CAP, whole.T[9:10, :], -1.0)
    match[...] = flags(iota((CAP, TILES), 1).astype(F32) == meta[:, 9:10])
    hot = flags(iota((TILES, CX), 0).astype(F32) == names)
    return jnp.concatenate([hot, hot], axis=1)


def brick_kernel(ref, *refs):
    match, weights, total, bricks = refs[-4:]
    hot = brick_products(ref, match, weights, bricks)
    for pair in range(PLANES // 2):
        part = slice(pair * 2 * CX, (pair + 1) * 2 * CX)
        found = dot(hot, bricks[:, part])
        total[:, part] = refs[0][:, part] + found if len(refs) > 4 else found


def charge_kernel(
    ref, partial, gather, match, weights, q0, s1, s2, s3, s4, to_pair, to_next, bricks, *rims
):
    hot = brick_products(ref, match, weights, bricks)
    lanes = iota((1, CX), 1)
    for pair in range(PLANES // 2):
        part = slice(pair * 2 * CX, (pair + 1) * 2 * CX)
        found = partial[:, part] + dot(hot, bricks[:, part])
        for i in range(2):
            z = 2 * pair + i
            plane = found[:, i * CX : (i + 1) * CX]
            bands = swap_groups([plane[b * BAND : (b + 1) * BAND] for b in range(8)])
            for level in range(LEVELS):
                plain = jnp.concatenate(bands, axis=0)
                (q0, s1, s2, s3)[level][z] = plain
                found_rims = dot(
                    jnp.concatenate(split(plain), axis=1), gather[level * PLANES + z]
                )
                rims[level][...] = rims[level][...] + found_rims if z else found_rims
                bands = [bands[2 * b] + bands[2 * b + 1] for b in range(len(bands) // 2)]
    size = HEIGHTS[LEVELS]
    coarse = jnp.zeros((size, CX), F32)
    for z in range(PLANES):
        value = s3[z, pl.ds(0, size, stride=2), :] + s3[z, pl.ds(1, size, stride=2), :]
        s4[z] = value
        coarse = coarse + dot(
            jnp.concatenate(split(value), axis=1), gather[LEVELS * PLANES + z]
        )
    even = (lax.axis_index("sect") & 1) == 0
    for level in range(1, LEVELS + 2):
        if level < LEVELS:
            rows = slice(RIM_ROW[level], RIM_ROW[level] + HEIGHTS[level])
            other = rims[level][...]
        elif level == LEVELS:
            rows, other = slice(RIM_ROW[level], RIM_ROW[level] + size), coarse
        else:
            rows = slice(RIM_ROW[LEVELS] + size, NY)
            other = jnp.zeros((NY - RIM_ROW[LEVELS] - size, CX), F32)
        right = jnp.where(lanes < CX // 2, rims[0][rows, :], other)
        left = jnp.where(lanes < CX // 2, other, rims[0][rows, :])
        to_pair[rows, :] = jnp.where(even, right, left)
        to_next[rows, :] = jnp.where(even, left, right)


def inner_kernel(
    mix_ref, q0, s1, s2, s3, s4, own_ref, own_low_ref, across, out_ref, ranked, high_ref, low_ref
):
    sources = (q0, s1, s2, s3, s4)

    def along(level):
        size = HEIGHTS[level]
        for z in range(PLANES):
            high, low = split(sources[level][z])
            found = dot(jnp.concatenate([high, low], axis=1), own_ref[level])
            rows = slice(MIX_ROW[level] + z * size, MIX_ROW[level] + (z + 1) * size)
            ranked[rows, :] = found + dot(high, own_low_ref[level])

    def blend(level, r):
        size, step = HEIGHTS[level], STEP[level]
        chunk = 24 if size < 32 else (48 if size == 48 else 32)
        chunk = 16 if chunk == 48 else chunk
        for start in range(0, size, chunk):
            parts = []
            for w in range(PLANES):
                line = MIX_ROW[level] + w * size + start
                parts.append(ranked[line : line + chunk, r * CX : (r + 1) * CX])
            for z in range(PLANES):
                total = parts[0] * mix_ref[level, r, z, 0]
                for w in range(1, PLANES):
                    total = total + parts[w] * mix_ref[level, r, z, w]
                if chunk == 24:
                    total = jnp.concatenate([total, jnp.zeros((8, CX), F32)], axis=0)
                high, low = split(total)
                line = TAP_ROW[level] + r * step + start
                high_ref[line : line + high.shape[0], z * CX : (z + 1) * CX] = high
                low_ref[line : line + high.shape[0], z * CX : (z + 1) * CX] = low

    def combine(level):
        size, step = HEIGHTS[level], STEP[level]
        rows = slice(ROW_OF[level], ROW_OF[level] + size)
        lines = slice(TAP_ROW[level], TAP_ROW[level] + 2 * step)
        taps = across[lines, : 2 * step]
        for pair in range(PLANES // 2):
            part = slice(pair * 2 * CX, (pair + 1) * 2 * CX)
            found = dot(taps, high_ref[lines, part])
            found = found[:size] + found[step : step + size]
            out_ref[rows, part] = found + dot(taps[:step], low_ref[lines, part])[:size]

    along(0)
    blend(0, 0)
    blend(0, 1)
    for level in range(1, LEVELS + 1):
        along(level)
    combine(0)
    for level in range(1, LEVELS + 1):
        blend(level, 0)
        blend(level, 1)
    for level in range(1, LEVELS + 1):
        combine(level)


def outer_kernel(*refs):
    inner, by_pair, by_next, across = refs[:4]
    blend_high, blend_low, rim_high, rim_low = refs[4:8]
    matches, weights = refs[8 : 8 + PEERS], refs[8 + PEERS : 8 + 2 * PEERS]
    grid_ref = refs[8 + 2 * PEERS]
    outs = refs[9 + 2 * PEERS : 9 + 3 * PEERS]
    high_ref, low_ref, tiles, picked, doubled = refs[9 + 3 * PEERS :]
    lanes = iota((1, CX), 1)
    even = (lax.axis_index("sect") & 1) == 0
    high_ref[...] = jnp.zeros((ALL_K, 2 * CX), BF16)
    low_ref[...] = jnp.zeros((ALL_K, 2 * CX), BF16)
    sums = []
    for level in range(LEVELS + 1):
        size, step = HEIGHTS[level], STEP[level]
        rows = slice(RIM_ROW[level], RIM_ROW[level] + size)
        from_left = jnp.where(even, by_next[rows, :], by_pair[rows, :])
        from_right = jnp.where(even, by_pair[rows, :], by_next[rows, :])
        if level == 0:
            rims = jnp.where(lanes < CX // 2, from_left, from_right)
        else:
            rims = jnp.where(lanes < CX // 2, from_right, from_left)
        high, low = split(rims)
        mixed = dot(high, blend_high[level]) + dot(low, blend_high[level])
        mixed = mixed + dot(high, blend_low[level])
        if size < step:
            mixed = jnp.concatenate([mixed, jnp.zeros((step - size, 2 * CX), F32)], axis=0)
        high, low = split(mixed)
        for r in range(2):
            part = slice(r * CX, (r + 1) * CX)
            place = slice(K_OF[level] + r * step, K_OF[level] + (r + 1) * step)
            high_ref[place, part] = high[:, part]
            low_ref[place, part] = low[:, part]
    for level in range(LEVELS + 1):
        size, step = HEIGHTS[level], STEP[level]
        place = slice(K_OF[level], K_OF[level] + 2 * step)
        taps = across[TAP_ROW[level] : TAP_ROW[level] + 2 * step, : 2 * step]
        found = dot(taps, high_ref[place, :])
        found = found[:step] + found[step:] + dot(taps[:step], low_ref[place, :])
        sums.append(jnp.concatenate(split(found), axis=0))
    for pair in range(PLANES // 2):
        part = slice(pair * 2 * CX, (pair + 1) * 2 * CX)
        above = None
        for level in range(LEVELS, -1, -1):
            size, step = HEIGHTS[level], STEP[level]
            value = dot(sums[level], rim_high[level, :, part])
            value = value[:size] + value[step : step + size]
            value = value + dot(sums[level][:step], rim_low[level, :, part])[:size]
            value = value + inner[ROW_OF[level] : ROW_OF[level] + HEIGHTS[level], part]
            if level == LEVELS:
                doubled[pl.ds(0, HEIGHTS[level], stride=2), :] = value[:, :CX]
                doubled[pl.ds(1, HEIGHTS[level], stride=2), :] = value[:, :CX]
                doubled[pl.ds(BAND, HEIGHTS[level], stride=2), :] = value[:, CX:]
                doubled[pl.ds(BAND + 1, HEIGHTS[level], stride=2), :] = value[:, CX:]
                above = [jnp.concatenate([doubled[:BAND, :], doubled[BAND:, :]], axis=1)]
                continue
            bands = 8 >> level
            fresh = []
            for b in range(bands):
                fresh.append(value[b * BAND : (b + 1) * BAND] + above[b * len(above) // bands])
            above = fresh
        for i in range(2):
            z = 2 * pair + i
            planes = [band[:, i * CX : (i + 1) * CX] for band in above]
            for b in range(8):
                grid_ref[z, pl.ds(b, BAND, stride=8), :] = planes[b]
            for b, band in enumerate(swap_groups(planes)):
                high, low = split(band)
                rows = slice(b * BAND, (b + 1) * BAND)
                tiles[rows, z * CX : (z + 1) * CX] = high
                rows = slice(TILES + b * BAND, TILES + (b + 1) * BAND)
                tiles[rows, z * CX : (z + 1) * CX] = low
    match = jnp.concatenate([ref[...] for ref in matches], axis=0)
    match = jnp.concatenate([match, match], axis=1)
    for pair in range(PLANES // 2):
        part = slice(pair * 2 * CX, (pair + 1) * 2 * CX)
        picked[:, part] = dot(match, tiles[:, part])
    for j in range(PEERS):
        mine = slice(j * CAP, (j + 1) * CAP)
        values = jnp.zeros((CAP, CX), F32)
        for s in range(SLOTS):
            total = picked[mine, :CX] * weights[j][s * PLANES]
            for z in range(1, PLANES):
                total = total + picked[mine, z * CX : (z + 1) * CX] * weights[j][s * PLANES + z]
            values = jnp.where(lanes == s, jnp.sum(total, axis=1, keepdims=True), values)
        values = jnp.concatenate([values, jnp.zeros((CX - CAP, CX), F32)], axis=0)
        outs[j][...] = values.T[:8, :]


def spread_kernel(slot_ref, match_ref):
    slot = slot_ref[0:1, :]
    away = jnp.floor((slot + 0.5) * (1.0 / CAP))
    pieces = jnp.concatenate(
        [away, slot - away * CAP, jnp.zeros((14, BRICKS), F32)], axis=0
    )
    spread = flags(iota((BRICKS, SEGS), 1) // SLOTS == iota((BRICKS, SEGS), 0))
    pieces = dot(pieces.astype(BF16), spread)
    place = pieces[0:1] * CX + pieces[1:2]
    match_ref[...] = flags(iota((PEERS * CX, SEGS), 0).astype(F32) == place)


def pick_kernel(count_ref, match_ref, b0, b1, b2, b3, out_ref):
    held = jnp.concatenate([b0[...], b1[...], b2[...], b3[...]], axis=1)
    value = dot(jnp.concatenate(split(held), axis=0), match_ref[...])
    value = value[:8] + value[8:]
    lane = iota((8, SEGS), 1)
    mine = (lane % SLOTS == iota((8, SEGS), 0)) & (lane // SLOTS < count_ref[0])
    out_ref[...] = jnp.sum(jnp.where(mine, value, 0.0), axis=0, keepdims=True)


VMEM = pl.BlockSpec(memory_space=pltpu.VMEM)
SMEM = pl.BlockSpec(memory_space=pltpu.SMEM)
ANY = pl.BlockSpec(memory_space=pl.ANY)
HBM = pl.BlockSpec(memory_space=pltpu.HBM)


def shape(*dims, kind=F32):
    return jax.ShapeDtypeStruct(dims, kind)


def call(kernel, inputs, outputs, scratch=(), megabytes=16):
    return pl.pallas_call(
        kernel,
        in_specs=list(inputs),
        out_specs=[VMEM] * len(outputs),
        out_shape=list(outputs),
        scratch_shapes=list(scratch),
        compiler_params=pltpu.CompilerParams(vmem_limit_bytes=int(megabytes * (1 << 20))),
    )


def body(
    currents, plane_weights, cell_weights, brick_dest, brick_tile, brick_count, kern_across,
    kern_along, plane_mix,
):
    *sends, slots = call(
        route_kernel,
        [SMEM] + [HBM] * 5,
        [shape(ROWS, CX)] * PEERS + [shape(8, BRICKS)],
        [
            pltpu.VMEM((SEGS, CX), F32),
            pltpu.VMEM((1, SEGS), F32),
            pltpu.VMEM((PLANES, SEGS), F32),
            pltpu.VMEM((SEGS, CX), F32),
            pltpu.VMEM((1, BRICKS), jnp.int32),
            pltpu.VMEM((1, BRICKS), jnp.int32),
            pltpu.SemaphoreType.DMA((5,)),
        ],
        megabytes=63,
    )(
        brick_count,
        currents.reshape(1, SEGS),
        plane_weights,
        cell_weights,
        brick_dest.reshape(1, BRICKS),
        brick_tile.reshape(1, BRICKS),
    )
    swaps = [[(i, i ^ k) for i in range(PEERS)] for k in range(PEERS)]
    held = [sends[0]] + [lax.ppermute(sends[k], "sect", swaps[k]) for k in range(1, PEERS)]
    prepared = call(
        prep_kernel,
        [VMEM, VMEM, VMEM],
        [
            shape(LEVELS + 1, 2 * CX, 2 * CX, kind=BF16),
            shape(LEVELS + 1, CX, 2 * CX, kind=BF16),
            shape(ALL_K, 2 * NY, kind=BF16),
            shape(LEVELS + 1, CX, 2 * CX, kind=BF16),
            shape(LEVELS + 1, CX, 2 * CX, kind=BF16),
            shape(LEVELS + 1, 2 * CX, HALF, kind=BF16),
            shape(LEVELS + 1, 2 * CX, HALF, kind=BF16),
            shape((LEVELS + 1) * PLANES, 2 * CX, CX, kind=BF16),
        ],
        [pltpu.VMEM((24, CX), F32)],
    )(kern_across, kern_along, plane_mix)
    own, own_low, across, *outer, gather = prepared
    kept = [shape(CAP, TILES, kind=BF16), shape(SLOTS * PLANES, CAP, CX)]
    products = pltpu.VMEM((2 * CX, HALF), BF16)
    matches, weights, total = [], [], []
    for value in held[:-1]:
        match, weight, partial = call(
            brick_kernel,
            [VMEM] * (1 + len(total)),
            kept + [shape(TILES, HALF)],
            [products],
        )(value, *total)
        matches.append(match)
        weights.append(weight)
        total = [partial]
    match, weight, *fields, to_pair, to_next = call(
        charge_kernel,
        [VMEM] * 3,
        kept + [shape(PLANES, size, CX) for size in HEIGHTS] + [shape(NY, CX)] * 2,
        [products] + [pltpu.VMEM((size, CX), F32) for size in HEIGHTS[:LEVELS]],
    )(held[-1], *total, gather)
    matches.append(match)
    weights.append(weight)
    axes = ("strip", "sect")
    devices = lax.axis_size(axes)
    paired = [(i, i ^ 1) for i in range(devices)]
    crossed = [(i, ((i + 1) ^ 1) - 1) for i in range(1, devices - 1)]
    by_pair = lax.ppermute(to_pair, axes, paired)
    by_next = lax.ppermute(to_next, axes, crossed)
    (inner,) = call(
        inner_kernel,
        [SMEM] + [VMEM] * 8,
        [shape(ALL_ROWS, HALF)],
        [
            pltpu.VMEM((MIX_ROWS, 2 * CX), F32),
            pltpu.VMEM((ALL_K, HALF), BF16),
            pltpu.VMEM((ALL_K, HALF), BF16),
        ],
        megabytes=24,
    )(plane_mix, *fields, own, own_low, across)
    grid, *samples = call(
        outer_kernel,
        [VMEM] * (8 + 2 * PEERS),
        [shape(PLANES, NY, CX)] + [shape(8, CX)] * PEERS,
        [
            pltpu.VMEM((ALL_K, 2 * CX), BF16),
            pltpu.VMEM((ALL_K, 2 * CX), BF16),
            pltpu.VMEM((2 * TILES, HALF), BF16),
            pltpu.VMEM((PEERS * CAP, HALF), F32),
            pltpu.VMEM((2 * BAND, CX), F32),
        ],
    )(inner, by_pair, by_next, across, *outer, *matches, *weights)
    back = [samples[0]] + [lax.ppermute(samples[k], "sect", swaps[k]) for k in range(1, PEERS)]
    (match,) = call(spread_kernel, [VMEM], [shape(PEERS * CX, SEGS, kind=BF16)])(slots)
    (segments,) = call(
        pick_kernel, [SMEM] + [VMEM] * 5, [shape(1, SEGS)]
    )(brick_count, match, *back)
    return grid, segments.reshape(SEGS)


def solution(mesh):
    flat = ("strip", "sect")
    placed = (
        P(flat), P(None, flat), P(flat, None), P(flat, None), P(flat), P(flat), P(), P(), P(),
    )
    return jax.shard_map(
        body,
        mesh=mesh,
        in_specs=placed,
        out_specs=(P(None, None, flat), P(flat)),
        check_vma=False,
    )
```

```python
import jax
import jax.numpy as jnp
from jax import lax
from jax.experimental import pallas as pl
from jax.experimental.pallas import tpu as pltpu
from jax.sharding import PartitionSpec as P

NY = 384
CX = 128
LEVELS = 4
TILES = 384
PLANES = 8
TAPS = 17
REACH = TAPS // 2
SLOTS = 4
BRICKS = 256
CAP = 96
PEERS = 4
CELLS = SLOTS * CAP
PACK = CAP // 3
SPAN = 10
WIDE = SPAN * SLOTS
ROWS = CELLS + PACK
SEGS = BRICKS * SLOTS
BAND = NY // 8
HALF = PLANES * CX
HEIGHTS = tuple(NY >> level for level in range(LEVELS + 1))
WIDTHS = tuple(CX >> level for level in range(LEVELS + 1))
STEP = (384, 192, 96, 48, 32)
ROW_OF = (0, 384, 576, 672, 720)
ALL_ROWS = 752
TAP_ROW = (0, 768, 1152, 1344, 1440)
K_OF = (0, 768, 1152, 1344, 1440)
ALL_K = 1504
RIM_ROW = (0, 0, 192, 288, 336)
MIX_ROW = tuple(PLANES * sum(HEIGHTS[:level]) for level in range(LEVELS + 1))
MIX_ROWS = PLANES * sum(HEIGHTS)
F32 = jnp.float32
BF16 = jnp.bfloat16


def split(value):
    high = value.astype(BF16)
    return high, (value - high.astype(F32)).astype(BF16)


def dot(left, right):
    return jnp.dot(left, right, preferred_element_type=F32)


def iota(shape, dim):
    return lax.broadcasted_iota(jnp.int32, shape, dim)


def flags(condition):
    return condition.astype(F32).astype(BF16)


def turn(value, amount):
    amount = amount % CX
    return pltpu.roll(value, amount, 1) if amount else value


def swap_groups(bands):
    group = iota((1, CX), 1) // 16
    bands = [turn(band, 16 * i) for i, band in enumerate(bands)]
    for bit in range(3):
        upper = ((group >> bit) & 1) == 1
        bands = [jnp.where(upper, bands[(i + (1 << bit)) % 8], bands[i]) for i in range(8)]
    return [turn(bands[-i % 8], -16 * i) for i in range(8)]


def route_kernel(
    count_ref, currents_hbm, planes_hbm, cells_hbm, dest_hbm, tile_hbm, *refs
):
    outs, slot_ref = refs[:PEERS], refs[PEERS]
    feature, currents_ref, planes_ref, cells_ref, dest_ref, tile_ref, sems = refs[PEERS + 1 :]
    pairs = (
        (dest_hbm, dest_ref), (tile_hbm, tile_ref), (currents_hbm, currents_ref),
        (planes_hbm, planes_ref), (cells_hbm, cells_ref),
    )
    copies = [pltpu.make_async_copy(a, b, sems.at[i]) for i, (a, b) in enumerate(pairs)]
    for copy in copies:
        copy.start()
    for copy in copies[:4]:
        copy.wait()
    me = lax.axis_index("sect")
    away = dest_ref[...] ^ me
    onehot = (iota((16, BRICKS), 0) == away).astype(F32)
    before = flags(iota((BRICKS, BRICKS), 0) < iota((BRICKS, BRICKS), 1))
    earlier = dot(onehot.astype(BF16), before)
    base = (iota((16, BRICKS), 0) * CAP).astype(F32)
    slot = jnp.sum(onehot * (earlier + base), axis=0, keepdims=True)
    slot_ref[...] = jnp.broadcast_to(slot, slot_ref.shape)
    choose = flags(iota((PEERS * CAP, BRICKS), 0).astype(F32) == slot)
    alive = (iota((1, SEGS), 1) // SLOTS < count_ref[0]).astype(F32)
    currents = currents_ref[...] * alive
    lines = jnp.concatenate(
        [planes_ref[...], currents, jnp.zeros((CX - PLANES - 1, SEGS), F32)], axis=0
    )
    for part in range(SEGS // CX):
        feature[part * CX : (part + 1) * CX, :] = lines[:, part * CX : (part + 1) * CX].T
    meta = jnp.zeros((BRICKS, CX), F32)
    for s in range(SLOTS):
        meta = meta + turn(feature[pl.ds(s, BRICKS, stride=SLOTS), :], SPAN * s)
    tile = tile_ref[...]
    tile = (tile & 7) * BAND + (tile >> 3)
    tiles = jnp.concatenate([tile.astype(F32), jnp.zeros((CX - 1, BRICKS), F32)], axis=0)
    tiles = jnp.concatenate([tiles[:, :CX].T, tiles[:, CX:].T], axis=0)
    meta = meta + turn(tiles, 9)
    both = dot(choose, jnp.concatenate(split(meta), axis=1))
    both = both[:, :CX] + both[:, CX:]
    for k in range(PEERS):
        packed = both[k * CAP : k * CAP + PACK]
        for i in range(1, 3):
            start = k * CAP + i * PACK
            packed = packed + turn(both[start : start + PACK], WIDE * i)
        outs[k][CELLS:, :] = packed
    copies[4].wait()
    for s in range(SLOTS):
        high, low = split(cells_ref[pl.ds(s, BRICKS, stride=SLOTS), :])
        moved = dot(choose, jnp.concatenate([high, low], axis=1))
        moved = moved[:, :CX] + moved[:, CX:]
        for k in range(PEERS):
            outs[k][s * CAP : (s + 1) * CAP, :] = moved[k * CAP : (k + 1) * CAP]


def height_of(place, level):
    if level == LEVELS:
        return place
    band = (place * 1366) >> 16
    return (place - band * BAND) * (8 >> level) + band


def rim_of(lane, level):
    j = lane & 7
    before = (lane < CX // 2) == (level == 0)
    return (lane >> 3) & 7, jnp.where(before, j - REACH, j + WIDTHS[level])


def taps_at(table, shift):
    spot = jnp.where((shift >= 0) & (shift < TAPS), shift, CX - 1)
    return jnp.take_along_axis(jnp.broadcast_to(table, spot.shape), spot, axis=1)


def prep_kernel(
    across_ref, along_ref, mix_ref, own_ref, own_low_ref, across, blend_high, blend_low,
    rim_high, rim_low, gather, table
):
    exact = lax.Precision.HIGHEST
    table[...] = jnp.zeros(table.shape, F32)
    for level in range(LEVELS + 1):
        for r in range(2):
            line = 4 * level + r
            table[line : line + 1, :TAPS] = along_ref[level, r : r + 1, :]
            table[line + 2 : line + 3, :TAPS] = across_ref[level, r : r + 1, :]
    for level in range(LEVELS + 1):
        scale = 0.25**level
        row = iota((CX, 1), 0)
        mark = row >> level
        lane_z, lane_place = rim_of(row, level)
        line_z, line_place = rim_of(iota((1, CX), 1), level)
        column = iota((CX, CX), 1) >> level
        shift = mark - column + REACH
        rim_shift = lane_place - column + REACH
        same = lane_place == line_place
        edge = jnp.where(line_place < 0, line_place + WIDTHS[level], line_place - WIDTHS[level])
        for z in range(PLANES):
            chosen = flags((mark == edge) & (line_z == z))
            gather[level * PLANES + z, :CX, :] = chosen
            gather[level * PLANES + z, CX:, :] = chosen
        pick = (lane_z == iota((CX, 8), 1)).astype(F32)
        pick_t = (line_z == iota((8, CX), 0)).astype(F32)
        masks = [
            jnp.broadcast_to((lane_z == z).astype(F32), (CX, CX)).astype(BF16)
            for z in range(PLANES)
        ]
        for r in range(2):
            part = slice(r * CX, (r + 1) * CX)
            line = table[4 * level + r : 4 * level + r + 1, :]
            high, low = split(taps_at(line, shift) * scale)
            own_ref[level, :CX, part] = high
            own_ref[level, CX:, part] = high
            own_low_ref[level, :, part] = low
            high, low = split(taps_at(line, rim_shift) * scale)
            for z in range(PLANES):
                rim_high[level, part, z * CX : (z + 1) * CX] = high * masks[z]
                rim_low[level, part, z * CX : (z + 1) * CX] = low * masks[z]
            mixes = lax.dot_general(
                pick, mix_ref[level, r], (((1,), (1,)), ((), ())), precision=exact,
                preferred_element_type=F32,
            )
            mixes = jnp.dot(mixes, pick_t, precision=exact, preferred_element_type=F32)
            high, low = split(jnp.where(same, mixes, 0.0))
            blend_high[level, :, part] = high
            blend_low[level, :, part] = low
        size, step = HEIGHTS[level], STEP[level]
        upper = slice(TAP_ROW[level], TAP_ROW[level] + size)
        lower = slice(TAP_ROW[level] + step, TAP_ROW[level] + step + size)
        mine = height_of(iota((size, 1), 0), level)
        first = table[4 * level + 2 : 4 * level + 3, :]
        both = first + turn(table[4 * level + 3 : 4 * level + 4, :], 32)
        for start in range(0, 2 * step, CX):
            lanes = min(CX, 2 * step - start)
            place = iota((1, CX), 1) + start
            second = place >= step
            place = jnp.where(second, place - step, place)
            other = jnp.where(place < size, height_of(place, level), 4 * NY)
            shift = other - mine + REACH
            spot = jnp.where(
                (shift >= 0) & (shift < TAPS), shift + jnp.where(second, 32, 0), CX - 1
            )
            taps = jnp.take_along_axis(jnp.broadcast_to(both, spot.shape), spot, axis=1)
            high, low = split(taps[:, :lanes])
            across[upper, start : start + lanes] = high
            across[lower, start : start + lanes] = low


def brick_products(ref, match, weights, bricks):
    packed = ref[CELLS:, :]
    meta = jnp.concatenate([packed, turn(packed, -WIDE), turn(packed, -2 * WIDE)], axis=0)
    cells = [ref[s * CAP : (s + 1) * CAP, :] for s in range(SLOTS)]
    totals = [None] * PLANES
    for s in range(SLOTS):
        current = meta[:, SPAN * s + 8 : SPAN * s + 9]
        for z in range(PLANES):
            piece = cells[s] * meta[:, SPAN * s + z : SPAN * s + z + 1]
            weights[s * PLANES + z] = piece
            piece = piece * current
            totals[z] = piece if s == 0 else totals[z] + piece
    blank = jnp.zeros((CX - CAP, HALF), BF16)
    bricks[CAP:CX, :] = blank
    bricks[CX + CAP :, :] = blank
    for z in range(PLANES):
        high, low = split(totals[z])
        bricks[:CAP, z * CX : (z + 1) * CX] = high
        bricks[CX : CX + CAP, z * CX : (z + 1) * CX] = low
    whole = jnp.concatenate([meta, jnp.zeros((CX - CAP, CX), F32)], axis=0)
    names = jnp.where(iota((1, CX), 1) < CAP, whole.T[9:10, :], -1.0)
    match[...] = flags(iota((CAP, TILES), 1).astype(F32) == meta[:, 9:10])
    hot = flags(iota((TILES, CX), 0).astype(F32) == names)
    return jnp.concatenate([hot, hot], axis=1)


def brick_kernel(ref, *refs):
    match, weights, total, bricks = refs[-4:]
    hot = brick_products(ref, match, weights, bricks)
    for pair in range(PLANES // 2):
        part = slice(pair * 2 * CX, (pair + 1) * 2 * CX)
        found = dot(hot, bricks[:, part])
        total[:, part] = refs[0][:, part] + found if len(refs) > 4 else found


def charge_kernel(
    ref, partial, gather, match, weights, q0, s1, s2, s3, s4, to_pair, to_next, bricks, *rims
):
    hot = brick_products(ref, match, weights, bricks)
    lanes = iota((1, CX), 1)
    for pair in range(PLANES // 2):
        part = slice(pair * 2 * CX, (pair + 1) * 2 * CX)
        found = partial[:, part] + dot(hot, bricks[:, part])
        for i in range(2):
            z = 2 * pair + i
            plane = found[:, i * CX : (i + 1) * CX]
            bands = swap_groups([plane[b * BAND : (b + 1) * BAND] for b in range(8)])
            for level in range(LEVELS):
                plain = jnp.concatenate(bands, axis=0)
                (q0, s1, s2, s3)[level][z] = plain
                found_rims = dot(
                    jnp.concatenate(split(plain), axis=1), gather[level * PLANES + z]
                )
                rims[level][...] = rims[level][...] + found_rims if z else found_rims
                bands = [bands[2 * b] + bands[2 * b + 1] for b in range(len(bands) // 2)]
    size = HEIGHTS[LEVELS]
    coarse = jnp.zeros((size, CX), F32)
    for z in range(PLANES):
        value = s3[z, pl.ds(0, size, stride=2), :] + s3[z, pl.ds(1, size, stride=2), :]
        s4[z] = value
        coarse = coarse + dot(
            jnp.concatenate(split(value), axis=1), gather[LEVELS * PLANES + z]
        )
    even = (lax.axis_index("sect") & 1) == 0
    for level in range(1, LEVELS + 2):
        if level < LEVELS:
            rows = slice(RIM_ROW[level], RIM_ROW[level] + HEIGHTS[level])
            other = rims[level][...]
        elif level == LEVELS:
            rows, other = slice(RIM_ROW[level], RIM_ROW[level] + size), coarse
        else:
            rows = slice(RIM_ROW[LEVELS] + size, NY)
            other = jnp.zeros((NY - RIM_ROW[LEVELS] - size, CX), F32)
        right = jnp.where(lanes < CX // 2, rims[0][rows, :], other)
        left = jnp.where(lanes < CX // 2, other, rims[0][rows, :])
        to_pair[rows, :] = jnp.where(even, right, left)
        to_next[rows, :] = jnp.where(even, left, right)


def inner_kernel(
    mix_ref, q0, s1, s2, s3, s4, own_ref, own_low_ref, across, out_ref, ranked, high_ref, low_ref
):
    sources = (q0, s1, s2, s3, s4)

    def along(level):
        size = HEIGHTS[level]
        for z in range(PLANES):
            high, low = split(sources[level][z])
            found = dot(jnp.concatenate([high, low], axis=1), own_ref[level])
            rows = slice(MIX_ROW[level] + z * size, MIX_ROW[level] + (z + 1) * size)
            ranked[rows, :] = found + dot(high, own_low_ref[level])

    def blend(level, r):
        size, step = HEIGHTS[level], STEP[level]
        chunk = 24 if size < 32 else (48 if size == 48 else 32)
        chunk = 16 if chunk == 48 else chunk
        for start in range(0, size, chunk):
            parts = []
            for w in range(PLANES):
                line = MIX_ROW[level] + w * size + start
                parts.append(ranked[line : line + chunk, r * CX : (r + 1) * CX])
            for z in range(PLANES):
                total = parts[0] * mix_ref[level, r, z, 0]
                for w in range(1, PLANES):
                    total = total + parts[w] * mix_ref[level, r, z, w]
                if chunk == 24:
                    total = jnp.concatenate([total, jnp.zeros((8, CX), F32)], axis=0)
                high, low = split(total)
                line = TAP_ROW[level] + r * step + start
                high_ref[line : line + high.shape[0], z * CX : (z + 1) * CX] = high
                low_ref[line : line + high.shape[0], z * CX : (z + 1) * CX] = low

    def combine(level):
        size, step = HEIGHTS[level], STEP[level]
        rows = slice(ROW_OF[level], ROW_OF[level] + size)
        lines = slice(TAP_ROW[level], TAP_ROW[level] + 2 * step)
        taps = across[lines, : 2 * step]
        for pair in range(PLANES // 2):
            part = slice(pair * 2 * CX, (pair + 1) * 2 * CX)
            found = dot(taps, high_ref[lines, part])
            found = found[:size] + found[step : step + size]
            out_ref[rows, part] = found + dot(taps[:step], low_ref[lines, part])[:size]

    along(0)
    blend(0, 0)
    blend(0, 1)
    for level in range(1, LEVELS + 1):
        along(level)
    combine(0)
    for level in range(1, LEVELS + 1):
        blend(level, 0)
        blend(level, 1)
    for level in range(1, LEVELS + 1):
        combine(level)


def outer_kernel(*refs):
    inner, by_pair, by_next, across = refs[:4]
    blend_high, blend_low, rim_high, rim_low = refs[4:8]
    matches, weights = refs[8 : 8 + PEERS], refs[8 + PEERS : 8 + 2 * PEERS]
    grid_ref = refs[8 + 2 * PEERS]
    outs = refs[9 + 2 * PEERS : 9 + 3 * PEERS]
    high_ref, low_ref, tiles, picked, doubled = refs[9 + 3 * PEERS :]
    lanes = iota((1, CX), 1)
    even = (lax.axis_index("sect") & 1) == 0
    high_ref[...] = jnp.zeros((ALL_K, 2 * CX), BF16)
    low_ref[...] = jnp.zeros((ALL_K, 2 * CX), BF16)
    sums = []
    for level in range(LEVELS + 1):
        size, step = HEIGHTS[level], STEP[level]
        rows = slice(RIM_ROW[level], RIM_ROW[level] + size)
        from_left = jnp.where(even, by_next[rows, :], by_pair[rows, :])
        from_right = jnp.where(even, by_pair[rows, :], by_next[rows, :])
        if level == 0:
            rims = jnp.where(lanes < CX // 2, from_left, from_right)
        else:
            rims = jnp.where(lanes < CX // 2, from_right, from_left)
        high, low = split(rims)
        heavy = jnp.concatenate([blend_high[level], blend_high[level]], axis=0)
        mixed = dot(jnp.concatenate([high, low], axis=1), heavy) + dot(high, blend_low[level])
        if size < step:
            mixed = jnp.concatenate([mixed, jnp.zeros((step - size, 2 * CX), F32)], axis=0)
        high, low = split(mixed)
        for r in range(2):
            part = slice(r * CX, (r + 1) * CX)
            place = slice(K_OF[level] + r * step, K_OF[level] + (r + 1) * step)
            high_ref[place, part] = high[:, part]
            low_ref[place, part] = low[:, part]
    for level in range(LEVELS + 1):
        size, step = HEIGHTS[level], STEP[level]
        place = slice(K_OF[level], K_OF[level] + 2 * step)
        taps = across[TAP_ROW[level] : TAP_ROW[level] + 2 * step, : 2 * step]
        found = dot(taps, high_ref[place, :])
        found = found[:step] + found[step:] + dot(taps[:step], low_ref[place, :])
        sums.append(jnp.concatenate(split(found), axis=0))
    for pair in range(PLANES // 2):
        part = slice(pair * 2 * CX, (pair + 1) * 2 * CX)
        above = None
        for level in range(LEVELS, -1, -1):
            size, step = HEIGHTS[level], STEP[level]
            value = dot(sums[level], rim_high[level, :, part])
            value = value[:size] + value[step : step + size]
            value = value + dot(sums[level][:step], rim_low[level, :, part])[:size]
            value = value + inner[ROW_OF[level] : ROW_OF[level] + HEIGHTS[level], part]
            if level == LEVELS:
                doubled[pl.ds(0, HEIGHTS[level], stride=2), :] = value[:, :CX]
                doubled[pl.ds(1, HEIGHTS[level], stride=2), :] = value[:, :CX]
                doubled[pl.ds(BAND, HEIGHTS[level], stride=2), :] = value[:, CX:]
                doubled[pl.ds(BAND + 1, HEIGHTS[level], stride=2), :] = value[:, CX:]
                above = [jnp.concatenate([doubled[:BAND, :], doubled[BAND:, :]], axis=1)]
                continue
            bands = 8 >> level
            fresh = []
            for b in range(bands):
                fresh.append(value[b * BAND : (b + 1) * BAND] + above[b * len(above) // bands])
            above = fresh
        for i in range(2):
            z = 2 * pair + i
            planes = [band[:, i * CX : (i + 1) * CX] for band in above]
            for b in range(8):
                grid_ref[z, pl.ds(b, BAND, stride=8), :] = planes[b]
            for b, band in enumerate(swap_groups(planes)):
                high, low = split(band)
                rows = slice(b * BAND, (b + 1) * BAND)
                tiles[rows, z * CX : (z + 1) * CX] = high
                rows = slice(TILES + b * BAND, TILES + (b + 1) * BAND)
                tiles[rows, z * CX : (z + 1) * CX] = low
    match = jnp.concatenate([ref[...] for ref in matches], axis=0)
    match = jnp.concatenate([match, match], axis=1)
    for pair in range(PLANES // 2):
        part = slice(pair * 2 * CX, (pair + 1) * 2 * CX)
        picked[:, part] = dot(match, tiles[:, part])
    for j in range(PEERS):
        mine = slice(j * CAP, (j + 1) * CAP)
        values = jnp.zeros((CAP, CX), F32)
        for s in range(SLOTS):
            total = picked[mine, :CX] * weights[j][s * PLANES]
            for z in range(1, PLANES):
                total = total + picked[mine, z * CX : (z + 1) * CX] * weights[j][s * PLANES + z]
            values = jnp.where(lanes == s, jnp.sum(total, axis=1, keepdims=True), values)
        values = jnp.concatenate([values, jnp.zeros((CX - CAP, CX), F32)], axis=0)
        outs[j][...] = values.T[:8, :]


def spread_kernel(slot_ref, match_ref):
    slot = slot_ref[0:1, :]
    away = jnp.floor((slot + 0.5) * (1.0 / CAP))
    pieces = jnp.concatenate(
        [away, slot - away * CAP, jnp.zeros((14, BRICKS), F32)], axis=0
    )
    spread = flags(iota((BRICKS, SEGS), 1) // SLOTS == iota((BRICKS, SEGS), 0))
    pieces = dot(pieces.astype(BF16), spread)
    place = pieces[0:1] * CX + pieces[1:2]
    match_ref[...] = flags(iota((PEERS * CX, SEGS), 0).astype(F32) == place)


def pick_kernel(count_ref, match_ref, b0, b1, b2, b3, out_ref):
    held = jnp.concatenate([b0[...], b1[...], b2[...], b3[...]], axis=1)
    value = dot(jnp.concatenate(split(held), axis=0), match_ref[...])
    value = value[:8] + value[8:]
    lane = iota((8, SEGS), 1)
    mine = (lane % SLOTS == iota((8, SEGS), 0)) & (lane // SLOTS < count_ref[0])
    out_ref[...] = jnp.sum(jnp.where(mine, value, 0.0), axis=0, keepdims=True)


VMEM = pl.BlockSpec(memory_space=pltpu.VMEM)
SMEM = pl.BlockSpec(memory_space=pltpu.SMEM)
ANY = pl.BlockSpec(memory_space=pl.ANY)
HBM = pl.BlockSpec(memory_space=pltpu.HBM)


def shape(*dims, kind=F32):
    return jax.ShapeDtypeStruct(dims, kind)


def call(kernel, inputs, outputs, scratch=(), megabytes=16):
    return pl.pallas_call(
        kernel,
        in_specs=list(inputs),
        out_specs=[VMEM] * len(outputs),
        out_shape=list(outputs),
        scratch_shapes=list(scratch),
        compiler_params=pltpu.CompilerParams(vmem_limit_bytes=int(megabytes * (1 << 20))),
    )


def body(
    currents, plane_weights, cell_weights, brick_dest, brick_tile, brick_count, kern_across,
    kern_along, plane_mix,
):
    *sends, slots = call(
        route_kernel,
        [SMEM] + [HBM] * 5,
        [shape(ROWS, CX)] * PEERS + [shape(8, BRICKS)],
        [
            pltpu.VMEM((SEGS, CX), F32),
            pltpu.VMEM((1, SEGS), F32),
            pltpu.VMEM((PLANES, SEGS), F32),
            pltpu.VMEM((SEGS, CX), F32),
            pltpu.VMEM((1, BRICKS), jnp.int32),
            pltpu.VMEM((1, BRICKS), jnp.int32),
            pltpu.SemaphoreType.DMA((5,)),
        ],
        megabytes=63,
    )(
        brick_count,
        currents.reshape(1, SEGS),
        plane_weights,
        cell_weights,
        brick_dest.reshape(1, BRICKS),
        brick_tile.reshape(1, BRICKS),
    )
    swaps = [[(i, i ^ k) for i in range(PEERS)] for k in range(PEERS)]
    held = [sends[0]] + [lax.ppermute(sends[k], "sect", swaps[k]) for k in range(1, PEERS)]
    prepared = call(
        prep_kernel,
        [VMEM, VMEM, VMEM],
        [
            shape(LEVELS + 1, 2 * CX, 2 * CX, kind=BF16),
            shape(LEVELS + 1, CX, 2 * CX, kind=BF16),
            shape(ALL_K, 2 * NY, kind=BF16),
            shape(LEVELS + 1, CX, 2 * CX, kind=BF16),
            shape(LEVELS + 1, CX, 2 * CX, kind=BF16),
            shape(LEVELS + 1, 2 * CX, HALF, kind=BF16),
            shape(LEVELS + 1, 2 * CX, HALF, kind=BF16),
            shape((LEVELS + 1) * PLANES, 2 * CX, CX, kind=BF16),
        ],
        [pltpu.VMEM((24, CX), F32)],
    )(kern_across, kern_along, plane_mix)
    own, own_low, across, *outer, gather = prepared
    kept = [shape(CAP, TILES, kind=BF16), shape(SLOTS * PLANES, CAP, CX)]
    products = pltpu.VMEM((2 * CX, HALF), BF16)
    matches, weights, total = [], [], []
    for value in held[:-1]:
        match, weight, partial = call(
            brick_kernel,
            [VMEM] * (1 + len(total)),
            kept + [shape(TILES, HALF)],
            [products],
        )(value, *total)
        matches.append(match)
        weights.append(weight)
        total = [partial]
    match, weight, *fields, to_pair, to_next = call(
        charge_kernel,
        [VMEM] * 3,
        kept + [shape(PLANES, size, CX) for size in HEIGHTS] + [shape(NY, CX)] * 2,
        [products] + [pltpu.VMEM((size, CX), F32) for size in HEIGHTS[:LEVELS]],
    )(held[-1], *total, gather)
    matches.append(match)
    weights.append(weight)
    axes = ("strip", "sect")
    devices = lax.axis_size(axes)
    paired = [(i, i ^ 1) for i in range(devices)]
    crossed = [(i, ((i + 1) ^ 1) - 1) for i in range(1, devices - 1)]
    by_pair = lax.ppermute(to_pair, axes, paired)
    by_next = lax.ppermute(to_next, axes, crossed)
    (inner,) = call(
        inner_kernel,
        [SMEM] + [VMEM] * 8,
        [shape(ALL_ROWS, HALF)],
        [
            pltpu.VMEM((MIX_ROWS, 2 * CX), F32),
            pltpu.VMEM((ALL_K, HALF), BF16),
            pltpu.VMEM((ALL_K, HALF), BF16),
        ],
        megabytes=24,
    )(plane_mix, *fields, own, own_low, across)
    grid, *samples = call(
        outer_kernel,
        [VMEM] * (8 + 2 * PEERS),
        [shape(PLANES, NY, CX)] + [shape(8, CX)] * PEERS,
        [
            pltpu.VMEM((ALL_K, 2 * CX), BF16),
            pltpu.VMEM((ALL_K, 2 * CX), BF16),
            pltpu.VMEM((2 * TILES, HALF), BF16),
            pltpu.VMEM((PEERS * CAP, HALF), F32),
            pltpu.VMEM((2 * BAND, CX), F32),
        ],
    )(inner, by_pair, by_next, across, *outer, *matches, *weights)
    back = [samples[0]] + [lax.ppermute(samples[k], "sect", swaps[k]) for k in range(1, PEERS)]
    (match,) = call(spread_kernel, [VMEM], [shape(PEERS * CX, SEGS, kind=BF16)])(slots)
    (segments,) = call(
        pick_kernel, [SMEM] + [VMEM] * 5, [shape(1, SEGS)]
    )(brick_count, match, *back)
    return grid, segments.reshape(SEGS)


def solution(mesh):
    flat = ("strip", "sect")
    placed = (
        P(flat), P(None, flat), P(flat, None), P(flat, None), P(flat), P(flat), P(), P(), P(),
    )
    return jax.shard_map(
        body,
        mesh=mesh,
        in_specs=placed,
        out_specs=(P(None, None, flat), P(flat)),
        check_vma=False,
    )
```
